32 devices in a mesh: shot: 2 (over x), gz: 16 (over z, y, core).
Axes of the slice: x: 2, y: 2, z: 4, core: 2. Of those that a mesh axis runs over, the one named last changes fastest.
Arguments:
- source_now: float32 [256, 128, 128], P(('shot', 'gz')), parts along dimension 0, may hold values from -6 to 6
- source_before: float32 [256, 128, 128], P(('shot', 'gz')), parts along dimension 0, may hold values from -6 to 6
- receiver_now: float32 [256, 128, 128], P(('shot', 'gz')), parts along dimension 0, may hold values from -6 to 6
- receiver_before: float32 [256, 128, 128], P(('shot', 'gz')), parts along dimension 0, may hold values from -6 to 6
- speed_term: float32 [128, 128, 128], P('gz'), may hold values from 0.03 to 0.18
- saved_faces: float32 [24, 8, 128, 128], P('shot', None, 'gz'), parts along dimension 0, may hold values from -6 to 6
- face_steps: int32 [12], replicated, may hold values from 0 to 11, each once
- traces: bfloat16 [24, 128, 128], P('shot'), parts along dimension 0, may hold values from -6 to 6
- lag_offsets: int32 [8], replicated, may hold values from -8 to 8, as said below
- snap_phase: int32 [2], replicated, may hold values from 0 to 5
Outputs:
- image_out: bfloat16 [16, 128, 128, 128], P('shot', None, 'gz'), parts along dimension 0
- source_final: float32 [256, 128, 128], P(('shot', 'gz')), parts along dimension 0
- receiver_final: float32 [256, 128, 128], P(('shot', 'gz')), parts along dimension 0
The draws below stay inside these ranges and needn't reach their ends.
There are 2 independent parts, one for each index of `shot`. The reference program is written for one: setup_inputs(seed, part) draws one part's arguments, and reference() takes and returns one part's arrays. A program takes and returns all parts, laid end to end along the dimension named above; an argument that names none is the same for every part. Nothing has to cross between parts.
Inputs may be any that keep to these rules, and one draw needn't show every extreme that they name: `face_steps`: each of the 12 saved slots belongs to exactly one step. `lag_offsets`: the 8 offsets are different, and both ends of the range occur.
All inputs are finite; a program needn't handle non-finite values.
Results may differ from the reference program's by a relative error of at most 0.001.
Values sent between devices are 32-bit elements; how exact they have to be, the bound alone decides.
No kernel may reach another device: no remote copies, remote signals or barrier semaphores. Data moves between devices by JAX's collectives and lax.ppermute only.
A program may use at most 64 MiB of HBM per device.

```python
import math
import jax
import jax.numpy as jnp
from jax import lax

NY = 128
NX = 128
LAGS = 8
LMAX = 8
STEPS = 12
SNAP_EVERY = 6
SNAPS = 2
NZ = 128


def draw_lag_offsets(key, part):
    first_key = jax.random.fold_in(key, 11)
    second_key = jax.random.fold_in(key, 12)
    interior = jax.random.permutation(first_key, 2 * LMAX - 1)[:LAGS - 2].astype(jnp.int32) - (LMAX - 1)
    ends_fixed = jnp.array([-LMAX, LMAX], jnp.int32)
    combined = jnp.concatenate([ends_fixed, interior])
    shuffle = jax.random.permutation(second_key, LAGS)
    return combined[shuffle]


def steps_of(key, extent, split, low, largest):
    factor_of = 1.0
    for position, shards_of in split:
        steps = jax.random.uniform(jax.random.fold_in(jax.random.fold_in(key, 6), position), (shards_of,), jnp.float32, low / len(split), largest / len(split))
        factor_of = factor_of * jnp.repeat(jnp.exp(steps), extent[position] // shards_of).reshape((-1,) + (1,) * (len(extent) - 1 - position))
    return factor_of


def gaussian(own_key, dims, spread, reach, split=(), kind=jnp.bfloat16):
    values = jax.random.normal(own_key, dims, jnp.float32) * spread
    if len(split) > 0:
        values = steps_of(own_key, dims, split, -0.22, 0.18) * values
    return jnp.clip(values, min=-reach, max=reach).astype(kind)


def setup_inputs(seed: int = 0, part: int = 0) -> dict:
    arg_keys = jax.random.split(jax.random.key(seed), 11)
    own_keys = jax.random.split(jax.random.fold_in(arg_keys[10], part), 11)
    source_now = gaussian(own_keys[0], (NZ, NY, NX), 1.0, 6.0, ((0, 16),), jnp.float32)
    source_before = gaussian(own_keys[1], (NZ, NY, NX), 1.0, 6.0, ((0, 16),), jnp.float32)
    receiver_now = gaussian(own_keys[2], (NZ, NY, NX), 1.0, 6.0, ((0, 16),), jnp.float32)
    receiver_before = gaussian(own_keys[3], (NZ, NY, NX), 1.0, 6.0, ((0, 16),), jnp.float32)
    speed_term = jnp.clip(jnp.exp(math.log(0.18) - 1.7917595 * jax.random.uniform(arg_keys[4], (NZ, NY, NX), jnp.float32) ** steps_of(arg_keys[4], (NZ, NY, NX), ((0, 16),), -0.2, 0.2)), 0.03, 0.18)
    saved_faces = gaussian(own_keys[5], (STEPS, 8, NZ, NY), 1.0, 6.0, ((2, 16),), jnp.float32)
    face_steps = jax.random.permutation(arg_keys[6], STEPS).astype(jnp.int32)
    traces = gaussian(own_keys[7], (STEPS, NY, NX), 1.0, 6.0)
    lag_offsets = draw_lag_offsets(jax.random.fold_in(arg_keys[10], 71), part)
    snap_phase = jax.random.randint(arg_keys[9], (SNAPS,), 0, SNAP_EVERY).astype(jnp.int32)
    return {"source_now": source_now, "source_before": source_before, "receiver_now": receiver_now, "receiver_before": receiver_before, "speed_term": speed_term, "saved_faces": saved_faces, "face_steps": face_steps, "traces": traces, "lag_offsets": lag_offsets, "snap_phase": snap_phase}


stencil_weights = (-205.0 / 72.0, 8.0 / 5.0, -1.0 / 5.0, 8.0 / 315.0, -1.0 / 560.0)
damping = 0.25
smoothing = 16.0

def stencil(extended, layers):
    center = extended[:, 4:4 + layers]
    height = center.shape[2]
    breadth = center.shape[3]
    padded = jnp.pad(center, ((0, 0), (0, 0), (4, 4), (4, 4)))
    summed = 3.0 * stencil_weights[0] * center
    for offset in range(1, 5):
        weight = stencil_weights[offset]
        summed = summed + weight * (extended[:, 4 + offset:4 + offset + layers] + extended[:, 4 - offset:4 - offset + layers])
        summed = summed + weight * (padded[:, :, 4 + offset:4 + offset + height, 4:4 + breadth] + padded[:, :, 4 - offset:4 - offset + height, 4:4 + breadth])
        summed = summed + weight * (padded[:, :, 4:4 + height, 4 + offset:4 + offset + breadth] + padded[:, :, 4:4 + height, 4 - offset:4 - offset + breadth])
    return summed

def advance(extended, center, previous, speed_term, faces_now, trace_now, top_row, layers):
    updated = 2.0 * center - previous + speed_term * stencil(extended, layers)
    left_faces = jnp.moveaxis(faces_now[:4], 0, -1)
    right_faces = jnp.moveaxis(faces_now[4:], 0, -1)
    source = updated[0].at[:, :, :4].set(left_faces).at[:, :, -4:].set(right_faces)
    top_mask = lax.broadcasted_iota(jnp.int32, (layers, 1, 1), 0) == top_row
    receiver = updated[1] + jnp.where(top_mask, trace_now[None], 0.0)
    return jnp.stack([source, receiver])

def lag_images(snapshot, lag_offsets):
    source = snapshot[0]
    receiver = snapshot[1]
    margin = ((0, 0), (0, 0), (LMAX, LMAX))
    source_pad = jnp.pad(source, margin)
    receiver_pad = jnp.pad(receiver, margin)
    breadth = source.shape[2]
    images = []
    for lag_index in range(LAGS):
        lag_now = lag_offsets[lag_index]
        shifted_source = lax.dynamic_slice_in_dim(source_pad, LMAX - lag_now, breadth, 2)
        shifted_receiver = lax.dynamic_slice_in_dim(receiver_pad, LMAX + lag_now, breadth, 2)
        images.append(shifted_source * shifted_receiver)
    return (jnp.stack(images), source * source)

def finish(raw_image, illumination):
    layers = illumination.shape[0]
    columns = illumination.reshape(layers, -1)
    lower = jnp.full((layers,), -smoothing, illumination.dtype).at[0].set(0.0)
    upper = jnp.full((layers,), -smoothing, illumination.dtype).at[-1].set(0.0)
    middle = jnp.full((layers,), 1.0 + 2.0 * smoothing, illumination.dtype)
    smooth = lax.linalg.tridiagonal_solve(lower, middle, upper, columns).reshape(illumination.shape)
    return (raw_image / (smooth + damping)).astype(jnp.bfloat16)

def reference(source_now, source_before, receiver_now, receiver_before, speed_term, saved_faces, face_steps, traces, lag_offsets, snap_phase):
    current = jnp.stack([source_now, receiver_now])
    previous = jnp.stack([source_before, receiver_before])
    layers = source_now.shape[0]
    zero_rows = jnp.zeros((2, 4) + source_now.shape[1:], source_now.dtype)
    raw_parts = []
    light_parts = []
    for window in range(SNAPS):
        snapshot = jnp.zeros_like(current)
        for local_index in range(SNAP_EVERY):
            step_index = window * SNAP_EVERY + local_index
            extended = jnp.concatenate([zero_rows, current, zero_rows], axis=1)
            updated = advance(extended, current, previous, speed_term, saved_faces[face_steps[step_index]], traces[step_index].astype(jnp.float32), 0, layers)
            snapshot = jnp.where(local_index == snap_phase[window], updated, snapshot)
            previous = current
            current = updated
        raw_now, light_now = lag_images(snapshot, lag_offsets)
        raw_parts.append(raw_now)
        light_parts.append(light_now)
    raw_image = raw_parts[0]
    illumination = light_parts[0]
    for window in range(1, SNAPS):
        raw_image = raw_image + raw_parts[window]
        illumination = illumination + light_parts[window]
    return (finish(raw_image, illumination), current[0], current[1])
```

```python
import functools

import jax
import jax.numpy as jnp
import numpy as np
from jax import lax
from jax.experimental import pallas as pl
from jax.experimental.pallas import tpu as pltpu
from jax.sharding import PartitionSpec as P

SNAP_EVERY = 6
SNAPS = 2
REACH = 4

SCALE = 5040.0
NEAR = (8064.0, -1008.0, 128.0, -9.0)
CENTRE = -43050.0
damping = 0.25
smoothing = 16.0

VMEM = pl.BlockSpec(memory_space=pltpu.VMEM)
SMEM = pl.BlockSpec(memory_space=pltpu.SMEM)
PARAMS = pltpu.CompilerParams(vmem_limit_bytes=24 * 1024 * 1024)


def f32(*shape):
    return jax.ShapeDtypeStruct(shape, jnp.float32)


def cost(flops, bytes_accessed):
    return pl.CostEstimate(flops=int(flops), bytes_accessed=int(bytes_accessed), transcendentals=0)


def banded(size):
    apart = np.abs(np.arange(size)[:, None] - np.arange(size)[None, :])
    table = np.zeros((size, size), np.float32)
    for k, weight in enumerate(NEAR):
        table[apart == k + 1] = weight
    return table


def roles(count):
    table = np.zeros((count, 8), np.int32)
    for i in range(count):
        group, field, half = i // 4, (i // 2) % 2, i % 2
        outer = (group == 0 and half == 0) or (group == count // 4 - 1 and half == 1)
        table[i, :4] = (field, half, outer, group == 0 and half == 0 and field == 1)
    return table


def pairs_to_fields(count):
    first, second = [], []
    for base in range(0, count, 4):
        first += [(base, base), (base + 1, base + 2), (base + 2, base + 1), (base + 3, base + 3)]
        second += [(base, base + 2), (base + 1, base), (base + 2, base + 3), (base + 3, base + 1)]
    return first, second


def pairs_of_halos(count):
    within = [(i, i ^ 1) for i in range(count)]
    between = [(0, 2), (2, 0), (count - 3, count - 1), (count - 1, count - 3)]
    for group in range(count // 4 - 1):
        for field in range(2):
            low, high = 4 * group + 2 * field + 1, 4 * group + 4 + 2 * field
            between += [(low, high), (high, low)]
    return between, within


def faces_kernel(face_steps, faces, out, gathered):
    steps, layers = face_steps.shape[0], out.shape[0]
    gathered[...] = jnp.zeros_like(gathered)

    def one_layer(layer, carry):
        for step in range(steps):
            base = face_steps[step] * (8 * layers) + layer
            gathered[8 * step : 8 * step + 4] = faces[pl.ds(base + 4 * layers, 4, stride=layers), :]
            gathered[8 * step + 4 : 8 * step + 8] = faces[pl.ds(base, 4, stride=layers), :]
        out[layer] = gathered[...].T
        return carry

    lax.fori_loop(0, layers, one_layer, 0)


def place_faces(saved_faces, face_steps):
    slots, eight, layers, ny = saved_faces.shape
    return pl.pallas_call(
        faces_kernel,
        out_shape=f32(layers, ny, 128),
        in_specs=[SMEM, VMEM],
        out_specs=VMEM,
        scratch_shapes=[pltpu.VMEM((128, ny), jnp.float32)],
        compiler_params=PARAMS,
        name="faces",
    )(face_steps, saved_faces.reshape(slots * eight * layers, ny))


def merge_kernel(role, now_a, now_b, before_a, before_b, speed_a, speed_b, face_a, face_b, cur, prev, speed, face, low, high):
    layers = now_a.shape[0]
    field, half = role[0], role[1]

    def one_layer(j, carry):
        place = jnp.where(half == 0, j, 2 * layers - 1 - j)
        part = (place >= layers).astype(jnp.int32)
        q = place - part * layers

        def take(a, b, scale=None):
            def run():
                cur[REACH + j] = a[0][q]
                prev[REACH + j] = a[1][q]
                speed[j] = a[2][q] * (1.0 / SCALE)
                face[j] = a[3][q]

            return run

        pl.when(part == field)(take((now_a, before_a, speed_a, face_a), None))
        pl.when(part != field)(take((now_b, before_b, speed_b, face_b), None))
        return carry

    lax.fori_loop(0, 2 * layers, one_layer, 0)
    low[...] = cur[REACH : 2 * REACH]
    high[...] = cur[2 * layers : 2 * layers + REACH]


def merge(role, parts):
    layers, ny, nx = parts[0].shape
    slab = f32(REACH, ny, nx)
    tall = f32(2 * layers + 2 * REACH, ny, nx)
    whole = f32(2 * layers, ny, nx)
    return pl.pallas_call(
        merge_kernel,
        out_shape=(tall, tall, whole, whole, slab, slab),
        in_specs=[SMEM] + [VMEM] * 8,
        out_specs=(VMEM,) * 6,
        compiler_params=PARAMS,
        name="merge",
    )(role, *parts)


def step_layers(step, role, across, along, cur, prev, speed, face, new, first, last, skip):
    ny, nx = speed.shape[1:]
    is_source = role[0] == 0
    column = lax.broadcasted_iota(jnp.int32, (ny, nx), 1)
    edge = ((column < REACH) | (column >= nx - REACH)) & is_source

    def one_layer(j, carry):
        layer = jnp.where(j < skip[0], j, j + skip[1]) if skip else j
        e = layer + REACH
        u = cur[e]
        high = u.astype(jnp.bfloat16)
        low = (u - high.astype(jnp.float32)).astype(jnp.bfloat16)
        total = jnp.dot(
            jnp.concatenate([high, low], axis=1), across[...], preferred_element_type=jnp.float32
        ) + jnp.dot(along[...], jnp.concatenate([high, low], axis=0), preferred_element_type=jnp.float32)
        for k in range(REACH):
            total = total + NEAR[k] * (cur[e + (k + 1)] + cur[e - (k + 1)])
        total = total + CENTRE * u
        updated = 2.0 * u - prev[e] + speed[layer] * total
        placed = pltpu.roll(face[layer], (128 - 8 * step - REACH) % 128, axis=1)
        new[e] = jnp.where(edge, placed, updated)
        return carry

    lax.fori_loop(first, last, one_layer, 0)


def fill_halos(role, low, high, cur):
    layers = cur.shape[0] - 2 * REACH
    inside = role[2] == 0
    for d in range(REACH):
        cur[REACH - 1 - d] = jnp.where(inside, low[d], 0.0)
        cur[REACH + layers + d] = high[REACH - 1 - d]


def add_trace(role, trace, new):
    @pl.when(role[3] == 1)
    def _():
        new[REACH] = new[REACH] + trace[...].astype(jnp.float32)


def keep_snapshot(step, role, phase, new, snap):
    count, layers, rows, _ = snap.shape
    window = step // SNAP_EVERY

    @pl.when(phase[window] == step - window * SNAP_EVERY)
    def _():
        def one_layer(j, carry):
            place = jnp.where(role[1] == 0, j, layers - 1 - j)
            for strip in range(count):
                snap[strip, place] = new[REACH + j, strip * rows : (strip + 1) * rows, :]
            return carry

        lax.fori_loop(0, layers, one_layer, 0)


def border_kernel(step, role, across, along, low, high, trace, speed, face, cur_in, prev, cur, new, low_out, high_out):
    layers = speed.shape[0]
    fill_halos(role, low, high, cur)
    step_layers(
        step, role, across, along, cur, prev, speed, face, new, 0, 2 * REACH, (REACH, layers - 2 * REACH)
    )
    add_trace(role, trace, new)
    low_out[...] = new[REACH : 2 * REACH]
    high_out[...] = new[layers : layers + REACH]


def inner_kernel(step, has_snap, role, phase, across, along, speed, face, cur, prev, *rest):
    new, snap = rest[-2:]
    layers = speed.shape[0]
    step_layers(step, role, across, along, cur, prev, speed, face, new, REACH, layers - REACH, None)
    keep_snapshot(step, role, phase, new, snap)


def last_kernel(
    step, role, phase, across, along, low, high, trace, speed, face, cur_in, prev, snap_in, cur, new, snap, out_a, out_b
):
    layers = speed.shape[0]
    fill_halos(role, low, high, cur)
    step_layers(step, role, across, along, cur, prev, speed, face, new, 0, layers, None)
    add_trace(role, trace, new)
    keep_snapshot(step, role, phase, new, snap)
    field, half = role[0], role[1]

    def one_layer(j, carry):
        place = jnp.where(half == 0, j, layers - 1 - j)
        part = (place >= layers // 2).astype(jnp.int32)
        q = place - part * (layers // 2)

        @pl.when(part == field)
        def _():
            out_a[q] = new[REACH + j]

        @pl.when(part != field)
        def _():
            out_b[q] = new[REACH + j]

        return carry

    lax.fori_loop(0, layers, one_layer, 0)


def image_kernel(lags, sweep, first, second, out, light):
    count, layers, rows, nx = first.shape
    depth = out.shape[1]

    def where_is(d):
        block = d // layers
        return (block // 2) * 4 + block % 2, d % layers

    def down(d, carried):
        block, layer = where_is(d)
        s0, s1 = first[block, layer], second[block, layer]
        carried = (s0 * s0 + s1 * s1) * sweep[d] + carried * (smoothing * sweep[d])
        light[d] = carried
        return carried

    lax.fori_loop(0, depth, down, jnp.zeros((rows, nx), jnp.float32), unroll=4)

    column = lax.broadcasted_iota(jnp.int32, (rows, nx), 1)

    def up(i, carried):
        d = depth - 1 - i
        block, layer = where_is(d)
        smooth = light[d] + carried * (smoothing * sweep[d])
        inverse = 1.0 / (smooth + damping)
        s0, s1 = first[block, layer], second[block, layer]
        r0, r1 = first[block + 2, layer], second[block + 2, layer]
        for index in range(out.shape[0]):
            lag = lags[index]
            size = jnp.abs(lag)
            right, left = lax.rem(lag + nx, nx), lax.rem(nx - lag, nx)
            raw = pltpu.roll(s0, right, axis=1) * pltpu.roll(r0, left, axis=1) + pltpu.roll(
                s1, right, axis=1
            ) * pltpu.roll(r1, left, axis=1)
            inside = (column >= size) & (column < nx - size)
            out[index, d] = jnp.where(inside, raw * inverse, 0.0).astype(out.dtype)
        return smooth

    lax.fori_loop(0, depth, up, jnp.zeros((rows, nx), jnp.float32), unroll=2)


def sweep_table(depth):
    table, before = [], 0.0
    for _ in range(depth):
        before = 1.0 / (1.0 + 2.0 * smoothing - smoothing * smoothing * before)
        table.append(before)
    return np.array(table, np.float32)


def images(lag_offsets, first, second):
    count, layers, rows, nx = first.shape
    depth = count // 2 * layers
    lags = lag_offsets.shape[0]
    return pl.pallas_call(
        image_kernel,
        out_shape=jax.ShapeDtypeStruct((lags, depth, rows, nx), jnp.bfloat16),
        in_specs=[SMEM, SMEM, VMEM, VMEM],
        out_specs=VMEM,
        scratch_shapes=[pltpu.VMEM((depth, rows, nx), jnp.float32)],
        compiler_params=pltpu.CompilerParams(vmem_limit_bytes=40 * 1024 * 1024),
        name="images",
    )(lag_offsets, jnp.asarray(sweep_table(depth)), first, second)


def local(
    source_now,
    source_before,
    receiver_now,
    receiver_before,
    speed_term,
    saved_faces,
    face_steps,
    traces,
    lag_offsets,
    snap_phase,
):
    count = lax.axis_size("gz")
    index = lax.axis_index("gz")
    own, ny, nx = source_now.shape
    layers = 2 * own
    rows = ny // count
    steps = face_steps.shape[0]
    role = lax.dynamic_index_in_dim(jnp.asarray(roles(count)), index, 0, keepdims=False)
    first_pairs, second_pairs = pairs_to_fields(count)
    back_pairs = [(b, a) for a, b in second_pairs]
    between, within = pairs_of_halos(count)
    band_x, band_y = banded(nx), banded(ny)
    across = jnp.asarray(np.concatenate([band_x, band_x], axis=0), jnp.bfloat16)
    along = jnp.asarray(np.concatenate([band_y, band_y], axis=1), jnp.bfloat16)

    keeps = index % 2 == 0

    def regroup(a, b):
        return (
            lax.ppermute(jnp.where(keeps, a, b), "gz", first_pairs),
            lax.ppermute(jnp.where(keeps, b, a), "gz", second_pairs),
        )

    faces = place_faces(saved_faces, face_steps)
    parts = (
        *regroup(source_now, receiver_now),
        *regroup(source_before, receiver_before),
        lax.ppermute(speed_term, "gz", first_pairs),
        lax.ppermute(speed_term, "gz", second_pairs),
        lax.ppermute(faces, "gz", first_pairs),
        lax.ppermute(faces, "gz", second_pairs),
    )
    cur, prev, speed, face, low, high = merge(role, parts)

    tall = f32(layers + 2 * REACH, ny, nx)
    slab = f32(REACH, ny, nx)
    strips = f32(count, layers, rows, nx)
    plane = ny * nx
    snap = None
    gathered = []
    for step in range(steps):
        low = lax.ppermute(low, "gz", between)
        high = lax.ppermute(high, "gz", within)
        trace = traces[step]
        if step < steps - 1:
            cur, new, low, high = pl.pallas_call(
                functools.partial(border_kernel, step),
                out_shape=(tall, tall, slab, slab),
                in_specs=[SMEM] + [VMEM] * 9,
                out_specs=(VMEM,) * 4,
                input_output_aliases={8: 0, 9: 1},
                compiler_params=PARAMS,
                cost_estimate=cost(60 * 8 * plane, 4 * 40 * plane),
                name="border",
            )(role, across, along, low, high, trace, speed, face, cur, prev)
            fresh = step % SNAP_EVERY == 0
            new, snap = pl.pallas_call(
                functools.partial(inner_kernel, step, not fresh),
                out_shape=(tall, strips),
                in_specs=[SMEM, SMEM] + [VMEM] * (6 if fresh else 7),
                out_specs=(VMEM,) * 2,
                input_output_aliases={7: 0} if fresh else {7: 0, 8: 1},
                compiler_params=PARAMS,
                cost_estimate=cost(60 * (layers - 8) * plane, 4 * 40 * plane),
                name="inner",
            )(role, snap_phase, across, along, speed, face, cur, new, *(() if fresh else (snap,)))
        else:
            cur, new, snap, out_a, out_b = pl.pallas_call(
                functools.partial(last_kernel, step),
                out_shape=(tall, tall, strips, f32(own, ny, nx), f32(own, ny, nx)),
                in_specs=[SMEM, SMEM] + [VMEM] * 10,
                out_specs=(VMEM,) * 5,
                input_output_aliases={9: 0, 10: 1, 11: 2},
                compiler_params=PARAMS,
                cost_estimate=cost(60 * layers * plane, 4 * 80 * plane),
                name="last",
            )(role, snap_phase, across, along, low, high, trace, speed, face, cur, prev, snap)
        prev, cur = cur, new
        if step % SNAP_EVERY == SNAP_EVERY - 1:
            gathered.append(lax.all_to_all(snap, "gz", split_axis=0, concat_axis=0, tiled=True))

    back_a = lax.ppermute(out_a, "gz", first_pairs)
    back_b = lax.ppermute(out_b, "gz", back_pairs)
    image_out = images(lag_offsets, *gathered)
    return (image_out, jnp.where(keeps, back_a, back_b), jnp.where(keeps, back_b, back_a))


def solution(mesh):
    return jax.shard_map(
        local,
        mesh=mesh,
        in_specs=(
            P(("shot", "gz"), None, None),
            P(("shot", "gz"), None, None),
            P(("shot", "gz"), None, None),
            P(("shot", "gz"), None, None),
            P("gz", None, None),
            P("shot", None, "gz", None),
            P(),
            P("shot", None, None),
            P(),
            P(),
        ),
        out_specs=(
            P("shot", None, "gz", None),
            P(("shot", "gz"), None, None),
            P(("shot", "gz"), None, None),
        ),
        check_vma=False,
    )
```

```python
import functools

import jax
import jax.numpy as jnp
import numpy as np
from jax import lax
from jax.experimental import pallas as pl
from jax.experimental.pallas import tpu as pltpu
from jax.sharding import PartitionSpec as P

SNAP_EVERY = 6
SNAPS = 2
REACH = 4
EARLY = 2

SCALE = 5040.0
NEAR = (8064.0, -1008.0, 128.0, -9.0)
CENTRE = -43050.0
damping = 0.25
smoothing = 16.0

VMEM = pl.BlockSpec(memory_space=pltpu.VMEM)
SMEM = pl.BlockSpec(memory_space=pltpu.SMEM)
ANY = pl.BlockSpec(memory_space=pl.ANY)
PARAMS = pltpu.CompilerParams(vmem_limit_bytes=24 * 1024 * 1024)


def f32(*shape):
    return jax.ShapeDtypeStruct(shape, jnp.float32)


def held(*shape):
    return pltpu.VMEM(shape, jnp.float32)


def cost(flops, bytes_accessed):
    return pl.CostEstimate(flops=int(flops), bytes_accessed=int(bytes_accessed), transcendentals=0)


def banded(size):
    apart = np.abs(np.arange(size)[:, None] - np.arange(size)[None, :])
    table = np.zeros((size, size), np.float32)
    for k, weight in enumerate(NEAR):
        table[apart == k + 1] = weight
    return table


def pairs_to_fields(count):
    first, second = [], []
    for base in range(0, count, 4):
        first += [(base, base), (base + 1, base + 2), (base + 2, base + 1), (base + 3, base + 3)]
        second += [(base, base + 2), (base + 1, base), (base + 2, base + 3), (base + 3, base + 1)]
    return first, second


def pairs_of_halos(count):
    within = [(i, i ^ 1) for i in range(count)]
    between = [(0, 2), (2, 0), (count - 3, count - 1), (count - 1, count - 3)]
    for group in range(count // 4 - 1):
        for field in range(2):
            low, high = 4 * group + 2 * field + 1, 4 * group + 4 + 2 * field
            between += [(low, high), (high, low)]
    return between, within


def my_field():
    return lax.rem(lax.axis_index("gz") // 2, 2)


def my_half():
    return lax.rem(lax.axis_index("gz"), 2)


def place_of(local, layers):
    return jnp.where(my_half() == 0, local, layers - 1 - local)


def choose_kernel(here, there, first, second, sem):
    def copies(a, b):
        return pltpu.make_async_copy(a, first, sem.at[0]), pltpu.make_async_copy(b, second, sem.at[1])

    def run(a, b):
        one, two = copies(a, b)
        one.start()
        two.start()
        one.wait()
        two.wait()

    pl.when(my_half() == 0)(lambda: run(here, there))
    pl.when(my_half() != 0)(lambda: run(there, here))


def choose(here, there, spec):
    like = jax.ShapeDtypeStruct(here.shape, here.dtype)
    return pl.pallas_call(
        choose_kernel,
        out_shape=(like, like),
        in_specs=[ANY, ANY],
        out_specs=(spec, spec),
        scratch_shapes=[pltpu.SemaphoreType.DMA((2,))],
        compiler_params=PARAMS,
        name="choose",
    )(here, there)


def prepare_kernel(face_steps, lags, faces, late, early, shifts, gathered):
    steps, layers = face_steps.shape[0], late.shape[0]
    nx = shifts.shape[1] // 2
    gathered[...] = jnp.zeros_like(gathered)

    def gather(step, layer, row):
        base = face_steps[step] * (8 * layers) + layer
        gathered[row : row + 4] = faces[pl.ds(base + 4 * layers, 4, stride=layers), :]
        gathered[row + 4 : row + 8] = faces[pl.ds(base, 4, stride=layers), :]

    for layer in range(layers):
        for step in range(EARLY):
            gather(step, layer, 8 * (EARLY * layer + step))
    early[...] = gathered[...].T

    def one_layer(layer, carry):
        for step in range(steps):
            gather(step, layer, 8 * step)
        late[layer] = gathered[...].T
        return carry

    lax.fori_loop(0, layers, one_layer, 0)

    apart = lax.broadcasted_iota(jnp.int32, (nx, nx), 1) - lax.broadcasted_iota(jnp.int32, (nx, nx), 0)
    for index in range(lags.shape[0]):
        columns = slice(index * nx, (index + 1) * nx)
        for which, lag in ((0, lags[index]), (1, -lags[index])):
            moved = jnp.where(apart == lag, 1.0, 0.0).astype(jnp.bfloat16)
            shifts[which, :nx, columns] = moved
            shifts[which, nx:, columns] = moved


def prepare(saved_faces, face_steps, lag_offsets, nx):
    slots, eight, layers, ny = saved_faces.shape
    return pl.pallas_call(
        prepare_kernel,
        out_shape=(
            f32(layers, ny, 128),
            f32(ny, 128),
            jax.ShapeDtypeStruct((2, 2 * nx, lag_offsets.shape[0] * nx), jnp.bfloat16),
        ),
        in_specs=[SMEM, SMEM, VMEM],
        out_specs=(VMEM,) * 3,
        scratch_shapes=[pltpu.VMEM((128, ny), jnp.float32)],
        compiler_params=PARAMS,
        name="prepare",
    )(face_steps, lag_offsets, saved_faces.reshape(slots * eight * layers, ny))


def for_each_part(layers, run):
    def one_layer(j, carry):
        place = place_of(j, layers)
        part = (place >= layers // 2).astype(jnp.int32)
        q = place - part * (layers // 2)
        pl.when(part == my_field())(lambda: run(j, q, 0))
        pl.when(part != my_field())(lambda: run(j, q, 1))
        return carry

    lax.fori_loop(0, layers, one_layer, 0, unroll=2)


def merge_now_kernel(now_a, now_b, cur, low, high):
    layers = 2 * now_a.shape[0]

    def run(j, q, which):
        cur[REACH + j] = (now_a, now_b)[which][q]

    for_each_part(layers, run)
    low[...] = cur[REACH : 2 * REACH]
    high[...] = cur[layers : layers + REACH]


def merge_rest_kernel(before_a, before_b, speed_a, speed_b, prev, speed):
    def run(j, q, which):
        prev[REACH + j] = (before_a, before_b)[which][q]
        speed[j] = (speed_a, speed_b)[which][q] * (1.0 / SCALE)

    for_each_part(2 * before_a.shape[0], run)


def merge_faces_kernel(face_a, face_b, face):
    def run(j, q, which):
        face[j] = (face_a, face_b)[which][q]

    for_each_part(2 * face_a.shape[0], run)


def merge(kernel, name, shapes, *parts):
    return pl.pallas_call(
        kernel,
        out_shape=shapes,
        in_specs=[VMEM] * len(parts),
        out_specs=(VMEM,) * len(shapes),
        compiler_params=PARAMS,
        name=name,
    )(*parts)


def split(u):
    high = u.astype(jnp.bfloat16)
    return high, (u - high.astype(jnp.float32)).astype(jnp.bfloat16)


def advance(step, across, along, cur, prev, speed, faces, new, local):
    layers, ny, nx = speed.shape
    column = lax.broadcasted_iota(jnp.int32, (ny, nx), 1)
    edge = ((column < REACH) | (column >= nx - REACH)) & (my_field() == 0)

    def placed(layer):
        if step >= EARLY:
            return pltpu.roll(faces[0][layer], (128 - 8 * step - REACH) % 128, axis=1)
        place = place_of(layer, layers)
        part = (place >= layers // 2).astype(jnp.int32)
        lane = 8 * (EARLY * (place - part * (layers // 2)) + step) + REACH
        held = jnp.where(part == 0, faces[0][...], faces[1][...])
        return pltpu.roll(held, lax.rem(128 - lane, 128), axis=1)

    for first in range(0, len(local), 2):
        pair = local[first : first + 2]
        inputs = [cur[REACH + layer] for layer in pair]
        halves = [split(u) for u in inputs]
        along_sum = jnp.dot(
            along[...],
            jnp.concatenate([jnp.concatenate(half, axis=0) for half in halves], axis=1),
            preferred_element_type=jnp.float32,
        )
        across_sum = jnp.dot(
            jnp.concatenate([jnp.concatenate(half, axis=1) for half in halves], axis=0),
            across[...],
            preferred_element_type=jnp.float32,
        )
        for i, layer in enumerate(pair):
            e, u = REACH + layer, inputs[i]
            total = across_sum[i * ny : (i + 1) * ny] + along_sum[:, i * nx : (i + 1) * nx]
            for k in range(REACH):
                total = total + NEAR[k] * (cur[e + (k + 1)] + cur[e - (k + 1)])
            total = total + CENTRE * u
            updated = 2.0 * u - prev[e] + speed[layer] * total
            new[e] = jnp.where(edge, placed(layer), updated)


def fill_halos(low, high, cur):
    layers = cur.shape[0] - 2 * REACH
    index = lax.axis_index("gz")
    count = lax.axis_size("gz")
    place = 2 * (index // 4) + my_half()
    inside = (place > 0) & (place < count // 2 - 1)
    for d in range(REACH):
        cur[REACH - 1 - d] = jnp.where(inside, low[d], 0.0)
        cur[REACH + layers + d] = high[REACH - 1 - d]


def add_trace(step, traces, new):
    @pl.when(lax.axis_index("gz") == 2)
    def _():
        new[REACH] = new[REACH] + traces[step].astype(jnp.float32)


def keep_snapshot(step, phase, new, snap):
    count, _, layers, rows, _ = snap.shape
    window = step // SNAP_EVERY

    @pl.when(phase[window] == step - window * SNAP_EVERY)
    def _():
        def one_layer(j, carry):
            place = place_of(j, layers)
            for strip in range(count):
                snap[strip, window, place] = new[REACH + j, strip * rows : (strip + 1) * rows, :]
            return carry

        lax.fori_loop(0, layers, one_layer, 0)


def border_layers(layers):
    return list(range(REACH)) + list(range(layers - REACH, layers))


def border_kernel(step, faces, across, along, low, high, traces, speed, *rest):
    face, (cur_in, prev, cur, new, low_out, high_out) = rest[:faces], rest[faces:]
    layers = speed.shape[0]
    fill_halos(low, high, cur)
    advance(step, across, along, cur, prev, speed, face, new, border_layers(layers))
    add_trace(step, traces, new)
    low_out[...] = new[REACH : 2 * REACH]
    high_out[...] = new[layers : layers + REACH]


def inner_kernel(step, faces, keep, phase, across, along, speed, *rest):
    face, rest = rest[:faces], rest[faces:]
    cur, prev, new = rest[0], rest[1], rest[-2] if keep else rest[-1]
    layers = speed.shape[0]
    advance(step, across, along, cur, prev, speed, face, new, list(range(REACH, layers - REACH)))
    if keep:
        keep_snapshot(step, phase, new, rest[-1])


def last_kernel(step, phase, across, along, low, high, traces, speed, face, cur_in, prev, snap_in, cur, new, snap, out_a, out_b, send):
    layers = speed.shape[0]
    fill_halos(low, high, cur)
    advance(step, across, along, cur, prev, speed, (face,), new, border_layers(layers))
    add_trace(step, traces, new)
    keep_snapshot(step, phase, new, snap)

    def run(j, q, which):
        (out_a, out_b)[which][q] = new[REACH + j]

    for_each_part(layers, run)

    def one_strip(strip, carry):
        send[strip] = snap[strip]
        return carry

    lax.fori_loop(0, snap.shape[0], one_strip, 0)


def image_kernel(shifts, gathered, out, light, stage, sem):
    _, _, layers, rows, nx = gathered.shape
    lags, depth = out.shape[:2]
    size = layers * rows
    blocks = depth // layers
    table = sweep_table(depth)

    carried = jnp.zeros((rows, nx), jnp.float32)
    for d in range(depth):
        block, layer = d // layers, d % layers
        device = (block // 2) * 4 + block % 2
        s0, s1 = gathered[device, 0, layer], gathered[device, 1, layer]
        carried = (s0 * s0 + s1 * s1) * table[d] + carried * (smoothing * table[d])
        light[d] = carried
    carried = jnp.zeros((rows, nx), jnp.float32)
    for d in reversed(range(depth)):
        carried = light[d] + carried * (smoothing * table[d])
        light[d] = 1.0 / (carried + damping)

    def put(block, slot):
        return pltpu.make_async_copy(
            stage.at[slot], out.at[:, pl.ds(block * layers, layers)], sem.at[slot]
        )

    def one_block(block, carry):
        slot = lax.rem(block, 2)
        device = (block // 2) * 4 + lax.rem(block, 2)
        pl.when(block >= 2)(lambda: put(block - 2, slot).wait())

        def both(device, window):
            return jnp.concatenate(split(gathered[device, window].reshape(size, nx)), axis=1)

        sources = [both(device, window) for window in range(SNAPS)]
        receivers = [both(device + 2, window) for window in range(SNAPS)]
        inverse = light[pl.ds(block * layers, layers)].reshape(size, nx)
        for lag in range(0, lags, 2):
            columns = slice(lag * nx, (lag + 2) * nx)
            raw = 0.0
            for window in range(SNAPS):
                raw = raw + jnp.dot(
                    sources[window], shifts[0, :, columns], preferred_element_type=jnp.float32
                ) * jnp.dot(receivers[window], shifts[1, :, columns], preferred_element_type=jnp.float32)
            for i in range(2):
                value = (raw[:, i * nx : (i + 1) * nx] * inverse).astype(stage.dtype)
                stage[slot, lag + i] = value.reshape(layers, rows, nx)
        put(block, slot).start()
        return carry

    lax.fori_loop(0, blocks, one_block, 0)
    for block in (blocks - 2, blocks - 1):
        put(block, block % 2).wait()


def sweep_table(depth):
    table, before = [], 0.0
    for _ in range(depth):
        before = 1.0 / (1.0 + 2.0 * smoothing - smoothing * smoothing * before)
        table.append(before)
    return table


def images(shifts, gathered, lags):
    count, _, layers, rows, nx = gathered.shape
    depth = count // 2 * layers
    return pl.pallas_call(
        image_kernel,
        out_shape=jax.ShapeDtypeStruct((lags, depth, rows, nx), jnp.bfloat16),
        in_specs=[VMEM, VMEM],
        out_specs=ANY,
        scratch_shapes=[
            pltpu.VMEM((depth, rows, nx), jnp.float32),
            pltpu.VMEM((2, lags, layers, rows, nx), jnp.bfloat16),
            pltpu.SemaphoreType.DMA((2,)),
        ],
        compiler_params=PARAMS,
        name="images",
    )(shifts, gathered)


def local(
    source_now,
    source_before,
    receiver_now,
    receiver_before,
    speed_term,
    saved_faces,
    face_steps,
    traces,
    lag_offsets,
    snap_phase,
):
    count = lax.axis_size("gz")
    own, ny, nx = source_now.shape
    layers = 2 * own
    rows = ny // count
    steps = face_steps.shape[0]
    first_pairs, second_pairs = pairs_to_fields(count)
    back_pairs = [(b, a) for a, b in second_pairs]
    between, within = pairs_of_halos(count)
    band_x, band_y = banded(nx), banded(ny)
    across = jnp.asarray(np.concatenate([band_x, band_x], axis=0), jnp.bfloat16)
    along = jnp.asarray(np.concatenate([band_y, band_y], axis=1), jnp.bfloat16)

    def regroup(a, b):
        return lax.ppermute(a, "gz", first_pairs), lax.ppermute(b, "gz", second_pairs)

    tall = held(layers + 2 * REACH, ny, nx)
    whole = f32(layers, ny, nx)
    slab = f32(REACH, ny, nx)
    half = f32(own, ny, nx)
    strips = held(count, SNAPS, layers, rows, nx)
    plane = ny * nx

    now = regroup(*choose(source_now, receiver_now, VMEM))
    before = regroup(*choose(source_before, receiver_before, VMEM))
    speed_parts = regroup(speed_term, speed_term)
    late, early, shifts = prepare(saved_faces, face_steps, lag_offsets, nx)
    early = regroup(early, early)
    late = regroup(late, late)
    cur, low, high = merge(merge_now_kernel, "merge_now", (tall, slab, slab), *now)
    low = lax.ppermute(low, "gz", between)
    high = lax.ppermute(high, "gz", within)
    prev, speed = merge(merge_rest_kernel, "merge_rest", (tall, whole), *before, *speed_parts)

    snap = None
    for step in range(steps):
        if step == EARLY:
            face = merge(merge_faces_kernel, "merge_faces", (whole,), *late)
        faces = tuple(face) if step >= EARLY else early
        wide = len(faces)
        if step < steps - 1:
            cur, new, low, high = pl.pallas_call(
                functools.partial(border_kernel, step, wide),
                out_shape=(tall, tall, slab, slab),
                in_specs=[VMEM] * (8 + wide),
                out_specs=(VMEM,) * 4,
                input_output_aliases={6 + wide: 0, 7 + wide: 1},
                compiler_params=PARAMS,
                cost_estimate=cost(60 * 8 * plane, 4 * 40 * plane),
                name="border",
            )(across, along, low, high, traces, speed, *faces, cur, prev)
            low = lax.ppermute(low, "gz", between)
            high = lax.ppermute(high, "gz", within)
        else:
            new = prev
        operands = (snap_phase, across, along, speed, *faces, cur, new)
        inner = functools.partial(
            pl.pallas_call,
            compiler_params=PARAMS,
            cost_estimate=cost(60 * (layers - 8) * plane, 4 * 40 * plane),
            name="inner",
        )
        if step < steps - 1:
            alias = {5 + wide: 0}
            if snap is not None:
                operands, alias = (*operands, snap), {5 + wide: 0, 6 + wide: 1}
            new, snap = inner(
                functools.partial(inner_kernel, step, wide, True),
                out_shape=(tall, strips),
                in_specs=[SMEM] + [VMEM] * (len(operands) - 1),
                out_specs=(VMEM,) * 2,
                input_output_aliases=alias,
            )(*operands)
        else:
            (new,) = inner(
                functools.partial(inner_kernel, step, wide, False, None),
                out_shape=(tall,),
                in_specs=[VMEM] * (len(operands) - 1),
                out_specs=(VMEM,),
                input_output_aliases={4 + wide: 0},
            )(*operands[1:])
            _, _, _, out_a, out_b, send = pl.pallas_call(
                functools.partial(last_kernel, step),
                out_shape=(tall, tall, strips, half, half, f32(*strips.shape)),
                in_specs=[SMEM] + [VMEM] * 10,
                out_specs=(VMEM,) * 6,
                input_output_aliases={8: 0, 9: 1, 10: 2},
                compiler_params=PARAMS,
                name="last",
            )(snap_phase, across, along, low, high, traces, speed, *faces, cur, new, snap)
        prev, cur = cur, new

    gathered = lax.all_to_all(send, "gz", split_axis=0, concat_axis=0, tiled=True)
    back_a = lax.ppermute(out_a, "gz", first_pairs)
    back_b = lax.ppermute(out_b, "gz", back_pairs)
    source_final, receiver_final = choose(back_a, back_b, ANY)
    image_out = images(shifts, gathered, lag_offsets.shape[0])
    return (image_out, source_final, receiver_final)


def solution(mesh):
    return jax.shard_map(
        local,
        mesh=mesh,
        in_specs=(
            P(("shot", "gz"), None, None),
            P(("shot", "gz"), None, None),
            P(("shot", "gz"), None, None),
            P(("shot", "gz"), None, None),
            P("gz", None, None),
            P("shot", None, "gz", None),
            P(),
            P("shot", None, None),
            P(),
            P(),
        ),
        out_specs=(
            P("shot", None, "gz", None),
            P(("shot", "gz"), None, None),
            P(("shot", "gz"), None, None),
        ),
        check_vma=False,
    )
```

```python
import functools

import jax
import jax.numpy as jnp
import numpy as np
from jax import lax
from jax.experimental import pallas as pl
from jax.experimental.pallas import tpu as pltpu
from jax.sharding import PartitionSpec as P

SNAP_EVERY = 6
SNAPS = 2
REACH = 4
EARLY = 2

SCALE = 5040.0
NEAR = (8064.0, -1008.0, 128.0, -9.0)
CENTRE = -43050.0
damping = 0.25
smoothing = 16.0

VMEM = pl.BlockSpec(memory_space=pltpu.VMEM)
SMEM = pl.BlockSpec(memory_space=pltpu.SMEM)
ANY = pl.BlockSpec(memory_space=pl.ANY)
PARAMS = pltpu.CompilerParams(vmem_limit_bytes=24 * 1024 * 1024)


def f32(*shape):
    return jax.ShapeDtypeStruct(shape, jnp.float32)


def held(*shape):
    return pltpu.VMEM(shape, jnp.float32)


def cost(flops, bytes_accessed):
    return pl.CostEstimate(flops=int(flops), bytes_accessed=int(bytes_accessed), transcendentals=0)


def banded(size):
    apart = np.abs(np.arange(size)[:, None] - np.arange(size)[None, :])
    table = np.zeros((size, size), np.float32)
    for k, weight in enumerate(NEAR):
        table[apart == k + 1] = weight
    return table


def pairs_to_fields(count):
    first, second = [], []
    for base in range(0, count, 4):
        first += [(base, base), (base + 1, base + 2), (base + 2, base + 1), (base + 3, base + 3)]
        second += [(base, base + 2), (base + 1, base), (base + 2, base + 3), (base + 3, base + 1)]
    return first, second


def pairs_of_halos(count):
    within = [(i, i ^ 1) for i in range(count)]
    between = [(0, 2), (2, 0), (count - 3, count - 1), (count - 1, count - 3)]
    for group in range(count // 4 - 1):
        for field in range(2):
            low, high = 4 * group + 2 * field + 1, 4 * group + 4 + 2 * field
            between += [(low, high), (high, low)]
    return between, within


def my_field():
    return lax.rem(lax.axis_index("gz") // 2, 2)


def my_half():
    return lax.rem(lax.axis_index("gz"), 2)


def place_of(local, layers):
    return jnp.where(my_half() == 0, local, layers - 1 - local)


def choose_kernel(here, there, first, second, sem):
    def copies(a, b):
        return pltpu.make_async_copy(a, first, sem.at[0]), pltpu.make_async_copy(b, second, sem.at[1])

    def run(a, b):
        one, two = copies(a, b)
        one.start()
        two.start()
        one.wait()
        two.wait()

    pl.when(my_half() == 0)(lambda: run(here, there))
    pl.when(my_half() != 0)(lambda: run(there, here))


def choose(here, there, spec):
    like = jax.ShapeDtypeStruct(here.shape, here.dtype)
    return pl.pallas_call(
        choose_kernel,
        out_shape=(like, like),
        in_specs=[ANY, ANY],
        out_specs=(spec, spec),
        scratch_shapes=[pltpu.SemaphoreType.DMA((2,))],
        compiler_params=PARAMS,
        name="choose",
    )(here, there)


def prepare_kernel(face_steps, lags, faces, late, early, shifts, gathered):
    steps, layers = face_steps.shape[0], late.shape[0]
    nx = shifts.shape[1] // 2
    gathered[...] = jnp.zeros_like(gathered)

    def gather(step, layer, row):
        base = face_steps[step] * (8 * layers) + layer
        gathered[row : row + 4] = faces[pl.ds(base + 4 * layers, 4, stride=layers), :]
        gathered[row + 4 : row + 8] = faces[pl.ds(base, 4, stride=layers), :]

    for layer in range(layers):
        for step in range(EARLY):
            gather(step, layer, 8 * (EARLY * layer + step))
    early[...] = gathered[...].T

    def one_layer(layer, carry):
        for step in range(steps):
            gather(step, layer, 8 * step)
        late[layer] = gathered[...].T
        return carry

    lax.fori_loop(0, layers, one_layer, 0)

    apart = lax.broadcasted_iota(jnp.int32, (nx, nx), 1) - lax.broadcasted_iota(jnp.int32, (nx, nx), 0)
    for index in range(lags.shape[0]):
        columns = slice(index * nx, (index + 1) * nx)
        for which, lag in ((0, lags[index]), (1, -lags[index])):
            moved = jnp.where(apart == lag, 1.0, 0.0).astype(jnp.bfloat16)
            shifts[which, :nx, columns] = moved
            shifts[which, nx:, columns] = moved


def prepare(saved_faces, face_steps, lag_offsets, nx):
    slots, eight, layers, ny = saved_faces.shape
    return pl.pallas_call(
        prepare_kernel,
        out_shape=(
            f32(layers, ny, 128),
            f32(ny, 128),
            jax.ShapeDtypeStruct((2, 2 * nx, lag_offsets.shape[0] * nx), jnp.bfloat16),
        ),
        in_specs=[SMEM, SMEM, VMEM],
        out_specs=(VMEM,) * 3,
        scratch_shapes=[pltpu.VMEM((128, ny), jnp.float32)],
        compiler_params=PARAMS,
        name="prepare",
    )(face_steps, lag_offsets, saved_faces.reshape(slots * eight * layers, ny))


def for_each_part(layers, run):
    def one_layer(j, carry):
        place = place_of(j, layers)
        part = (place >= layers // 2).astype(jnp.int32)
        q = place - part * (layers // 2)
        pl.when(part == my_field())(lambda: run(j, q, 0))
        pl.when(part != my_field())(lambda: run(j, q, 1))
        return carry

    lax.fori_loop(0, layers, one_layer, 0, unroll=2)


def merge_now_kernel(now_a, now_b, cur, low, high):
    layers = 2 * now_a.shape[0]

    def run(j, q, which):
        cur[REACH + j] = (now_a, now_b)[which][q]

    for_each_part(layers, run)
    low[...] = cur[REACH : 2 * REACH]
    high[...] = cur[layers : layers + REACH]


def merge_rest_kernel(before_a, before_b, speed_a, speed_b, prev, speed):
    def run(j, q, which):
        prev[REACH + j] = (before_a, before_b)[which][q]
        speed[j] = (speed_a, speed_b)[which][q] * (1.0 / SCALE)

    for_each_part(2 * before_a.shape[0], run)


def merge_faces_kernel(face_a, face_b, face):
    def run(j, q, which):
        face[j] = (face_a, face_b)[which][q]

    for_each_part(2 * face_a.shape[0], run)


def merge(kernel, name, shapes, *parts):
    return pl.pallas_call(
        kernel,
        out_shape=shapes,
        in_specs=[VMEM] * len(parts),
        out_specs=(VMEM,) * len(shapes),
        compiler_params=PARAMS,
        name=name,
    )(*parts)


def split(u):
    high = u.astype(jnp.bfloat16)
    return high, (u - high.astype(jnp.float32)).astype(jnp.bfloat16)


def advance(step, across, along, cur, prev, speed, faces, new, local):
    layers, ny, nx = speed.shape
    column = lax.broadcasted_iota(jnp.int32, (ny, nx), 1)
    edge = ((column < REACH) | (column >= nx - REACH)) & (my_field() == 0)

    def placed(layer):
        if step >= EARLY:
            return pltpu.roll(faces[0][layer], (128 - 8 * step - REACH) % 128, axis=1)
        place = place_of(layer, layers)
        part = (place >= layers // 2).astype(jnp.int32)
        lane = 8 * (EARLY * (place - part * (layers // 2)) + step) + REACH
        held = jnp.where(part == 0, faces[0][...], faces[1][...])
        return pltpu.roll(held, lax.rem(128 - lane, 128), axis=1)

    for first in range(0, len(local), 2):
        pair = local[first : first + 2]
        inputs = [cur[REACH + layer] for layer in pair]
        halves = [split(u) for u in inputs]
        along_sum = jnp.dot(
            along[...],
            jnp.concatenate([jnp.concatenate(half, axis=0) for half in halves], axis=1),
            preferred_element_type=jnp.float32,
        )
        across_sum = jnp.dot(
            jnp.concatenate([jnp.concatenate(half, axis=1) for half in halves], axis=0),
            across[...],
            preferred_element_type=jnp.float32,
        )
        for i, layer in enumerate(pair):
            e, u = REACH + layer, inputs[i]
            total = across_sum[i * ny : (i + 1) * ny] + along_sum[:, i * nx : (i + 1) * nx]
            for k in range(REACH):
                total = total + NEAR[k] * (cur[e + (k + 1)] + cur[e - (k + 1)])
            total = total + CENTRE * u
            updated = 2.0 * u - prev[e] + speed[layer] * total
            new[e] = jnp.where(edge, placed(layer), updated)


def fill_halos(low, high, cur):
    layers = cur.shape[0] - 2 * REACH
    index = lax.axis_index("gz")
    count = lax.axis_size("gz")
    place = 2 * (index // 4) + my_half()
    inside = (place > 0) & (place < count // 2 - 1)
    for d in range(REACH):
        cur[REACH - 1 - d] = jnp.where(inside, low[d], 0.0)
        cur[REACH + layers + d] = high[REACH - 1 - d]


def add_trace(step, traces, new):
    @pl.when(lax.axis_index("gz") == 2)
    def _():
        new[REACH] = new[REACH] + traces[step].astype(jnp.float32)


def keep_snapshot(step, phase, new, snap):
    count, layers, rows, _ = snap.shape
    window = step // SNAP_EVERY

    @pl.when(phase[window] == step - window * SNAP_EVERY)
    def _():
        def one_layer(j, carry):
            place = place_of(j, layers)
            for strip in range(count):
                snap[strip, place] = new[REACH + j, strip * rows : (strip + 1) * rows, :]
            return carry

        lax.fori_loop(0, layers, one_layer, 0)


def border_layers(layers):
    return list(range(REACH)) + list(range(layers - REACH, layers))


def border_kernel(step, faces, across, along, low, high, traces, speed, *rest):
    face, (cur_in, prev, cur, new, low_out, high_out) = rest[:faces], rest[faces:]
    layers = speed.shape[0]
    fill_halos(low, high, cur)
    advance(step, across, along, cur, prev, speed, face, new, border_layers(layers))
    add_trace(step, traces, new)
    low_out[...] = new[REACH : 2 * REACH]
    high_out[...] = new[layers : layers + REACH]


def inner_kernel(step, faces, keep, phase, across, along, speed, *rest):
    face, rest = rest[:faces], rest[faces:]
    cur, prev, new = rest[0], rest[1], rest[-2] if keep else rest[-1]
    layers = speed.shape[0]
    advance(step, across, along, cur, prev, speed, face, new, list(range(REACH, layers - REACH)))
    if keep:
        keep_snapshot(step, phase, new, rest[-1])


def last_kernel(step, phase, across, along, low, high, traces, speed, face, cur_in, prev, snap_in, cur, new, snap, out_a, out_b, send):
    layers = speed.shape[0]
    fill_halos(low, high, cur)
    advance(step, across, along, cur, prev, speed, (face,), new, border_layers(layers))
    add_trace(step, traces, new)
    keep_snapshot(step, phase, new, snap)

    def run(j, q, which):
        (out_a, out_b)[which][q] = new[REACH + j]

    for_each_part(layers, run)

    def one_strip(strip, carry):
        send[strip] = snap[strip]
        return carry

    lax.fori_loop(0, snap.shape[0], one_strip, 0)


def spread_kernel(snap, own, *parts):
    groups = snap.shape[0] // 4
    group = lax.axis_index("gz") // 4

    def copy(target, first):
        def one(i, carry):
            target[i] = snap[first + i]
            return carry

        lax.fori_loop(0, target.shape[0], one, 0)

    copy(own, 4 * group)
    pieces = len(parts) // (groups - 1)
    for i, part in enumerate(parts):
        other = jnp.bitwise_xor(group, i // pieces + 1)
        copy(part, 4 * other + (i % pieces) * (4 // pieces))


def regather_kernel(own, *refs):
    parts, outs = refs[:-4], refs[-4:]
    groups = outs[0].shape[0]
    pieces = len(parts) // (groups - 1)
    size = 4 // pieces
    group = lax.axis_index("gz") // 4
    mine = lax.rem(lax.axis_index("gz"), 4)
    for which, out in enumerate(outs):
        strip = jnp.bitwise_xor(mine, which)
        out[group] = own[strip]
        for i, part in enumerate(parts):
            first = (i % pieces) * size

            @pl.when((strip >= first) & (strip < first + size))
            def _(i=i, part=part, first=first, strip=strip, out=out):
                out[jnp.bitwise_xor(group, i // pieces + 1)] = part[strip - first]


def collect_kernel(*refs):
    out = refs[-1]
    mine = lax.rem(lax.axis_index("gz"), 4)
    for which in range(4):
        source = jnp.bitwise_xor(mine, which)

        def one(group, carry):
            out[4 * group + source] = refs[which][group]
            return carry

        lax.fori_loop(0, refs[which].shape[0], one, 0)


def image_kernel(shifts, *refs):
    windows, (out, light, stage, sem) = refs[:-4], refs[-4:]
    _, layers, rows, nx = windows[0].shape
    lags, depth = out.shape[:2]
    size = layers * rows
    blocks = depth // layers
    table = sweep_table(depth)

    carried = jnp.zeros((rows, nx), jnp.float32)
    for d in range(depth):
        block, layer = d // layers, d % layers
        device = (block // 2) * 4 + block % 2
        squares = sum(window[device, layer] * window[device, layer] for window in windows)
        carried = squares * table[d] + carried * (smoothing * table[d])
        light[d] = carried
    carried = jnp.zeros((rows, nx), jnp.float32)
    for d in reversed(range(depth)):
        carried = light[d] + carried * (smoothing * table[d])
        light[d] = 1.0 / (carried + damping)

    def put(block, slot):
        return pltpu.make_async_copy(
            stage.at[slot], out.at[:, pl.ds(block * layers, layers)], sem.at[slot]
        )

    def one_block(block, carry):
        slot = lax.rem(block, 2)
        device = (block // 2) * 4 + lax.rem(block, 2)
        pl.when(block >= 2)(lambda: put(block - 2, slot).wait())

        def both(device, window):
            return jnp.concatenate(split(window[device].reshape(size, nx)), axis=1)

        sources = [both(device, window) for window in windows]
        receivers = [both(device + 2, window) for window in windows]
        inverse = light[pl.ds(block * layers, layers)].reshape(size, nx)
        for lag in range(0, lags, 2):
            columns = slice(lag * nx, (lag + 2) * nx)
            raw = 0.0
            for window in range(len(windows)):
                raw = raw + jnp.dot(
                    sources[window], shifts[0, :, columns], preferred_element_type=jnp.float32
                ) * jnp.dot(receivers[window], shifts[1, :, columns], preferred_element_type=jnp.float32)
            for i in range(2):
                value = (raw[:, i * nx : (i + 1) * nx] * inverse).astype(stage.dtype)
                stage[slot, lag + i] = value.reshape(layers, rows, nx)
        put(block, slot).start()
        return carry

    lax.fori_loop(0, blocks, one_block, 0)
    for block in (blocks - 2, blocks - 1):
        put(block, block % 2).wait()


def sweep_table(depth):
    table, before = [], 0.0
    for _ in range(depth):
        before = 1.0 / (1.0 + 2.0 * smoothing - smoothing * smoothing * before)
        table.append(before)
    return table


def images(shifts, windows, lags):
    count, layers, rows, nx = windows[0].shape
    depth = count // 2 * layers
    return pl.pallas_call(
        image_kernel,
        out_shape=jax.ShapeDtypeStruct((lags, depth, rows, nx), jnp.bfloat16),
        in_specs=[VMEM] * (1 + len(windows)),
        out_specs=ANY,
        scratch_shapes=[
            pltpu.VMEM((depth, rows, nx), jnp.float32),
            pltpu.VMEM((2, lags, layers, rows, nx), jnp.bfloat16),
            pltpu.SemaphoreType.DMA((2,)),
        ],
        compiler_params=PARAMS,
        name="images",
    )(shifts, *windows)


def local(
    source_now,
    source_before,
    receiver_now,
    receiver_before,
    speed_term,
    saved_faces,
    face_steps,
    traces,
    lag_offsets,
    snap_phase,
):
    count = lax.axis_size("gz")
    own, ny, nx = source_now.shape
    layers = 2 * own
    rows = ny // count
    steps = face_steps.shape[0]
    first_pairs, second_pairs = pairs_to_fields(count)
    back_pairs = [(b, a) for a, b in second_pairs]
    between, within = pairs_of_halos(count)
    band_x, band_y = banded(nx), banded(ny)
    across = jnp.asarray(np.concatenate([band_x, band_x], axis=0), jnp.bfloat16)
    along = jnp.asarray(np.concatenate([band_y, band_y], axis=1), jnp.bfloat16)

    def regroup(a, b):
        return lax.ppermute(a, "gz", first_pairs), lax.ppermute(b, "gz", second_pairs)

    tall = held(layers + 2 * REACH, ny, nx)
    whole = f32(layers, ny, nx)
    slab = f32(REACH, ny, nx)
    half = f32(own, ny, nx)
    strips = held(count, layers, rows, nx)
    plane = ny * nx

    now = regroup(*choose(source_now, receiver_now, VMEM))
    before = regroup(*choose(source_before, receiver_before, VMEM))
    speed_parts = regroup(speed_term, speed_term)
    late, early, shifts = prepare(saved_faces, face_steps, lag_offsets, nx)
    early = regroup(early, early)
    cur, low, high = merge(merge_now_kernel, "merge_now", (tall, slab, slab), *now)
    low = lax.ppermute(low, "gz", between)
    high = lax.ppermute(high, "gz", within)
    prev, speed = merge(merge_rest_kernel, "merge_rest", (tall, whole), *before, *speed_parts)

    groups = count // 4
    pieces = 2
    waiting, arrived = [], []

    snap = None
    for step in range(steps):
        if step % SNAP_EVERY == 0 and step:
            own_strips, *sent = merge(
                spread_kernel,
                "spread",
                (f32(4, layers, rows, nx), *[f32(4 // pieces, layers, rows, nx)] * (pieces * (groups - 1))),
                snap,
            )
            waiting = [
                (pieces_now, [(i, 4 * ((i // 4) ^ (j // pieces + 1)) + i % 4) for i in range(count)])
                for j, pieces_now in enumerate(sent)
            ]
            snap = None
        if step == EARLY:
            face = merge(merge_faces_kernel, "merge_faces", (whole,), *late)
        faces = tuple(face) if step >= EARLY else early
        wide = len(faces)
        if step < steps - 1:
            cur, new, low, high = pl.pallas_call(
                functools.partial(border_kernel, step, wide),
                out_shape=(tall, tall, slab, slab),
                in_specs=[VMEM] * (8 + wide),
                out_specs=(VMEM,) * 4,
                input_output_aliases={6 + wide: 0, 7 + wide: 1},
                compiler_params=PARAMS,
                cost_estimate=cost(60 * 8 * plane, 4 * 40 * plane),
                name="border",
            )(across, along, low, high, traces, speed, *faces, cur, prev)
            low = lax.ppermute(low, "gz", between)
            high = lax.ppermute(high, "gz", within)
        else:
            new = prev
        operands = (snap_phase, across, along, speed, *faces, cur, new)
        inner = functools.partial(
            pl.pallas_call,
            compiler_params=PARAMS,
            cost_estimate=cost(60 * (layers - 8) * plane, 4 * 40 * plane),
            name="inner",
        )
        if step < steps - 1:
            alias = {5 + wide: 0}
            if snap is not None:
                operands, alias = (*operands, snap), {5 + wide: 0, 6 + wide: 1}
            new, snap = inner(
                functools.partial(inner_kernel, step, wide, True),
                out_shape=(tall, strips),
                in_specs=[SMEM] + [VMEM] * (len(operands) - 1),
                out_specs=(VMEM,) * 2,
                input_output_aliases=alias,
            )(*operands)
        else:
            (new,) = inner(
                functools.partial(inner_kernel, step, wide, False, None),
                out_shape=(tall,),
                in_specs=[VMEM] * (len(operands) - 1),
                out_specs=(VMEM,),
                input_output_aliases={4 + wide: 0},
            )(*operands[1:])
            _, _, _, out_a, out_b, send = pl.pallas_call(
                functools.partial(last_kernel, step),
                out_shape=(tall, tall, strips, half, half, f32(*strips.shape)),
                in_specs=[SMEM] + [VMEM] * 10,
                out_specs=(VMEM,) * 6,
                input_output_aliases={8: 0, 9: 1, 10: 2},
                compiler_params=PARAMS,
                name="last",
            )(snap_phase, across, along, low, high, traces, speed, *faces, cur, new, snap)
        if step == 0:
            late, new = lax.optimization_barrier((late, new))
            late = regroup(late, late)
        left = steps - 1 - step
        now_many = -(-len(waiting) // left) if left else len(waiting)
        for payload, pairs in waiting[:now_many]:
            payload, new = lax.optimization_barrier((payload, new))
            arrived.append(lax.ppermute(payload, "gz", pairs))
        waiting = waiting[now_many:]
        prev, cur = cur, new

    mine, *others = merge(
        regather_kernel, "regather", (f32(groups, layers, rows, nx),) * 4, own_strips, *arrived
    )
    others = [
        lax.ppermute(other, "gz", [(i, i ^ (which + 1)) for i in range(count)]) for which, other in enumerate(others)
    ]
    (first,) = merge(collect_kernel, "collect", (f32(count, layers, rows, nx),), mine, *others)
    second = lax.all_to_all(send, "gz", split_axis=0, concat_axis=0, tiled=True)
    back_a = lax.ppermute(out_a, "gz", first_pairs)
    back_b = lax.ppermute(out_b, "gz", back_pairs)
    source_final, receiver_final = choose(back_a, back_b, ANY)
    image_out = images(shifts, (first, second), lag_offsets.shape[0])
    return (image_out, source_final, receiver_final)


def solution(mesh):
    return jax.shard_map(
        local,
        mesh=mesh,
        in_specs=(
            P(("shot", "gz"), None, None),
            P(("shot", "gz"), None, None),
            P(("shot", "gz"), None, None),
            P(("shot", "gz"), None, None),
            P("gz", None, None),
            P("shot", None, "gz", None),
            P(),
            P("shot", None, None),
            P(),
            P(),
        ),
        out_specs=(
            P("shot", None, "gz", None),
            P(("shot", "gz"), None, None),
            P(("shot", "gz"), None, None),
        ),
        check_vma=False,
    )
```

```python
import functools

import jax
import jax.numpy as jnp
import numpy as np
from jax import lax
from jax.experimental import pallas as pl
from jax.experimental.pallas import tpu as pltpu
from jax.sharding import PartitionSpec as P


SNAP_EVERY = 6
REACH = 4
EARLY = 4
PACKED = 2

SCALE = 5040.0
NEAR = (8064.0, -1008.0, 128.0, -9.0)
CENTRE = -43050.0
damping = 0.25
smoothing = 16.0

VMEM = pl.BlockSpec(memory_space=pltpu.VMEM)
SMEM = pl.BlockSpec(memory_space=pltpu.SMEM)
ANY = pl.BlockSpec(memory_space=pl.ANY)
PARAMS = pltpu.CompilerParams(vmem_limit_bytes=24 * 1024 * 1024)


def f32(*shape):
    return jax.ShapeDtypeStruct(shape, jnp.float32)


def held(*shape):
    return pltpu.VMEM(shape, jnp.float32)


def cost(flops, bytes_accessed):
    return pl.CostEstimate(flops=int(flops), bytes_accessed=int(bytes_accessed), transcendentals=0)


def banded(size):
    apart = np.abs(np.arange(size)[:, None] - np.arange(size)[None, :])
    table = np.zeros((size, size), np.float32)
    for k, weight in enumerate(NEAR):
        table[apart == k + 1] = weight
    return table


def pairs_to_fields(count):
    first, second = [], []
    for base in range(0, count, 4):
        first += [(base, base), (base + 1, base + 2), (base + 2, base + 1), (base + 3, base + 3)]
        second += [(base, base + 2), (base + 1, base), (base + 2, base + 3), (base + 3, base + 1)]
    return first, second


def pairs_of_halos(count):
    within = [(i, i ^ 1) for i in range(count)]
    between = [(0, 2), (2, 0), (count - 3, count - 1), (count - 1, count - 3)]
    for group in range(count // 4 - 1):
        for field in range(2):
            low, high = 4 * group + 2 * field + 1, 4 * group + 4 + 2 * field
            between += [(low, high), (high, low)]
    return between, within


def my_field():
    return lax.rem(lax.axis_index("gz") // 2, 2)


def my_half():
    return lax.rem(lax.axis_index("gz"), 2)


def place_of(local, layers):
    return jnp.where(my_half() == 0, local, layers - 1 - local)


def choose_kernel(here, there, first, second, sem):
    def copies(a, b):
        return pltpu.make_async_copy(a, first, sem.at[0]), pltpu.make_async_copy(b, second, sem.at[1])

    def run(a, b):
        one, two = copies(a, b)
        one.start()
        two.start()
        one.wait()
        two.wait()

    pl.when(my_half() == 0)(lambda: run(here, there))
    pl.when(my_half() != 0)(lambda: run(there, here))


def choose(here, there, spec):
    like = jax.ShapeDtypeStruct(here.shape, here.dtype)
    return pl.pallas_call(
        choose_kernel,
        out_shape=(like, like),
        in_specs=[ANY, ANY],
        out_specs=(spec, spec),
        scratch_shapes=[pltpu.SemaphoreType.DMA((2,))],
        compiler_params=PARAMS,
        name="choose",
    )(here, there)


def prepare_kernel(face_steps, lags, faces, late, early, shifts, gathered):
    steps, layers = face_steps.shape[0], late.shape[0]
    nx = shifts.shape[1] // 2
    gathered[...] = jnp.zeros_like(gathered)

    def gather(step, layer, row):
        base = face_steps[step] * (8 * layers) + layer
        gathered[row : row + 4] = faces[pl.ds(base + 4 * layers, 4, stride=layers), :]
        gathered[row + 4 : row + 8] = faces[pl.ds(base, 4, stride=layers), :]

    for plane in range(EARLY // PACKED):
        for layer in range(layers):
            for step in range(PACKED):
                gather(PACKED * plane + step, layer, 8 * (PACKED * layer + step))
        early[plane] = gathered[...].T

    def one_layer(layer, carry):
        for step in range(steps):
            gather(step, layer, 8 * step)
        late[layer] = gathered[...].T
        return carry

    lax.fori_loop(0, layers, one_layer, 0)

    apart = lax.broadcasted_iota(jnp.int32, (nx, nx), 1) - lax.broadcasted_iota(jnp.int32, (nx, nx), 0)
    for index in range(lags.shape[0]):
        columns = slice(index * nx, (index + 1) * nx)
        for which, lag in ((0, lags[index]), (1, -lags[index])):
            moved = jnp.where(apart == lag, 1.0, 0.0).astype(jnp.bfloat16)
            shifts[which, :nx, columns] = moved
            shifts[which, nx:, columns] = moved


def prepare(saved_faces, face_steps, lag_offsets, nx):
    slots, eight, layers, ny = saved_faces.shape
    return pl.pallas_call(
        prepare_kernel,
        out_shape=(
            f32(layers, ny, 128),
            f32(EARLY // PACKED, ny, 128),
            jax.ShapeDtypeStruct((2, 2 * nx, lag_offsets.shape[0] * nx), jnp.bfloat16),
        ),
        in_specs=[SMEM, SMEM, VMEM],
        out_specs=(VMEM,) * 3,
        scratch_shapes=[pltpu.VMEM((128, ny), jnp.float32)],
        compiler_params=PARAMS,
        name="prepare",
    )(face_steps, lag_offsets, saved_faces.reshape(slots * eight * layers, ny))


def for_each_part(layers, run):
    def one_layer(j, carry):
        place = place_of(j, layers)
        part = (place >= layers // 2).astype(jnp.int32)
        q = place - part * (layers // 2)
        pl.when(part == my_field())(lambda: run(j, q, 0))
        pl.when(part != my_field())(lambda: run(j, q, 1))
        return carry

    lax.fori_loop(0, layers, one_layer, 0, unroll=2)


def merge_now_kernel(now_a, now_b, cur, low, high):
    layers = 2 * now_a.shape[0]

    def run(j, q, which):
        cur[REACH + j] = (now_a, now_b)[which][q]

    for_each_part(layers, run)
    low[...] = cur[REACH : 2 * REACH]
    high[...] = cur[layers : layers + REACH]


def merge_rest_kernel(before_a, before_b, speed_a, speed_b, prev, speed):
    def run(j, q, which):
        prev[REACH + j] = (before_a, before_b)[which][q]
        speed[j] = (speed_a, speed_b)[which][q] * (1.0 / SCALE)

    for_each_part(2 * before_a.shape[0], run)


def merge_faces_kernel(face_a, face_b, face):
    def run(j, q, which):
        face[j] = (face_a, face_b)[which][q]

    for_each_part(2 * face_a.shape[0], run)


def merge(kernel, shapes, *parts):
    return pl.pallas_call(
        kernel, out_shape=shapes, in_specs=[VMEM] * len(parts), out_specs=(VMEM,) * len(shapes), compiler_params=PARAMS
    )(*parts)


def split(u):
    high = u.astype(jnp.bfloat16)
    return high, (u - high.astype(jnp.float32)).astype(jnp.bfloat16)


def advance(step, across, along, cur, prev, speed, faces, new, local):
    layers, ny, nx = speed.shape
    column = lax.broadcasted_iota(jnp.int32, (ny, nx), 1)
    edge = ((column < REACH) | (column >= nx - REACH)) & (my_field() == 0)

    def placed(layer):
        if step >= EARLY:
            return pltpu.roll(faces[0][layer], (128 - 8 * step - REACH) % 128, axis=1)
        place = place_of(layer, layers)
        part = (place >= layers // 2).astype(jnp.int32)
        plane, inside = step // PACKED, step % PACKED
        lane = 8 * (PACKED * (place - part * (layers // 2)) + inside) + REACH
        held = jnp.where(part == 0, faces[0][plane], faces[1][plane])
        return pltpu.roll(held, lax.rem(128 - lane, 128), axis=1)

    for first in range(0, len(local), 2):
        pair = local[first : first + 2]
        inputs = [cur[REACH + layer] for layer in pair]
        halves = [split(u) for u in inputs]
        along_sum = jnp.dot(
            along[...],
            jnp.concatenate([jnp.concatenate(half, axis=0) for half in halves], axis=1),
            preferred_element_type=jnp.float32,
        )
        across_sum = jnp.dot(
            jnp.concatenate([jnp.concatenate(half, axis=1) for half in halves], axis=0),
            across[...],
            preferred_element_type=jnp.float32,
        )
        for i, layer in enumerate(pair):
            e, u = REACH + layer, inputs[i]
            total = across_sum[i * ny : (i + 1) * ny] + along_sum[:, i * nx : (i + 1) * nx]
            for k in range(REACH):
                total = total + NEAR[k] * (cur[e + (k + 1)] + cur[e - (k + 1)])
            total = total + CENTRE * u
            updated = 2.0 * u - prev[e] + speed[layer] * total
            new[e] = jnp.where(edge, placed(layer), updated)


def fill_halos(low, high, cur):
    layers = cur.shape[0] - 2 * REACH
    index = lax.axis_index("gz")
    count = lax.axis_size("gz")
    place = 2 * (index // 4) + my_half()
    inside = (place > 0) & (place < count // 2 - 1)
    for d in range(REACH):
        cur[REACH - 1 - d] = jnp.where(inside, low[d], 0.0)
        cur[REACH + layers + d] = high[REACH - 1 - d]


def add_trace(step, traces, new):
    @pl.when(lax.axis_index("gz") == 2)
    def _():
        new[REACH] = new[REACH] + traces[step].astype(jnp.float32)


def keep_snapshot(step, phase, new, snap):
    count, layers, rows, _ = snap.shape
    window = step // SNAP_EVERY

    @pl.when(phase[window] == step - window * SNAP_EVERY)
    def _():
        def one_layer(j, carry):
            place = place_of(j, layers)
            for strip in range(count):
                snap[strip, place] = new[REACH + j, strip * rows : (strip + 1) * rows, :]
            return carry

        lax.fori_loop(0, layers, one_layer, 0)


def border_layers(layers):
    return list(range(REACH)) + list(range(layers - REACH, layers))


def border_kernel(step, faces, across, along, low, high, traces, speed, *rest):
    face, (cur_in, prev, cur, new, low_out, high_out) = rest[:faces], rest[faces:]
    layers = speed.shape[0]
    fill_halos(low, high, cur)
    advance(step, across, along, cur, prev, speed, face, new, border_layers(layers))
    add_trace(step, traces, new)
    low_out[...] = new[REACH : 2 * REACH]
    high_out[...] = new[layers : layers + REACH]


def inner_kernel(step, faces, keep, phase, across, along, speed, *rest):
    face, rest = rest[:faces], rest[faces:]
    cur, prev, new = rest[0], rest[1], rest[-2] if keep else rest[-1]
    layers = speed.shape[0]
    advance(step, across, along, cur, prev, speed, face, new, list(range(REACH, layers - REACH)))
    if keep:
        keep_snapshot(step, phase, new, rest[-1])


def last_kernel(step, phase, across, along, low, high, traces, speed, face, cur_in, prev, snap_in, cur, new, snap, out_a, out_b, send):
    layers = speed.shape[0]
    fill_halos(low, high, cur)
    advance(step, across, along, cur, prev, speed, (face,), new, border_layers(layers))
    add_trace(step, traces, new)
    keep_snapshot(step, phase, new, snap)

    def run(j, q, which):
        (out_a, out_b)[which][q] = new[REACH + j]

    for_each_part(layers, run)

    def one_strip(strip, carry):
        send[strip] = snap[strip]
        return carry

    lax.fori_loop(0, snap.shape[0], one_strip, 0)


def spread_kernel(snap, own, *parts):
    groups = snap.shape[0] // 4
    group = lax.axis_index("gz") // 4

    def copy(target, first):
        def one(i, carry):
            target[i] = snap[first + i]
            return carry

        lax.fori_loop(0, target.shape[0], one, 0)

    copy(own, 4 * group)
    pieces = len(parts) // (groups - 1)
    for i, part in enumerate(parts):
        other = jnp.bitwise_xor(group, i // pieces + 1)
        copy(part, 4 * other + (i % pieces) * (4 // pieces))


def regather_kernel(own, *refs):
    parts, outs = refs[:-4], refs[-4:]
    groups = outs[0].shape[0]
    pieces = len(parts) // (groups - 1)
    size = 4 // pieces
    group = lax.axis_index("gz") // 4
    mine = lax.rem(lax.axis_index("gz"), 4)
    for which, out in enumerate(outs):
        strip = jnp.bitwise_xor(mine, which)
        out[group] = own[strip]
        for i, part in enumerate(parts):
            first = (i % pieces) * size

            @pl.when((strip >= first) & (strip < first + size))
            def _(i=i, part=part, first=first, strip=strip, out=out):
                out[jnp.bitwise_xor(group, i // pieces + 1)] = part[strip - first]


def collect_kernel(*refs):
    out = refs[-1]
    mine = lax.rem(lax.axis_index("gz"), 4)
    for which in range(4):
        source = jnp.bitwise_xor(mine, which)

        def one(group, carry):
            out[4 * group + source] = refs[which][group]
            return carry

        lax.fori_loop(0, refs[which].shape[0], one, 0)


def image_kernel(shifts, *refs):
    windows, (out, light, stage, sem) = refs[:-4], refs[-4:]
    _, layers, rows, nx = windows[0].shape
    lags, depth = out.shape[:2]
    size = layers * rows
    blocks = depth // layers
    table = sweep_table(depth)

    carried = jnp.zeros((rows, nx), jnp.float32)
    for d in range(depth):
        block, layer = d // layers, d % layers
        device = (block // 2) * 4 + block % 2
        squares = sum(window[device, layer] * window[device, layer] for window in windows)
        carried = squares * table[d] + carried * (smoothing * table[d])
        light[d] = carried
    carried = jnp.zeros((rows, nx), jnp.float32)
    for d in reversed(range(depth)):
        carried = light[d] + carried * (smoothing * table[d])
        light[d] = 1.0 / (carried + damping)

    def put(block, slot):
        return pltpu.make_async_copy(
            stage.at[slot], out.at[:, pl.ds(block * layers, layers)], sem.at[slot]
        )

    def one_block(block, carry):
        slot = lax.rem(block, 2)
        device = (block // 2) * 4 + lax.rem(block, 2)
        pl.when(block >= 2)(lambda: put(block - 2, slot).wait())

        def both(device, window):
            return jnp.concatenate(split(window[device].reshape(size, nx)), axis=1)

        sources = [both(device, window) for window in windows]
        receivers = [both(device + 2, window) for window in windows]
        inverse = light[pl.ds(block * layers, layers)].reshape(size, nx)
        for lag in range(0, lags, 2):
            columns = slice(lag * nx, (lag + 2) * nx)
            raw = 0.0
            for window in range(len(windows)):
                raw = raw + jnp.dot(
                    sources[window], shifts[0, :, columns], preferred_element_type=jnp.float32
                ) * jnp.dot(receivers[window], shifts[1, :, columns], preferred_element_type=jnp.float32)
            for i in range(2):
                value = (raw[:, i * nx : (i + 1) * nx] * inverse).astype(stage.dtype)
                stage[slot, lag + i] = value.reshape(layers, rows, nx)
        put(block, slot).start()
        return carry

    lax.fori_loop(0, blocks, one_block, 0)
    for block in (blocks - 2, blocks - 1):
        put(block, block % 2).wait()


def sweep_table(depth):
    table, before = [], 0.0
    for _ in range(depth):
        before = 1.0 / (1.0 + 2.0 * smoothing - smoothing * smoothing * before)
        table.append(before)
    return table


def images(shifts, windows, lags):
    count, layers, rows, nx = windows[0].shape
    depth = count // 2 * layers
    return pl.pallas_call(
        image_kernel,
        out_shape=jax.ShapeDtypeStruct((lags, depth, rows, nx), jnp.bfloat16),
        in_specs=[VMEM] * (1 + len(windows)),
        out_specs=ANY,
        scratch_shapes=[
            pltpu.VMEM((depth, rows, nx), jnp.float32),
            pltpu.VMEM((2, lags, layers, rows, nx), jnp.bfloat16),
            pltpu.SemaphoreType.DMA((2,)),
        ],
        compiler_params=PARAMS,
        name="images",
    )(shifts, *windows)


def local(
    source_now,
    source_before,
    receiver_now,
    receiver_before,
    speed_term,
    saved_faces,
    face_steps,
    traces,
    lag_offsets,
    snap_phase,
):
    count = lax.axis_size("gz")
    own, ny, nx = source_now.shape
    layers = 2 * own
    rows = ny // count
    steps = face_steps.shape[0]
    first_pairs, second_pairs = pairs_to_fields(count)
    back_pairs = [(b, a) for a, b in second_pairs]
    between, within = pairs_of_halos(count)
    band_x, band_y = banded(nx), banded(ny)
    across = jnp.asarray(np.concatenate([band_x, band_x], axis=0), jnp.bfloat16)
    along = jnp.asarray(np.concatenate([band_y, band_y], axis=1), jnp.bfloat16)

    def regroup(a, b):
        return lax.ppermute(a, "gz", first_pairs), lax.ppermute(b, "gz", second_pairs)

    tall = held(layers + 2 * REACH, ny, nx)
    whole = f32(layers, ny, nx)
    slab = f32(REACH, ny, nx)
    half = f32(own, ny, nx)
    strips = held(count, layers, rows, nx)
    plane = ny * nx

    now = regroup(*choose(source_now, receiver_now, VMEM))
    before = regroup(*choose(source_before, receiver_before, VMEM))
    speed_parts = regroup(speed_term, speed_term)
    late, early, shifts = prepare(saved_faces, face_steps, lag_offsets, nx)
    early = regroup(early, early)
    cur, low, high = merge(merge_now_kernel, (tall, slab, slab), *now)
    low = lax.ppermute(low, "gz", between)
    high = lax.ppermute(high, "gz", within)
    prev, speed = merge(merge_rest_kernel, (tall, whole), *before, *speed_parts)

    groups = count // 4
    pieces = max(1, 8 // groups)
    waiting, under_way, arrived = [], [], []

    snap = None
    for step in range(steps):
        if step % SNAP_EVERY == 0 and step:
            own_strips, *sent = merge(
                spread_kernel,
                (f32(4, layers, rows, nx), *[f32(4 // pieces, layers, rows, nx)] * (pieces * (groups - 1))),
                snap,
            )
            waiting = [
                (pieces_now, [(i, 4 * ((i // 4) ^ (j // pieces + 1)) + i % 4) for i in range(count)])
                for j, pieces_now in enumerate(sent)
            ]
            snap = None
        if step == EARLY:
            face = merge(merge_faces_kernel, (whole,), *late)
        faces = tuple(face) if step >= EARLY else early
        wide = len(faces)
        if step < steps - 1:
            border = pl.pallas_call(
                functools.partial(border_kernel, step, wide),
                out_shape=(tall, tall, slab, slab),
                in_specs=[VMEM] * (8 + wide),
                out_specs=(VMEM,) * 4,
                input_output_aliases={6 + wide: 0, 7 + wide: 1},
                compiler_params=PARAMS,
                cost_estimate=cost(60 * 8 * plane, 4 * 40 * plane),
                name="border",
            )
            cur, new, low, high = border(across, along, low, high, traces, speed, *faces, cur, prev)
            low = lax.ppermute(low, "gz", between)
            high = lax.ppermute(high, "gz", within)
            low, *under_way = lax.optimization_barrier((low, *under_way))
            arrived, under_way = arrived + under_way, []
        else:
            new = prev
        operands = (snap_phase, across, along, speed, *faces, cur, new)
        inner = functools.partial(
            pl.pallas_call,
            compiler_params=PARAMS,
            cost_estimate=cost(60 * (layers - 8) * plane, 4 * 40 * plane),
            name="inner",
        )
        if step < steps - 1:
            alias = {5 + wide: 0}
            if snap is not None:
                operands, alias = (*operands, snap), {5 + wide: 0, 6 + wide: 1}
            new, snap = inner(
                functools.partial(inner_kernel, step, wide, True),
                out_shape=(tall, strips),
                in_specs=[SMEM] + [VMEM] * (len(operands) - 1),
                out_specs=(VMEM,) * 2,
                input_output_aliases=alias,
            )(*operands)
        else:
            (new,) = inner(
                functools.partial(inner_kernel, step, wide, False, None),
                out_shape=(tall,),
                in_specs=[VMEM] * (len(operands) - 1),
                out_specs=(VMEM,),
                input_output_aliases={4 + wide: 0},
            )(*operands[1:])
            last = pl.pallas_call(
                functools.partial(last_kernel, step),
                out_shape=(tall, tall, strips, half, half, f32(*strips.shape)),
                in_specs=[SMEM] + [VMEM] * 10,
                out_specs=(VMEM,) * 6,
                input_output_aliases={8: 0, 9: 1, 10: 2},
                compiler_params=PARAMS,
                name="last",
            )
            _, _, _, out_a, out_b, send = last(snap_phase, across, along, low, high, traces, speed, *faces, cur, new, snap)
        if step == 0:
            late, new = lax.optimization_barrier((late, new))
            late = regroup(late, late)
        left = steps - 1 - step
        now_many = -(-len(waiting) // left) if left else len(waiting)
        for payload, pairs in waiting[:now_many]:
            payload, new = lax.optimization_barrier((payload, new))
            under_way.append(lax.ppermute(payload, "gz", pairs))
        waiting = waiting[now_many:]
        prev, cur = cur, new

    mine, *others = merge(regather_kernel, (f32(groups, layers, rows, nx),) * 4, own_strips, *arrived, *under_way)
    others = [
        lax.ppermute(other, "gz", [(i, i ^ (which + 1)) for i in range(count)]) for which, other in enumerate(others)
    ]
    (first,) = merge(collect_kernel, (f32(count, layers, rows, nx),), mine, *others)
    second = lax.all_to_all(send, "gz", split_axis=0, concat_axis=0, tiled=True)
    back_a = lax.ppermute(out_a, "gz", first_pairs)
    back_b = lax.ppermute(out_b, "gz", back_pairs)
    source_final, receiver_final = choose(back_a, back_b, ANY)
    image_out = images(shifts, (first, second), lag_offsets.shape[0])
    return (image_out, source_final, receiver_final)


def solution(mesh):
    return jax.shard_map(
        local,
        mesh=mesh,
        in_specs=(
            P(("shot", "gz"), None, None),
            P(("shot", "gz"), None, None),
            P(("shot", "gz"), None, None),
            P(("shot", "gz"), None, None),
            P("gz", None, None),
            P("shot", None, "gz", None),
            P(),
            P("shot", None, None),
            P(),
            P(),
        ),
        out_specs=(
            P("shot", None, "gz", None),
            P(("shot", "gz"), None, None),
            P(("shot", "gz"), None, None),
        ),
        check_vma=False,
    )
```

```python
import functools

import jax
import jax.numpy as jnp
import numpy as np
from jax import lax
from jax.experimental import pallas as pl
from jax.experimental.pallas import tpu as pltpu
from jax.sharding import PartitionSpec as P


SNAP_EVERY = 6
REACH = 4
EARLY = 4
PACKED = 2

SCALE = 5040.0
NEAR = (8064.0, -1008.0, 128.0, -9.0)
CENTRE = -43050.0
damping = 0.25
smoothing = 16.0

VMEM = pl.BlockSpec(memory_space=pltpu.VMEM)
SMEM = pl.BlockSpec(memory_space=pltpu.SMEM)
ANY = pl.BlockSpec(memory_space=pl.ANY)
HBM = pl.BlockSpec(memory_space=pltpu.HBM)
PARAMS = pltpu.CompilerParams(vmem_limit_bytes=24 * 1024 * 1024)


def f32(*shape):
    return jax.ShapeDtypeStruct(shape, jnp.float32)


def held(*shape):
    return pltpu.VMEM(shape, jnp.float32)


def cost(flops, bytes_accessed):
    return pl.CostEstimate(flops=int(flops), bytes_accessed=int(bytes_accessed), transcendentals=0)


def banded(size):
    apart = np.abs(np.arange(size)[:, None] - np.arange(size)[None, :])
    table = np.zeros((size, size), np.float32)
    for k, weight in enumerate(NEAR):
        table[apart == k + 1] = weight
    return table


def pairs_to_fields(count):
    first, second = [], []
    for base in range(0, count, 4):
        first += [(base, base), (base + 1, base + 2), (base + 2, base + 1), (base + 3, base + 3)]
        second += [(base, base + 2), (base + 1, base), (base + 2, base + 3), (base + 3, base + 1)]
    return first, second


def pairs_of_halos(count):
    within = [(i, i ^ 1) for i in range(count)]
    between = [(0, 2), (2, 0), (count - 3, count - 1), (count - 1, count - 3)]
    for group in range(count // 4 - 1):
        for field in range(2):
            low, high = 4 * group + 2 * field + 1, 4 * group + 4 + 2 * field
            between += [(low, high), (high, low)]
    return between, within


def my_field():
    return lax.rem(lax.axis_index("gz") // 2, 2)


def my_half():
    return lax.rem(lax.axis_index("gz"), 2)


def place_of(local, layers):
    return jnp.where(my_half() == 0, local, layers - 1 - local)


def in_order(run, here, there):
    pl.when(my_half() == 0)(lambda: run(here, there))
    pl.when(my_half() != 0)(lambda: run(there, here))


def copy_both(pairs, sem):
    copies = [pltpu.make_async_copy(a, b, sem.at[i]) for i, (a, b) in enumerate(pairs)]
    for copy in copies:
        copy.start()
    for copy in copies:
        copy.wait()


def choose_kernel(here, there, first, second, sem):
    in_order(lambda a, b: copy_both(((a, first), (b, second)), sem), here, there)


def choose_back_kernel(here, there, first, second, one, two, sem):
    in_order(lambda a, b: copy_both(((a, one), (b, two)), sem), here, there)
    copy_both(((one, first), (two, second)), sem)


def choose(here, there, back=False):
    like = jax.ShapeDtypeStruct(here.shape, here.dtype)
    staged = [pltpu.VMEM(here.shape, here.dtype)] * 2 if back else []
    return pl.pallas_call(
        choose_back_kernel if back else choose_kernel,
        out_shape=(like, like),
        in_specs=[ANY if back else HBM] * 2,
        out_specs=(ANY if back else VMEM,) * 2,
        scratch_shapes=[*staged, pltpu.SemaphoreType.DMA((2,))],
        compiler_params=PARAMS,
        name="choose",
    )(here, there)


def prepare_kernel(face_steps, lags, faces, late, early, shifts, gathered):
    steps, layers = face_steps.shape[0], late.shape[0]
    nx = shifts.shape[1] // 2
    gathered[...] = jnp.zeros_like(gathered)

    def gather(step, layer, row):
        base = face_steps[step] * (8 * layers) + layer
        gathered[row : row + 4] = faces[pl.ds(base + 4 * layers, 4, stride=layers), :]
        gathered[row + 4 : row + 8] = faces[pl.ds(base, 4, stride=layers), :]

    for plane in range(EARLY // PACKED):
        for layer in range(layers):
            for step in range(PACKED):
                gather(PACKED * plane + step, layer, 8 * (PACKED * layer + step))
        early[plane] = gathered[...].T

    def one_layer(layer, carry):
        for step in range(steps):
            gather(step, layer, 8 * step)
        late[layer] = gathered[...].T
        return carry

    lax.fori_loop(0, layers, one_layer, 0)

    apart = lax.broadcasted_iota(jnp.int32, (nx, nx), 1) - lax.broadcasted_iota(jnp.int32, (nx, nx), 0)
    for index in range(lags.shape[0]):
        columns = slice(index * nx, (index + 1) * nx)
        for which, lag in ((0, lags[index]), (1, -lags[index])):
            moved = jnp.where(apart == lag, 1.0, 0.0).astype(jnp.bfloat16)
            shifts[which, :nx, columns] = moved
            shifts[which, nx:, columns] = moved


def prepare(saved_faces, face_steps, lag_offsets, nx):
    slots, eight, layers, ny = saved_faces.shape
    return pl.pallas_call(
        prepare_kernel,
        out_shape=(
            f32(layers, ny, 128),
            f32(EARLY // PACKED, ny, 128),
            jax.ShapeDtypeStruct((2, 2 * nx, lag_offsets.shape[0] * nx), jnp.bfloat16),
        ),
        in_specs=[SMEM, SMEM, VMEM],
        out_specs=(VMEM,) * 3,
        scratch_shapes=[pltpu.VMEM((128, ny), jnp.float32)],
        compiler_params=PARAMS,
        name="prepare",
    )(face_steps, lag_offsets, saved_faces.reshape(slots * eight * layers, ny))


def for_each_part(layers, run):
    def one_layer(j, carry):
        place = place_of(j, layers)
        part = (place >= layers // 2).astype(jnp.int32)
        q = place - part * (layers // 2)
        pl.when(part == my_field())(lambda: run(j, q, 0))
        pl.when(part != my_field())(lambda: run(j, q, 1))
        return carry

    lax.fori_loop(0, layers, one_layer, 0, unroll=2)


def merge_now_kernel(now_a, now_b, cur, low, high):
    layers = 2 * now_a.shape[0]

    def run(j, q, which):
        cur[REACH + j] = (now_a, now_b)[which][q]

    for_each_part(layers, run)
    low[...] = cur[REACH : 2 * REACH]
    high[...] = cur[layers : layers + REACH]


def merge_rest_kernel(shared, before_a, before_b, speed_a, speed_b, prev, speed):
    flipped = (lax.rem(lax.axis_index("shot"), 2) == 1) & shared

    def run(j, q, which):
        prev[REACH + j] = (before_a, before_b)[which][q]
        ahead, other = (speed_a, speed_b) if which == 0 else (speed_b, speed_a)
        speed[j] = jnp.where(flipped, other[q], ahead[q]) * (1.0 / SCALE)

    for_each_part(2 * before_a.shape[0], run)


def merge_faces_kernel(face_a, face_b, face):
    def run(j, q, which):
        face[j] = (face_a, face_b)[which][q]

    for_each_part(2 * face_a.shape[0], run)


def merge(kernel, shapes, *parts):
    return pl.pallas_call(
        kernel, out_shape=shapes, in_specs=[VMEM] * len(parts), out_specs=(VMEM,) * len(shapes), compiler_params=PARAMS
    )(*parts)


def split(u):
    high = u.astype(jnp.bfloat16)
    return high, (u - high.astype(jnp.float32)).astype(jnp.bfloat16)


def advance(step, across, along, cur, prev, speed, faces, new, local):
    layers, ny, nx = speed.shape
    column = lax.broadcasted_iota(jnp.int32, (ny, nx), 1)
    edge = ((column < REACH) | (column >= nx - REACH)) & (my_field() == 0)

    def placed(layer):
        if step >= EARLY:
            return pltpu.roll(faces[0][layer], (128 - 8 * step - REACH) % 128, axis=1)
        place = place_of(layer, layers)
        part = (place >= layers // 2).astype(jnp.int32)
        plane, inside = step // PACKED, step % PACKED
        lane = 8 * (PACKED * (place - part * (layers // 2)) + inside) + REACH
        held = jnp.where(part == 0, faces[0][plane], faces[1][plane])
        return pltpu.roll(held, lax.rem(128 - lane, 128), axis=1)

    for first in range(0, len(local), 2):
        pair = local[first : first + 2]
        inputs = [cur[REACH + layer] for layer in pair]
        halves = [split(u) for u in inputs]
        along_sum = jnp.dot(
            along[...],
            jnp.concatenate([jnp.concatenate(half, axis=0) for half in halves], axis=1),
            preferred_element_type=jnp.float32,
        )
        across_sum = jnp.dot(
            jnp.concatenate([jnp.concatenate(half, axis=1) for half in halves], axis=0),
            across[...],
            preferred_element_type=jnp.float32,
        )
        for i, layer in enumerate(pair):
            e, u = REACH + layer, inputs[i]
            total = across_sum[i * ny : (i + 1) * ny] + along_sum[:, i * nx : (i + 1) * nx]
            for k in range(REACH):
                total = total + NEAR[k] * (cur[e + (k + 1)] + cur[e - (k + 1)])
            total = total + CENTRE * u
            updated = 2.0 * u - prev[e] + speed[layer] * total
            new[e] = jnp.where(edge, placed(layer), updated)


def fill_halos(low, high, cur):
    layers = cur.shape[0] - 2 * REACH
    index = lax.axis_index("gz")
    count = lax.axis_size("gz")
    place = 2 * (index // 4) + my_half()
    inside = (place > 0) & (place < count // 2 - 1)
    for d in range(REACH):
        cur[REACH - 1 - d] = jnp.where(inside, low[d], 0.0)
        cur[REACH + layers + d] = high[REACH - 1 - d]


def add_trace(step, traces, new):
    @pl.when(lax.axis_index("gz") == 2)
    def _():
        new[REACH] = new[REACH] + traces[step].astype(jnp.float32)


def keep_snapshot(step, phase, new, snap):
    count, layers, rows, _ = snap.shape
    window = step // SNAP_EVERY

    @pl.when(phase[window] == step - window * SNAP_EVERY)
    def _():
        def one_layer(j, carry):
            place = place_of(j, layers)
            for strip in range(count):
                snap[strip, place] = new[REACH + j, strip * rows : (strip + 1) * rows, :]
            return carry

        lax.fori_loop(0, layers, one_layer, 0)


def border_layers(layers):
    return list(range(REACH)) + list(range(layers - REACH, layers))


def border_kernel(step, faces, across, along, low, high, traces, speed, *rest):
    face, (cur_in, prev, cur, new, low_out, high_out) = rest[:faces], rest[faces:]
    layers = speed.shape[0]
    fill_halos(low, high, cur)
    advance(step, across, along, cur, prev, speed, face, new, border_layers(layers))
    add_trace(step, traces, new)
    low_out[...] = new[REACH : 2 * REACH]
    high_out[...] = new[layers : layers + REACH]


def inner_kernel(step, faces, keep, phase, across, along, speed, *rest):
    face, rest = rest[:faces], rest[faces:]
    cur, prev, new = rest[0], rest[1], rest[-2] if keep else rest[-1]
    layers = speed.shape[0]
    advance(step, across, along, cur, prev, speed, face, new, list(range(REACH, layers - REACH)))
    if keep:
        keep_snapshot(step, phase, new, rest[-1])


def last_kernel(step, phase, across, along, low, high, traces, speed, face, cur_in, prev, snap_in, cur, new, snap, out_a, out_b, send):
    layers = speed.shape[0]
    fill_halos(low, high, cur)
    advance(step, across, along, cur, prev, speed, (face,), new, border_layers(layers))
    add_trace(step, traces, new)
    keep_snapshot(step, phase, new, snap)

    def run(j, q, which):
        (out_a, out_b)[which][q] = new[REACH + j]

    for_each_part(layers, run)

    def one_strip(strip, carry):
        send[strip] = snap[strip]
        return carry

    lax.fori_loop(0, snap.shape[0], one_strip, 0)


def spread_kernel(snap, *outs):
    mine = lax.rem(lax.axis_index("gz"), 4)
    for which, out in enumerate(outs):

        def one(group, carry):
            out[group] = snap[4 * group + jnp.bitwise_xor(mine, which)]
            return carry

        lax.fori_loop(0, out.shape[0], one, 0)


def regather_kernel(*refs):
    held_by, (own, *parts) = refs[:4], refs[4:]
    groups = held_by[0].shape[0]
    pieces = len(parts) // (groups - 1)
    size = 4 // pieces
    group = lax.axis_index("gz") // 4
    mine = lax.rem(lax.axis_index("gz"), 4)
    for which, strips in enumerate(held_by):
        source = jnp.bitwise_xor(mine, which)
        own[source] = strips[group]
        for i, part in enumerate(parts):
            first = (i % pieces) * size

            @pl.when((source >= first) & (source < first + size))
            def _(i=i, part=part, first=first, source=source, strips=strips):
                part[source - first] = strips[jnp.bitwise_xor(group, i // pieces + 1)]


def collect_kernel(own, *refs):
    parts, out = refs[:-1], refs[-1]
    pieces = len(parts) // (out.shape[0] // 4 - 1)
    size = 4 // pieces
    group = lax.axis_index("gz") // 4
    for i in range(4):
        out[4 * group + i] = own[i]
    for i, part in enumerate(parts):
        first = 4 * jnp.bitwise_xor(group, i // pieces + 1) + (i % pieces) * size
        for j in range(size):
            out[first + j] = part[j]


def image_kernel(shifts, *refs):
    windows, (out, light, stage, sem) = refs[:-4], refs[-4:]
    _, layers, rows, nx = windows[0].shape
    lags, depth = out.shape[:2]
    size = layers * rows
    blocks = depth // layers
    table = sweep_table(depth)

    carried = jnp.zeros((rows, nx), jnp.float32)
    for d in range(depth):
        block, layer = d // layers, d % layers
        device = (block // 2) * 4 + block % 2
        squares = sum(window[device, layer] * window[device, layer] for window in windows)
        carried = squares * table[d] + carried * (smoothing * table[d])
        light[d] = carried
    carried = jnp.zeros((rows, nx), jnp.float32)
    for d in reversed(range(depth)):
        carried = light[d] + carried * (smoothing * table[d])
        light[d] = 1.0 / (carried + damping)

    def put(block, slot):
        return pltpu.make_async_copy(
            stage.at[slot], out.at[:, pl.ds(block * layers, layers)], sem.at[slot]
        )

    def one_block(block, carry):
        slot = lax.rem(block, 2)
        device = (block // 2) * 4 + lax.rem(block, 2)
        pl.when(block >= 2)(lambda: put(block - 2, slot).wait())

        def both(device, window):
            return jnp.concatenate(split(window[device].reshape(size, nx)), axis=1)

        sources = [both(device, window) for window in windows]
        receivers = [both(device + 2, window) for window in windows]
        inverse = light[pl.ds(block * layers, layers)].reshape(size, nx)
        for lag in range(0, lags, 2):
            columns = slice(lag * nx, (lag + 2) * nx)
            raw = 0.0
            for window in range(len(windows)):
                raw = raw + jnp.dot(
                    sources[window], shifts[0, :, columns], preferred_element_type=jnp.float32
                ) * jnp.dot(receivers[window], shifts[1, :, columns], preferred_element_type=jnp.float32)
            for i in range(2):
                value = (raw[:, i * nx : (i + 1) * nx] * inverse).astype(stage.dtype)
                stage[slot, lag + i] = value.reshape(layers, rows, nx)
        put(block, slot).start()
        return carry

    lax.fori_loop(0, blocks, one_block, 0)
    for block in (blocks - 2, blocks - 1):
        put(block, block % 2).wait()


def sweep_table(depth):
    table, before = [], 0.0
    for _ in range(depth):
        before = 1.0 / (1.0 + 2.0 * smoothing - smoothing * smoothing * before)
        table.append(before)
    return table


def images(shifts, windows, lags):
    count, layers, rows, nx = windows[0].shape
    depth = count // 2 * layers
    return pl.pallas_call(
        image_kernel,
        out_shape=jax.ShapeDtypeStruct((lags, depth, rows, nx), jnp.bfloat16),
        in_specs=[VMEM] * (1 + len(windows)),
        out_specs=ANY,
        scratch_shapes=[
            pltpu.VMEM((depth, rows, nx), jnp.float32),
            pltpu.VMEM((2, lags, layers, rows, nx), jnp.bfloat16),
            pltpu.SemaphoreType.DMA((2,)),
        ],
        compiler_params=PARAMS,
        name="images",
    )(shifts, *windows)


def local(
    source_now,
    source_before,
    receiver_now,
    receiver_before,
    speed_term,
    saved_faces,
    face_steps,
    traces,
    lag_offsets,
    snap_phase,
):
    count = lax.axis_size("gz")
    own, ny, nx = source_now.shape
    layers = 2 * own
    rows = ny // count
    steps = face_steps.shape[0]
    first_pairs, second_pairs = pairs_to_fields(count)
    back_pairs = [(b, a) for a, b in second_pairs]
    between, within = pairs_of_halos(count)
    band_x, band_y = banded(nx), banded(ny)
    across = jnp.asarray(np.concatenate([band_x, band_x], axis=0), jnp.bfloat16)
    along = jnp.asarray(np.concatenate([band_y, band_y], axis=1), jnp.bfloat16)

    def regroup(a, b):
        return lax.ppermute(a, "gz", first_pairs), lax.ppermute(b, "gz", second_pairs)

    tall = held(layers + 2 * REACH, ny, nx)
    whole = f32(layers, ny, nx)
    slab = f32(REACH, ny, nx)
    half = f32(own, ny, nx)
    strips = held(count, layers, rows, nx)
    plane = ny * nx

    shots = lax.axis_size("shot")
    shared = shots % 2 == 0
    if shared:
        both = [
            (shot * count + a, shot * count + b)
            for shot in range(shots)
            for a, b in (first_pairs, second_pairs)[shot % 2]
        ]
        one = lax.ppermute(speed_term, ("shot", "gz"), both)
        speed_parts = one, lax.ppermute(one, "shot", [(shot, shot ^ 1) for shot in range(shots)])
    else:
        speed_parts = regroup(speed_term, speed_term)
    now = regroup(*choose(source_now, receiver_now))
    before = regroup(*choose(source_before, receiver_before))
    late, early, shifts = prepare(saved_faces, face_steps, lag_offsets, nx)
    early = regroup(early, early)
    cur, low, high = merge(merge_now_kernel, (tall, slab, slab), *now)
    low = lax.ppermute(low, "gz", between)
    high = lax.ppermute(high, "gz", within)
    prev, speed = merge(functools.partial(merge_rest_kernel, shared), (tall, whole), *before, *speed_parts)

    groups = count // 4
    pieces = max(1, 8 // groups)
    waiting, under_way, arrived = [], [], []

    snap = None
    for step in range(steps):
        if step == EARLY:
            face = merge(merge_faces_kernel, (whole,), *late)
        faces = tuple(face) if step >= EARLY else early
        wide = len(faces)
        if step < steps - 1:
            border = pl.pallas_call(
                functools.partial(border_kernel, step, wide),
                out_shape=(tall, tall, slab, slab),
                in_specs=[VMEM] * (8 + wide),
                out_specs=(VMEM,) * 4,
                input_output_aliases={6 + wide: 0, 7 + wide: 1},
                compiler_params=PARAMS,
                cost_estimate=cost(60 * 8 * plane, 4 * 40 * plane),
                name="border",
            )
            cur, new, low, high = border(across, along, low, high, traces, speed, *faces, cur, prev)
            low = lax.ppermute(low, "gz", between)
            high = lax.ppermute(high, "gz", within)
            low, *under_way = lax.optimization_barrier((low, *under_way))
            if step == SNAP_EVERY:
                own_strips, *sent = merge(
                    regather_kernel,
                    (f32(4, layers, rows, nx), *[f32(4 // pieces, layers, rows, nx)] * (pieces * (groups - 1))),
                    *under_way,
                )
                waiting = [
                    (part, [(i, 4 * ((i // 4) ^ (j // pieces + 1)) + i % 4) for i in range(count)])
                    for j, part in enumerate(sent)
                ]
            else:
                arrived += under_way
            under_way = []
        else:
            new = prev
        operands = (snap_phase, across, along, speed, *faces, cur, new)
        inner = functools.partial(
            pl.pallas_call,
            compiler_params=PARAMS,
            cost_estimate=cost(60 * (layers - 8) * plane, 4 * 40 * plane),
            name="inner",
        )
        if step < steps - 1:
            alias = {5 + wide: 0}
            if snap is not None:
                operands, alias = (*operands, snap), {5 + wide: 0, 6 + wide: 1}
            new, snap = inner(
                functools.partial(inner_kernel, step, wide, True),
                out_shape=(tall, strips),
                in_specs=[SMEM] + [VMEM] * (len(operands) - 1),
                out_specs=(VMEM,) * 2,
                input_output_aliases=alias,
            )(*operands)
        else:
            (new,) = inner(
                functools.partial(inner_kernel, step, wide, False, None),
                out_shape=(tall,),
                in_specs=[VMEM] * (len(operands) - 1),
                out_specs=(VMEM,),
                input_output_aliases={4 + wide: 0},
            )(*operands[1:])
            last = pl.pallas_call(
                functools.partial(last_kernel, step),
                out_shape=(tall, tall, strips, half, half, f32(*strips.shape)),
                in_specs=[SMEM] + [VMEM] * 10,
                out_specs=(VMEM,) * 6,
                input_output_aliases={8: 0, 9: 1, 10: 2},
                compiler_params=PARAMS,
                name="last",
            )
            _, _, _, out_a, out_b, send = last(snap_phase, across, along, low, high, traces, speed, *faces, cur, new, snap)
        if step == 0:
            late, new = lax.optimization_barrier((late, new))
            late = regroup(late, late)
        if step == SNAP_EVERY - 1:
            strip_parts = merge(spread_kernel, (f32(groups, layers, rows, nx),) * 4, snap)
            under_way.append(strip_parts[0])
            for which in (2, 3, 1):
                payload, new = lax.optimization_barrier((strip_parts[which], new))
                under_way.append(lax.ppermute(payload, "gz", [(i, i ^ which) for i in range(count)]))
            under_way = [under_way[i] for i in (0, 3, 1, 2)]
            snap = None
        left = steps - 1 - step
        now_many = -(-len(waiting) // left) if left else len(waiting)
        for payload, pairs in waiting[:now_many]:
            payload, new = lax.optimization_barrier((payload, new))
            under_way.append(lax.ppermute(payload, "gz", pairs))
        waiting = waiting[now_many:]
        prev, cur = cur, new

    (first,) = merge(collect_kernel, (f32(count, layers, rows, nx),), own_strips, *arrived, *under_way)
    second = lax.all_to_all(send, "gz", split_axis=0, concat_axis=0, tiled=True)
    back_a = lax.ppermute(out_a, "gz", first_pairs)
    back_b = lax.ppermute(out_b, "gz", back_pairs)
    source_final, receiver_final = choose(back_a, back_b, back=True)
    image_out = images(shifts, (first, second), lag_offsets.shape[0])
    return (image_out, source_final, receiver_final)


def solution(mesh):
    return jax.shard_map(
        local,
        mesh=mesh,
        in_specs=(
            P(("shot", "gz"), None, None),
            P(("shot", "gz"), None, None),
            P(("shot", "gz"), None, None),
            P(("shot", "gz"), None, None),
            P("gz", None, None),
            P("shot", None, "gz", None),
            P(),
            P("shot", None, None),
            P(),
            P(),
        ),
        out_specs=(
            P("shot", None, "gz", None),
            P(("shot", "gz"), None, None),
            P(("shot", "gz"), None, None),
        ),
        check_vma=False,
    )
```

```python
import functools

import jax
import jax.numpy as jnp
import numpy as np
from jax import lax
from jax.experimental import pallas as pl
from jax.experimental.pallas import tpu as pltpu
from jax.sharding import PartitionSpec as P


SNAP_EVERY = 6
REACH = 4
EARLY = 4
PACKED = 2

SCALE = 5040.0
NEAR = (8064.0, -1008.0, 128.0, -9.0)
CENTRE = -43050.0
damping = 0.25
smoothing = 16.0

VMEM = pl.BlockSpec(memory_space=pltpu.VMEM)
SMEM = pl.BlockSpec(memory_space=pltpu.SMEM)
ANY = pl.BlockSpec(memory_space=pl.ANY)
HBM = pl.BlockSpec(memory_space=pltpu.HBM)
PARAMS = pltpu.CompilerParams(vmem_limit_bytes=24 * 1024 * 1024)


def f32(*shape):
    return jax.ShapeDtypeStruct(shape, jnp.float32)


def held(*shape):
    return pltpu.VMEM(shape, jnp.float32)


def cost(flops, bytes_accessed):
    return pl.CostEstimate(flops=int(flops), bytes_accessed=int(bytes_accessed), transcendentals=0)


def banded(size):
    apart = np.abs(np.arange(size)[:, None] - np.arange(size)[None, :])
    table = np.zeros((size, size), np.float32)
    for k, weight in enumerate(NEAR):
        table[apart == k + 1] = weight
    return table


def pairs_to_fields(count):
    first, second = [], []
    for base in range(0, count, 4):
        first += [(base, base), (base + 1, base + 2), (base + 2, base + 1), (base + 3, base + 3)]
        second += [(base, base + 2), (base + 1, base), (base + 2, base + 3), (base + 3, base + 1)]
    return first, second


def pairs_of_halos(count):
    within = [(i, i ^ 1) for i in range(count)]
    between = [(0, 2), (2, 0), (count - 3, count - 1), (count - 1, count - 3)]
    for group in range(count // 4 - 1):
        for field in range(2):
            low, high = 4 * group + 2 * field + 1, 4 * group + 4 + 2 * field
            between += [(low, high), (high, low)]
    return between, within


def my_field():
    return lax.rem(lax.axis_index("gz") // 2, 2)


def my_half():
    return lax.rem(lax.axis_index("gz"), 2)


def place_of(local, layers):
    return jnp.where(my_half() == 0, local, layers - 1 - local)


def in_order(run, here, there):
    pl.when(my_half() == 0)(lambda: run(here, there))
    pl.when(my_half() != 0)(lambda: run(there, here))


def copy_both(pairs, sem):
    copies = [pltpu.make_async_copy(a, b, sem.at[i]) for i, (a, b) in enumerate(pairs)]
    for copy in copies:
        copy.start()
    for copy in copies:
        copy.wait()


def choose_kernel(here, there, first, second, sem):
    in_order(lambda a, b: copy_both(((a, first), (b, second)), sem), here, there)


def choose_back_kernel(here, there, first, second, one, two, sem):
    in_order(lambda a, b: copy_both(((a, one), (b, two)), sem), here, there)
    copy_both(((one, first), (two, second)), sem)


def choose(here, there, back=False):
    like = jax.ShapeDtypeStruct(here.shape, here.dtype)
    staged = [pltpu.VMEM(here.shape, here.dtype)] * 2 if back else []
    return pl.pallas_call(
        choose_back_kernel if back else choose_kernel,
        out_shape=(like, like),
        in_specs=[ANY if back else HBM] * 2,
        out_specs=(ANY if back else VMEM,) * 2,
        scratch_shapes=[*staged, pltpu.SemaphoreType.DMA((2,))],
        compiler_params=PARAMS,
        name="choose",
    )(here, there)


def prepare_kernel(layers, face_steps, lags, faces, late, early, shifts, gathered):
    steps = face_steps.shape[0]
    nx = shifts.shape[1] // 2
    gathered[...] = jnp.zeros_like(gathered)

    def gather(step, layer, row):
        base = face_steps[step] * (8 * layers) + layer
        gathered[row : row + 4] = faces[pl.ds(base + 4 * layers, 4, stride=layers), :]
        gathered[row + 4 : row + 8] = faces[pl.ds(base, 4, stride=layers), :]

    for plane in range(steps // PACKED):
        for layer in range(layers):
            for step in range(PACKED):
                gather(PACKED * plane + step, layer, 8 * (PACKED * layer + step))
        if plane < EARLY // PACKED:
            early[plane] = gathered[...].T
        else:
            late[plane - EARLY // PACKED] = gathered[...].T

    apart = lax.broadcasted_iota(jnp.int32, (nx, nx), 1) - lax.broadcasted_iota(jnp.int32, (nx, nx), 0)
    for index in range(lags.shape[0]):
        columns = slice(index * nx, (index + 1) * nx)
        for which, lag in ((0, lags[index]), (1, -lags[index])):
            moved = jnp.where(apart == lag, 1.0, 0.0).astype(jnp.bfloat16)
            shifts[which, :nx, columns] = moved
            shifts[which, nx:, columns] = moved


def prepare(saved_faces, face_steps, lag_offsets, nx):
    slots, eight, layers, ny = saved_faces.shape
    planes = face_steps.shape[0] // PACKED
    return pl.pallas_call(
        functools.partial(prepare_kernel, layers),
        out_shape=(
            f32(planes - EARLY // PACKED, ny, 128),
            f32(EARLY // PACKED, ny, 128),
            jax.ShapeDtypeStruct((2, 2 * nx, lag_offsets.shape[0] * nx), jnp.bfloat16),
        ),
        in_specs=[SMEM, SMEM, VMEM],
        out_specs=(VMEM,) * 3,
        scratch_shapes=[pltpu.VMEM((128, ny), jnp.float32)],
        compiler_params=PARAMS,
        name="prepare",
    )(face_steps, lag_offsets, saved_faces.reshape(slots * eight * layers, ny))


def for_each_part(layers, run):
    def one_layer(j, carry):
        place = place_of(j, layers)
        part = (place >= layers // 2).astype(jnp.int32)
        q = place - part * (layers // 2)
        pl.when(part == my_field())(lambda: run(j, q, 0))
        pl.when(part != my_field())(lambda: run(j, q, 1))
        return carry

    lax.fori_loop(0, layers, one_layer, 0, unroll=2)


def merge_now_kernel(now_a, now_b, cur, low, high):
    layers = 2 * now_a.shape[0]

    def run(j, q, which):
        cur[REACH + j] = (now_a, now_b)[which][q]

    for_each_part(layers, run)
    low[...] = cur[REACH : 2 * REACH]
    high[...] = cur[layers : layers + REACH]


def merge_rest_kernel(shared, before_a, before_b, speed_a, speed_b, prev, speed):
    flipped = (lax.rem(lax.axis_index("shot"), 2) == 1) & shared

    def run(j, q, which):
        prev[REACH + j] = (before_a, before_b)[which][q]
        ahead, other = (speed_a, speed_b) if which == 0 else (speed_b, speed_a)
        speed[j] = jnp.where(flipped, other[q], ahead[q]) * (1.0 / SCALE)

    for_each_part(2 * before_a.shape[0], run)


def merge(kernel, shapes, *parts):
    return pl.pallas_call(
        kernel, out_shape=shapes, in_specs=[VMEM] * len(parts), out_specs=(VMEM,) * len(shapes), compiler_params=PARAMS
    )(*parts)


def split(u):
    high = u.astype(jnp.bfloat16)
    return high, (u - high.astype(jnp.float32)).astype(jnp.bfloat16)


def advance(step, across, along, cur, prev, speed, faces, new, local):
    layers, ny, nx = speed.shape
    column = lax.broadcasted_iota(jnp.int32, (ny, nx), 1)
    edge = ((column < REACH) | (column >= nx - REACH)) & (my_field() == 0)

    def placed(layer):
        place = place_of(layer, layers)
        part = (place >= layers // 2).astype(jnp.int32)
        plane, inside = (step if step < EARLY else step - EARLY) // PACKED, step % PACKED
        lane = 8 * (PACKED * (place - part * (layers // 2)) + inside) + REACH
        held = jnp.where(part == 0, faces[0][plane], faces[1][plane])
        return pltpu.roll(held, lax.rem(128 - lane, 128), axis=1)

    for first in range(0, len(local), 2):
        pair = local[first : first + 2]
        inputs = [cur[REACH + layer] for layer in pair]
        halves = [split(u) for u in inputs]
        along_sum = jnp.dot(
            along[...],
            jnp.concatenate([jnp.concatenate(half, axis=0) for half in halves], axis=1),
            preferred_element_type=jnp.float32,
        )
        across_sum = jnp.dot(
            jnp.concatenate([jnp.concatenate(half, axis=1) for half in halves], axis=0),
            across[...],
            preferred_element_type=jnp.float32,
        )
        for i, layer in enumerate(pair):
            e, u = REACH + layer, inputs[i]
            total = across_sum[i * ny : (i + 1) * ny] + along_sum[:, i * nx : (i + 1) * nx]
            for k in range(REACH):
                total = total + NEAR[k] * (cur[e + (k + 1)] + cur[e - (k + 1)])
            total = total + CENTRE * u
            updated = 2.0 * u - prev[e] + speed[layer] * total
            new[e] = jnp.where(edge, placed(layer), updated)


def fill_halos(low, high, cur):
    layers = cur.shape[0] - 2 * REACH
    index = lax.axis_index("gz")
    count = lax.axis_size("gz")
    place = 2 * (index // 4) + my_half()
    inside = (place > 0) & (place < count // 2 - 1)
    for d in range(REACH):
        cur[REACH - 1 - d] = jnp.where(inside, low[d], 0.0)
        cur[REACH + layers + d] = high[REACH - 1 - d]


def add_trace(step, traces, new):
    @pl.when(lax.axis_index("gz") == 2)
    def _():
        new[REACH] = new[REACH] + traces[step].astype(jnp.float32)


def keep_snapshot(step, phase, new, snap):
    count, layers, rows, _ = snap.shape
    window = step // SNAP_EVERY

    @pl.when(phase[window] == step - window * SNAP_EVERY)
    def _():
        def one_layer(j, carry):
            place = place_of(j, layers)
            for strip in range(count):
                snap[strip, place] = new[REACH + j, strip * rows : (strip + 1) * rows, :]
            return carry

        lax.fori_loop(0, layers, one_layer, 0)


def border_layers(layers):
    return list(range(REACH)) + list(range(layers - REACH, layers))


def border_kernel(step, faces, across, along, low, high, traces, speed, *rest):
    face, (cur_in, prev, cur, new, low_out, high_out) = rest[:faces], rest[faces:]
    layers = speed.shape[0]
    fill_halos(low, high, cur)
    advance(step, across, along, cur, prev, speed, face, new, border_layers(layers))
    add_trace(step, traces, new)
    low_out[...] = new[REACH : 2 * REACH]
    high_out[...] = new[layers : layers + REACH]


def inner_kernel(step, faces, keep, phase, across, along, speed, *rest):
    face, rest = rest[:faces], rest[faces:]
    cur, prev, new = rest[0], rest[1], rest[-2] if keep else rest[-1]
    layers = speed.shape[0]
    advance(step, across, along, cur, prev, speed, face, new, list(range(REACH, layers - REACH)))
    if keep:
        keep_snapshot(step, phase, new, rest[-1])


def last_kernel(
    step, phase, across, along, low, high, traces, speed, face_a, face_b, cur_in, prev, snap_in, cur, new, snap, out_a, out_b, send
):
    layers = speed.shape[0]
    fill_halos(low, high, cur)
    advance(step, across, along, cur, prev, speed, (face_a, face_b), new, border_layers(layers))
    add_trace(step, traces, new)
    keep_snapshot(step, phase, new, snap)

    def run(j, q, which):
        (out_a, out_b)[which][q] = new[REACH + j]

    for_each_part(layers, run)

    def one_strip(strip, carry):
        send[strip] = snap[strip]
        return carry

    lax.fori_loop(0, snap.shape[0], one_strip, 0)


def spread_kernel(snap, *outs):
    mine = lax.rem(lax.axis_index("gz"), 4)
    for which, out in enumerate(outs):

        def one(group, carry):
            out[group] = snap[4 * group + jnp.bitwise_xor(mine, which)]
            return carry

        lax.fori_loop(0, out.shape[0], one, 0)


def regather_kernel(*refs):
    held_by, (own, *parts) = refs[:4], refs[4:]
    groups = held_by[0].shape[0]
    pieces = len(parts) // (groups - 1)
    size = 4 // pieces
    group = lax.axis_index("gz") // 4
    mine = lax.rem(lax.axis_index("gz"), 4)
    for which, strips in enumerate(held_by):
        source = jnp.bitwise_xor(mine, which)
        own[source] = strips[group]
        for i, part in enumerate(parts):
            first = (i % pieces) * size

            @pl.when((source >= first) & (source < first + size))
            def _(i=i, part=part, first=first, source=source, strips=strips):
                part[source - first] = strips[jnp.bitwise_xor(group, i // pieces + 1)]


def collect_kernel(own, *refs):
    parts, out = refs[:-1], refs[-1]
    pieces = len(parts) // (out.shape[0] // 4 - 1)
    size = 4 // pieces
    group = lax.axis_index("gz") // 4
    for i in range(4):
        out[4 * group + i] = own[i]
    for i, part in enumerate(parts):
        first = 4 * jnp.bitwise_xor(group, i // pieces + 1) + (i % pieces) * size
        for j in range(size):
            out[first + j] = part[j]


def image_kernel(shifts, *refs):
    windows, (out, light, stage, sem) = refs[:-4], refs[-4:]
    _, layers, rows, nx = windows[0].shape
    lags, depth = out.shape[:2]
    size = layers * rows
    blocks = depth // layers
    table = sweep_table(depth)

    carried = jnp.zeros((rows, nx), jnp.float32)
    for d in range(depth):
        block, layer = d // layers, d % layers
        device = (block // 2) * 4 + block % 2
        squares = sum(window[device, layer] * window[device, layer] for window in windows)
        carried = squares * table[d] + carried * (smoothing * table[d])
        light[d] = carried
    carried = jnp.zeros((rows, nx), jnp.float32)
    for d in reversed(range(depth)):
        carried = light[d] + carried * (smoothing * table[d])
        light[d] = 1.0 / (carried + damping)

    def put(block, slot):
        return pltpu.make_async_copy(
            stage.at[slot], out.at[:, pl.ds(block * layers, layers)], sem.at[slot]
        )

    def one_block(block, carry):
        slot = lax.rem(block, 2)
        device = (block // 2) * 4 + lax.rem(block, 2)
        pl.when(block >= 2)(lambda: put(block - 2, slot).wait())

        def both(device, window):
            return jnp.concatenate(split(window[device].reshape(size, nx)), axis=1)

        sources = [both(device, window) for window in windows]
        receivers = [both(device + 2, window) for window in windows]
        inverse = light[pl.ds(block * layers, layers)].reshape(size, nx)
        for lag in range(0, lags, 2):
            columns = slice(lag * nx, (lag + 2) * nx)
            raw = 0.0
            for window in range(len(windows)):
                raw = raw + jnp.dot(
                    sources[window], shifts[0, :, columns], preferred_element_type=jnp.float32
                ) * jnp.dot(receivers[window], shifts[1, :, columns], preferred_element_type=jnp.float32)
            for i in range(2):
                value = (raw[:, i * nx : (i + 1) * nx] * inverse).astype(stage.dtype)
                stage[slot, lag + i] = value.reshape(layers, rows, nx)
        put(block, slot).start()
        return carry

    lax.fori_loop(0, blocks, one_block, 0)
    for block in (blocks - 2, blocks - 1):
        put(block, block % 2).wait()


def sweep_table(depth):
    table, before = [], 0.0
    for _ in range(depth):
        before = 1.0 / (1.0 + 2.0 * smoothing - smoothing * smoothing * before)
        table.append(before)
    return table


def images(shifts, windows, lags):
    count, layers, rows, nx = windows[0].shape
    depth = count // 2 * layers
    return pl.pallas_call(
        image_kernel,
        out_shape=jax.ShapeDtypeStruct((lags, depth, rows, nx), jnp.bfloat16),
        in_specs=[VMEM] * (1 + len(windows)),
        out_specs=ANY,
        scratch_shapes=[
            pltpu.VMEM((depth, rows, nx), jnp.float32),
            pltpu.VMEM((2, lags, layers, rows, nx), jnp.bfloat16),
            pltpu.SemaphoreType.DMA((2,)),
        ],
        compiler_params=PARAMS,
        name="images",
    )(shifts, *windows)


def local(
    source_now,
    source_before,
    receiver_now,
    receiver_before,
    speed_term,
    saved_faces,
    face_steps,
    traces,
    lag_offsets,
    snap_phase,
):
    count = lax.axis_size("gz")
    own, ny, nx = source_now.shape
    layers = 2 * own
    rows = ny // count
    steps = face_steps.shape[0]
    first_pairs, second_pairs = pairs_to_fields(count)
    back_pairs = [(b, a) for a, b in second_pairs]
    between, within = pairs_of_halos(count)
    band_x, band_y = banded(nx), banded(ny)
    across = jnp.asarray(np.concatenate([band_x, band_x], axis=0), jnp.bfloat16)
    along = jnp.asarray(np.concatenate([band_y, band_y], axis=1), jnp.bfloat16)

    def regroup(a, b):
        return lax.ppermute(a, "gz", first_pairs), lax.ppermute(b, "gz", second_pairs)

    tall = held(layers + 2 * REACH, ny, nx)
    whole = f32(layers, ny, nx)
    slab = f32(REACH, ny, nx)
    half = f32(own, ny, nx)
    strips = held(count, layers, rows, nx)
    plane = ny * nx

    shots = lax.axis_size("shot")
    shared = shots % 2 == 0
    if shared:
        both = [
            (shot * count + a, shot * count + b)
            for shot in range(shots)
            for a, b in (first_pairs, second_pairs)[shot % 2]
        ]
        one = lax.ppermute(speed_term, ("shot", "gz"), both)
        speed_parts = one, lax.ppermute(one, "shot", [(shot, shot ^ 1) for shot in range(shots)])
    else:
        speed_parts = regroup(speed_term, speed_term)
    now = regroup(*choose(source_now, receiver_now))
    before = regroup(*choose(source_before, receiver_before))
    late, early, shifts = prepare(saved_faces, face_steps, lag_offsets, nx)
    early = regroup(early, early)
    cur, low, high = merge(merge_now_kernel, (tall, slab, slab), *now)
    low = lax.ppermute(low, "gz", between)
    high = lax.ppermute(high, "gz", within)
    prev, speed = merge(functools.partial(merge_rest_kernel, shared), (tall, whole), *before, *speed_parts)

    groups = count // 4
    pieces = max(1, 8 // groups)
    waiting, under_way, arrived = [], [], []

    snap = None
    for step in range(steps):
        faces = late if step >= EARLY else early
        wide = len(faces)
        if step < steps - 1:
            border = pl.pallas_call(
                functools.partial(border_kernel, step, wide),
                out_shape=(tall, tall, slab, slab),
                in_specs=[VMEM] * (8 + wide),
                out_specs=(VMEM,) * 4,
                input_output_aliases={6 + wide: 0, 7 + wide: 1},
                compiler_params=PARAMS,
                cost_estimate=cost(60 * 8 * plane, 4 * 40 * plane),
                name="border",
            )
            cur, new, low, high = border(across, along, low, high, traces, speed, *faces, cur, prev)
            low = lax.ppermute(low, "gz", between)
            high = lax.ppermute(high, "gz", within)
            low, *landed = lax.optimization_barrier((low, *[array for _, array in under_way]))
            if step == SNAP_EVERY:
                own_strips, *sent = merge(
                    regather_kernel,
                    (f32(4, layers, rows, nx), *[f32(4 // pieces, layers, rows, nx)] * (pieces * (groups - 1))),
                    strip_parts[0],
                    *landed,
                )
                waiting = [
                    (j < pieces, j, [(i, 4 * ((i // 4) ^ (j // pieces + 1)) + i % 4) for i in range(count)])
                    for j in range(len(sent))
                ]
            else:
                arrived += [(part, array) for (part, _), array in zip(under_way, landed)]
            under_way = []
        else:
            new = prev
        operands = (snap_phase, across, along, speed, *faces, cur, new)
        inner = functools.partial(
            pl.pallas_call,
            compiler_params=PARAMS,
            cost_estimate=cost(60 * (layers - 8) * plane, 4 * 40 * plane),
            name="inner",
        )
        if step < steps - 1:
            alias = {5 + wide: 0}
            if snap is not None:
                operands, alias = (*operands, snap), {5 + wide: 0, 6 + wide: 1}
            new, snap = inner(
                functools.partial(inner_kernel, step, wide, True),
                out_shape=(tall, strips),
                in_specs=[SMEM] + [VMEM] * (len(operands) - 1),
                out_specs=(VMEM,) * 2,
                input_output_aliases=alias,
            )(*operands)
        else:
            (new,) = inner(
                functools.partial(inner_kernel, step, wide, False, None),
                out_shape=(tall,),
                in_specs=[VMEM] * (len(operands) - 1),
                out_specs=(VMEM,),
                input_output_aliases={4 + wide: 0},
            )(*operands[1:])
            last = pl.pallas_call(
                functools.partial(last_kernel, step),
                out_shape=(tall, tall, strips, half, half, f32(*strips.shape)),
                in_specs=[SMEM] + [VMEM] * 11,
                out_specs=(VMEM,) * 6,
                input_output_aliases={9: 0, 10: 1, 11: 2},
                compiler_params=PARAMS,
                name="last",
            )
            _, _, _, out_a, out_b, send = last(snap_phase, across, along, low, high, traces, speed, *faces, cur, new, snap)
        if step == 0:
            late, new = lax.optimization_barrier((late, new))
            late = regroup(late, late)
        if step == SNAP_EVERY - 1:
            strip_parts = merge(spread_kernel, (f32(groups, layers, rows, nx),) * 4, snap)
            for which in (1, 2, 3):
                payload, new = lax.optimization_barrier((strip_parts[which], new))
                under_way.append((which, lax.ppermute(payload, "gz", [(i, i ^ which) for i in range(count)])))
            snap = None
        slots = max(1, steps - 2 - step)
        far = [item for item in waiting if not item[0]]
        near = [item for item in waiting if item[0]]
        chosen = far[: -(-len(far) // slots)] + (near[: -(-len(near) // slots)] if step > SNAP_EVERY or not far else [])
        waiting = [item for item in waiting if item not in chosen]
        for _, which_part, pairs in chosen:
            payload = sent[which_part]
            payload, new = lax.optimization_barrier((payload, new))
            under_way.append((which_part, lax.ppermute(payload, "gz", pairs)))
        prev, cur = cur, new

    (first,) = merge(
        collect_kernel, (f32(count, layers, rows, nx),), own_strips, *[array for _, array in sorted(arrived + under_way, key=lambda item: item[0])]
    )
    second = lax.all_to_all(send, "gz", split_axis=0, concat_axis=0, tiled=True)
    back_a = lax.ppermute(out_a, "gz", first_pairs)
    back_b = lax.ppermute(out_b, "gz", back_pairs)
    source_final, receiver_final = choose(back_a, back_b, back=True)
    image_out = images(shifts, (first, second), lag_offsets.shape[0])
    return (image_out, source_final, receiver_final)


def solution(mesh):
    return jax.shard_map(
        local,
        mesh=mesh,
        in_specs=(
            P(("shot", "gz"), None, None),
            P(("shot", "gz"), None, None),
            P(("shot", "gz"), None, None),
            P(("shot", "gz"), None, None),
            P("gz", None, None),
            P("shot", None, "gz", None),
            P(),
            P("shot", None, None),
            P(),
            P(),
        ),
        out_specs=(
            P("shot", None, "gz", None),
            P(("shot", "gz"), None, None),
            P(("shot", "gz"), None, None),
        ),
        check_vma=False,
    )
```

```python
import functools

import jax
import jax.numpy as jnp
import numpy as np
from jax import lax
from jax.experimental import pallas as pl
from jax.experimental.pallas import tpu as pltpu
from jax.sharding import PartitionSpec as P


SNAP_EVERY = 6
REACH = 4
EARLY = 4
PACKED = 2

SCALE = 5040.0
NEAR = (8064.0, -1008.0, 128.0, -9.0)
CENTRE = -43050.0
damping = 0.25
smoothing = 16.0

VMEM = pl.BlockSpec(memory_space=pltpu.VMEM)
SMEM = pl.BlockSpec(memory_space=pltpu.SMEM)
ANY = pl.BlockSpec(memory_space=pl.ANY)
HBM = pl.BlockSpec(memory_space=pltpu.HBM)
PARAMS = pltpu.CompilerParams(vmem_limit_bytes=24 * 1024 * 1024)


def f32(*shape):
    return jax.ShapeDtypeStruct(shape, jnp.float32)


def held(*shape):
    return pltpu.VMEM(shape, jnp.float32)


def cost(flops, bytes_accessed):
    return pl.CostEstimate(flops=int(flops), bytes_accessed=int(bytes_accessed), transcendentals=0)


def banded(size):
    apart = np.abs(np.arange(size)[:, None] - np.arange(size)[None, :])
    table = np.zeros((size, size), np.float32)
    for k, weight in enumerate(NEAR):
        table[apart == k + 1] = weight
    return table


def pairs_to_fields(count):
    first, second = [], []
    for base in range(0, count, 4):
        first += [(base, base), (base + 1, base + 2), (base + 2, base + 1), (base + 3, base + 3)]
        second += [(base, base + 2), (base + 1, base), (base + 2, base + 3), (base + 3, base + 1)]
    return first, second


def pairs_of_halos(count):
    within = [(i, i ^ 1) for i in range(count)]
    between = [(0, 2), (2, 0), (count - 3, count - 1), (count - 1, count - 3)]
    for group in range(count // 4 - 1):
        for field in range(2):
            low, high = 4 * group + 2 * field + 1, 4 * group + 4 + 2 * field
            between += [(low, high), (high, low)]
    return between, within


def my_field():
    return lax.rem(lax.axis_index("gz") // 2, 2)


def my_half():
    return lax.rem(lax.axis_index("gz"), 2)


def place_of(local, layers):
    return jnp.where(my_half() == 0, local, layers - 1 - local)


def in_order(run, here, there):
    pl.when(my_half() == 0)(lambda: run(here, there))
    pl.when(my_half() != 0)(lambda: run(there, here))


def copy_both(pairs, sem):
    copies = [pltpu.make_async_copy(a, b, sem.at[i]) for i, (a, b) in enumerate(pairs)]
    for copy in copies:
        copy.start()
    for copy in copies:
        copy.wait()


def choose_kernel(here, there, first, second, sem):
    in_order(lambda a, b: copy_both(((a, first), (b, second)), sem), here, there)


def choose_back_kernel(here, there, first, second, one, two, sem):
    in_order(lambda a, b: copy_both(((a, one), (b, two)), sem), here, there)
    copy_both(((one, first), (two, second)), sem)


def choose(here, there, back=False):
    like = jax.ShapeDtypeStruct(here.shape, here.dtype)
    staged = [pltpu.VMEM(here.shape, here.dtype)] * 2 if back else []
    return pl.pallas_call(
        choose_back_kernel if back else choose_kernel,
        out_shape=(like, like),
        in_specs=[ANY if back else HBM] * 2,
        out_specs=(ANY if back else VMEM,) * 2,
        scratch_shapes=[*staged, pltpu.SemaphoreType.DMA((2,))],
        compiler_params=PARAMS,
        name="choose",
    )(here, there)


def prepare_kernel(layers, face_steps, lags, faces, late, early, shifts, gathered):
    steps = face_steps.shape[0]
    nx = shifts.shape[1] // 2
    gathered[...] = jnp.zeros_like(gathered)

    def gather(step, layer, row):
        base = face_steps[step] * (8 * layers) + layer
        gathered[row : row + 4] = faces[pl.ds(base + 4 * layers, 4, stride=layers), :]
        gathered[row + 4 : row + 8] = faces[pl.ds(base, 4, stride=layers), :]

    for plane in range(steps // PACKED):
        for layer in range(layers):
            for step in range(PACKED):
                gather(PACKED * plane + step, layer, 8 * (PACKED * layer + step))
        if plane < EARLY // PACKED:
            early[plane] = gathered[...].T
        else:
            late[plane - EARLY // PACKED] = gathered[...].T

    apart = lax.broadcasted_iota(jnp.int32, (nx, nx), 1) - lax.broadcasted_iota(jnp.int32, (nx, nx), 0)
    for index in range(lags.shape[0]):
        columns = slice(index * nx, (index + 1) * nx)
        for which, lag in ((0, lags[index]), (1, -lags[index])):
            moved = jnp.where(apart == lag, 1.0, 0.0).astype(jnp.bfloat16)
            shifts[which, :nx, columns] = moved
            shifts[which, nx:, columns] = moved


def prepare(saved_faces, face_steps, lag_offsets, nx):
    slots, eight, layers, ny = saved_faces.shape
    planes = face_steps.shape[0] // PACKED
    return pl.pallas_call(
        functools.partial(prepare_kernel, layers),
        out_shape=(
            f32(planes - EARLY // PACKED, ny, 128),
            f32(EARLY // PACKED, ny, 128),
            jax.ShapeDtypeStruct((2, 2 * nx, lag_offsets.shape[0] * nx), jnp.bfloat16),
        ),
        in_specs=[SMEM, SMEM, VMEM],
        out_specs=(VMEM,) * 3,
        scratch_shapes=[pltpu.VMEM((128, ny), jnp.float32)],
        compiler_params=PARAMS,
        name="prepare",
    )(face_steps, lag_offsets, saved_faces.reshape(slots * eight * layers, ny))


def for_each_part(layers, run):
    def one_layer(j, carry):
        place = place_of(j, layers)
        part = (place >= layers // 2).astype(jnp.int32)
        q = place - part * (layers // 2)
        pl.when(part == my_field())(lambda: run(j, q, 0))
        pl.when(part != my_field())(lambda: run(j, q, 1))
        return carry

    lax.fori_loop(0, layers, one_layer, 0, unroll=2)


def merge_now_kernel(now_a, now_b, cur, low, high):
    layers = 2 * now_a.shape[0]

    def run(j, q, which):
        cur[REACH + j] = (now_a, now_b)[which][q]

    for_each_part(layers, run)
    low[...] = cur[REACH : 2 * REACH]
    high[...] = cur[layers : layers + REACH]


def merge_rest_kernel(shared, before_a, before_b, speed_a, speed_b, prev, speed):
    flipped = (lax.rem(lax.axis_index("shot"), 2) == 1) & shared

    def run(j, q, which):
        prev[REACH + j] = (before_a, before_b)[which][q]
        ahead, other = (speed_a, speed_b) if which == 0 else (speed_b, speed_a)
        speed[j] = jnp.where(flipped, other[q], ahead[q]) * (1.0 / SCALE)

    for_each_part(2 * before_a.shape[0], run)


def merge(kernel, shapes, *parts):
    return pl.pallas_call(
        kernel, out_shape=shapes, in_specs=[VMEM] * len(parts), out_specs=(VMEM,) * len(shapes), compiler_params=PARAMS
    )(*parts)


def split(u):
    high = u.astype(jnp.bfloat16)
    return high, (u - high.astype(jnp.float32)).astype(jnp.bfloat16)


def advance(step, across, along, cur, prev, speed, faces, new, local):
    layers, ny, nx = speed.shape
    column = lax.broadcasted_iota(jnp.int32, (ny, nx), 1)
    edge = ((column < REACH) | (column >= nx - REACH)) & (my_field() == 0)

    def placed(layer):
        place = place_of(layer, layers)
        part = (place >= layers // 2).astype(jnp.int32)
        plane, inside = (step if step < EARLY else step - EARLY) // PACKED, step % PACKED
        lane = 8 * (PACKED * (place - part * (layers // 2)) + inside) + REACH
        held = jnp.where(part == 0, faces[0][plane], faces[1][plane])
        return pltpu.roll(held, lax.rem(128 - lane, 128), axis=1)

    for first in range(0, len(local), 2):
        pair = local[first : first + 2]
        inputs = [cur[REACH + layer] for layer in pair]
        halves = [split(u) for u in inputs]
        along_sum = jnp.dot(
            along[...],
            jnp.concatenate([jnp.concatenate(half, axis=0) for half in halves], axis=1),
            preferred_element_type=jnp.float32,
        )
        across_sum = jnp.dot(
            jnp.concatenate([jnp.concatenate(half, axis=1) for half in halves], axis=0),
            across[...],
            preferred_element_type=jnp.float32,
        )
        for i, layer in enumerate(pair):
            e, u = REACH + layer, inputs[i]
            total = across_sum[i * ny : (i + 1) * ny] + along_sum[:, i * nx : (i + 1) * nx]
            for k in range(REACH):
                total = total + NEAR[k] * (cur[e + (k + 1)] + cur[e - (k + 1)])
            total = total + CENTRE * u
            updated = 2.0 * u - prev[e] + speed[layer] * total
            new[e] = jnp.where(edge, placed(layer), updated)


def fill_low(low, cur):
    index = lax.axis_index("gz")
    place = 2 * (index // 4) + my_half()
    inside = (place > 0) & (place < lax.axis_size("gz") // 2 - 1)
    for d in range(REACH):
        cur[REACH - 1 - d] = jnp.where(inside, low[d], 0.0)


def fill_high(high, cur):
    layers = cur.shape[0] - 2 * REACH
    for d in range(REACH):
        cur[REACH + layers + d] = high[REACH - 1 - d]


def add_trace(step, traces, new):
    @pl.when(lax.axis_index("gz") == 2)
    def _():
        new[REACH] = new[REACH] + traces[step].astype(jnp.float32)


def keep_snapshot(step, phase, new, snap):
    count, layers, rows, _ = snap.shape
    window = step // SNAP_EVERY

    @pl.when(phase[window] == step - window * SNAP_EVERY)
    def _():
        def one_layer(j, carry):
            place = place_of(j, layers)
            for strip in range(count):
                snap[strip, place] = new[REACH + j, strip * rows : (strip + 1) * rows, :]
            return carry

        lax.fori_loop(0, layers, one_layer, 0)


def lower_kernel(step, across, along, low, speed, face_a, face_b, traces, cur_in, prev, cur, new, low_out):
    fill_low(low, cur)
    advance(step, across, along, cur, prev, speed, (face_a, face_b), new, list(range(REACH)))
    add_trace(step, traces, new)
    low_out[...] = new[REACH : 2 * REACH]


def upper_kernel(step, across, along, high, speed, face_a, face_b, cur_in, prev, cur, new, high_out):
    layers = speed.shape[0]
    fill_high(high, cur)
    advance(step, across, along, cur, prev, speed, (face_a, face_b), new, list(range(layers - REACH, layers)))
    high_out[...] = new[layers : layers + REACH]


def inner_kernel(step, faces, keep, phase, across, along, speed, *rest):
    face, rest = rest[:faces], rest[faces:]
    cur, prev, new = rest[0], rest[1], rest[-2] if keep else rest[-1]
    layers = speed.shape[0]
    advance(step, across, along, cur, prev, speed, face, new, list(range(REACH, layers - REACH)))
    if keep:
        keep_snapshot(step, phase, new, rest[-1])


def last_kernel(
    step, phase, across, along, low, high, traces, speed, face_a, face_b, cur_in, prev, snap_in, cur, new, snap, out_a, out_b, send
):
    layers = speed.shape[0]
    fill_low(low, cur)
    fill_high(high, cur)
    outer = [*range(REACH), *range(layers - REACH, layers)]
    advance(step, across, along, cur, prev, speed, (face_a, face_b), new, outer)
    add_trace(step, traces, new)
    keep_snapshot(step, phase, new, snap)

    def run(j, q, which):
        (out_a, out_b)[which][q] = new[REACH + j]

    for_each_part(layers, run)

    def one_strip(strip, carry):
        send[strip] = snap[strip]
        return carry

    lax.fori_loop(0, snap.shape[0], one_strip, 0)


def spread_kernel(snap, *outs):
    mine = lax.rem(lax.axis_index("gz"), 4)
    for which, out in enumerate(outs):

        def one(group, carry):
            out[group] = snap[4 * group + jnp.bitwise_xor(mine, which)]
            return carry

        lax.fori_loop(0, out.shape[0], one, 0)


def regather_kernel(*refs):
    held_by, (own, *parts) = refs[:4], refs[4:]
    groups = held_by[0].shape[0]
    pieces = len(parts) // (groups - 1)
    size = 4 // pieces
    group = lax.axis_index("gz") // 4
    mine = lax.rem(lax.axis_index("gz"), 4)
    for which, strips in enumerate(held_by):
        source = jnp.bitwise_xor(mine, which)
        own[source] = strips[group]
        for i, part in enumerate(parts):
            first = (i % pieces) * size

            @pl.when((source >= first) & (source < first + size))
            def _(i=i, part=part, first=first, source=source, strips=strips):
                part[source - first] = strips[jnp.bitwise_xor(group, i // pieces + 1)]


def collect_kernel(own, *refs):
    parts, out = refs[:-1], refs[-1]
    pieces = len(parts) // (out.shape[0] // 4 - 1)
    size = 4 // pieces
    group = lax.axis_index("gz") // 4
    for i in range(4):
        out[4 * group + i] = own[i]
    for i, part in enumerate(parts):
        first = 4 * jnp.bitwise_xor(group, i // pieces + 1) + (i % pieces) * size
        for j in range(size):
            out[first + j] = part[j]


def image_kernel(shifts, *refs):
    windows, (out, light, stage, sem) = refs[:-4], refs[-4:]
    _, layers, rows, nx = windows[0].shape
    lags, depth = out.shape[:2]
    size = layers * rows
    blocks = depth // layers
    table = sweep_table(depth)

    carried = jnp.zeros((rows, nx), jnp.float32)
    for d in range(depth):
        block, layer = d // layers, d % layers
        device = (block // 2) * 4 + block % 2
        squares = sum(window[device, layer] * window[device, layer] for window in windows)
        carried = squares * table[d] + carried * (smoothing * table[d])
        light[d] = carried
    carried = jnp.zeros((rows, nx), jnp.float32)
    for d in reversed(range(depth)):
        carried = light[d] + carried * (smoothing * table[d])
        light[d] = 1.0 / (carried + damping)

    def put(block, slot):
        return pltpu.make_async_copy(
            stage.at[slot], out.at[:, pl.ds(block * layers, layers)], sem.at[slot]
        )

    def one_block(block, carry):
        slot = lax.rem(block, 2)
        device = (block // 2) * 4 + lax.rem(block, 2)
        pl.when(block >= 2)(lambda: put(block - 2, slot).wait())

        def both(device, window):
            return jnp.concatenate(split(window[device].reshape(size, nx)), axis=1)

        sources = [both(device, window) for window in windows]
        receivers = [both(device + 2, window) for window in windows]
        inverse = light[pl.ds(block * layers, layers)].reshape(size, nx)
        for lag in range(0, lags, 2):
            columns = slice(lag * nx, (lag + 2) * nx)
            raw = 0.0
            for window in range(len(windows)):
                raw = raw + jnp.dot(
                    sources[window], shifts[0, :, columns], preferred_element_type=jnp.float32
                ) * jnp.dot(receivers[window], shifts[1, :, columns], preferred_element_type=jnp.float32)
            for i in range(2):
                value = (raw[:, i * nx : (i + 1) * nx] * inverse).astype(stage.dtype)
                stage[slot, lag + i] = value.reshape(layers, rows, nx)
        put(block, slot).start()
        return carry

    lax.fori_loop(0, blocks, one_block, 0)
    for block in (blocks - 2, blocks - 1):
        put(block, block % 2).wait()


def sweep_table(depth):
    table, before = [], 0.0
    for _ in range(depth):
        before = 1.0 / (1.0 + 2.0 * smoothing - smoothing * smoothing * before)
        table.append(before)
    return table


def images(shifts, windows, lags):
    count, layers, rows, nx = windows[0].shape
    depth = count // 2 * layers
    return pl.pallas_call(
        image_kernel,
        out_shape=jax.ShapeDtypeStruct((lags, depth, rows, nx), jnp.bfloat16),
        in_specs=[VMEM] * (1 + len(windows)),
        out_specs=ANY,
        scratch_shapes=[
            pltpu.VMEM((depth, rows, nx), jnp.float32),
            pltpu.VMEM((2, lags, layers, rows, nx), jnp.bfloat16),
            pltpu.SemaphoreType.DMA((2,)),
        ],
        compiler_params=PARAMS,
        name="images",
    )(shifts, *windows)


def local(
    source_now,
    source_before,
    receiver_now,
    receiver_before,
    speed_term,
    saved_faces,
    face_steps,
    traces,
    lag_offsets,
    snap_phase,
):
    count = lax.axis_size("gz")
    own, ny, nx = source_now.shape
    layers = 2 * own
    rows = ny // count
    steps = face_steps.shape[0]
    first_pairs, second_pairs = pairs_to_fields(count)
    back_pairs = [(b, a) for a, b in second_pairs]
    between, within = pairs_of_halos(count)
    band_x, band_y = banded(nx), banded(ny)
    across = jnp.asarray(np.concatenate([band_x, band_x], axis=0), jnp.bfloat16)
    along = jnp.asarray(np.concatenate([band_y, band_y], axis=1), jnp.bfloat16)

    def regroup(a, b):
        return lax.ppermute(a, "gz", first_pairs), lax.ppermute(b, "gz", second_pairs)

    tall = held(layers + 2 * REACH, ny, nx)
    whole = f32(layers, ny, nx)
    slab = f32(REACH, ny, nx)
    half = f32(own, ny, nx)
    strips = held(count, layers, rows, nx)
    plane = ny * nx

    shots = lax.axis_size("shot")
    shared = shots % 2 == 0
    if shared:
        both = [
            (shot * count + a, shot * count + b)
            for shot in range(shots)
            for a, b in (first_pairs, second_pairs)[shot % 2]
        ]
        one = lax.ppermute(speed_term, ("shot", "gz"), both)
        speed_parts = one, lax.ppermute(one, "shot", [(shot, shot ^ 1) for shot in range(shots)])
    else:
        speed_parts = regroup(speed_term, speed_term)
    now = regroup(*choose(source_now, receiver_now))
    before = regroup(*choose(source_before, receiver_before))
    late, early, shifts = prepare(saved_faces, face_steps, lag_offsets, nx)
    early = regroup(early, early)
    cur, low, high = merge(merge_now_kernel, (tall, slab, slab), *now)
    low = lax.ppermute(low, "gz", between)
    high = lax.ppermute(high, "gz", within)
    prev, speed = merge(functools.partial(merge_rest_kernel, shared), (tall, whole), *before, *speed_parts)

    groups = count // 4
    pieces = max(1, 8 // groups)
    waiting, under_way, arrived = [], [], []

    snap = None
    for step in range(steps):
        faces = late if step >= EARLY else early
        wide = len(faces)
        if step < steps - 1:
            lower = pl.pallas_call(
                functools.partial(lower_kernel, step),
                out_shape=(tall, tall, slab),
                in_specs=[VMEM] * 9,
                out_specs=(VMEM,) * 3,
                input_output_aliases={7: 0, 8: 1},
                compiler_params=PARAMS,
                cost_estimate=cost(60 * 4 * plane, 4 * 20 * plane),
                name="lower",
            )
            upper = pl.pallas_call(
                functools.partial(upper_kernel, step),
                out_shape=(tall, tall, slab),
                in_specs=[VMEM] * 8,
                out_specs=(VMEM,) * 3,
                input_output_aliases={6: 0, 7: 1},
                compiler_params=PARAMS,
                cost_estimate=cost(60 * 4 * plane, 4 * 20 * plane),
                name="upper",
            )
            cur, new, low = lower(across, along, low, speed, *faces, traces, cur, prev)
            low = lax.ppermute(low, "gz", between)
            cur, new, high = upper(across, along, high, speed, *faces, cur, new)
            high = lax.ppermute(high, "gz", within)
            landed = []
            if step != SNAP_EVERY:
                low, *landed = lax.optimization_barrier((low, *[array for _, array in under_way]))
            if step == SNAP_EVERY + 1:
                own_strips, *sent = merge(
                    regather_kernel,
                    (f32(4, layers, rows, nx), *[f32(4 // pieces, layers, rows, nx)] * (pieces * (groups - 1))),
                    strip_parts[0],
                    *[array for _, array in under_way],
                )
                waiting = [
                    (j < pieces, j, [(i, 4 * ((i // 4) ^ (j // pieces + 1)) + i % 4) for i in range(count)])
                    for j in range(len(sent))
                ]
            elif step != SNAP_EVERY:
                arrived += [(part, array) for (part, _), array in zip(under_way, landed)]
            if step != SNAP_EVERY:
                under_way = []
        else:
            new = prev
        operands = (snap_phase, across, along, speed, *faces, cur, new)
        inner = functools.partial(
            pl.pallas_call,
            compiler_params=PARAMS,
            cost_estimate=cost(60 * (layers - 8) * plane, 4 * 40 * plane),
            name="inner",
        )
        if step < steps - 1:
            alias = {5 + wide: 0}
            if snap is not None:
                operands, alias = (*operands, snap), {5 + wide: 0, 6 + wide: 1}
            new, snap = inner(
                functools.partial(inner_kernel, step, wide, True),
                out_shape=(tall, strips),
                in_specs=[SMEM] + [VMEM] * (len(operands) - 1),
                out_specs=(VMEM,) * 2,
                input_output_aliases=alias,
            )(*operands)
        else:
            (new,) = inner(
                functools.partial(inner_kernel, step, wide, False, None),
                out_shape=(tall,),
                in_specs=[VMEM] * (len(operands) - 1),
                out_specs=(VMEM,),
                input_output_aliases={4 + wide: 0},
            )(*operands[1:])
            last = pl.pallas_call(
                functools.partial(last_kernel, step),
                out_shape=(tall, tall, strips, half, half, f32(*strips.shape)),
                in_specs=[SMEM] + [VMEM] * 11,
                out_specs=(VMEM,) * 6,
                input_output_aliases={9: 0, 10: 1, 11: 2},
                compiler_params=PARAMS,
                name="last",
            )
            _, _, _, out_a, out_b, send = last(snap_phase, across, along, low, high, traces, speed, *faces, cur, new, snap)
        if step == 0:
            late, new = lax.optimization_barrier((late, new))
            late = regroup(late, late)
        if step == SNAP_EVERY - 1:
            strip_parts = merge(spread_kernel, (f32(groups, layers, rows, nx),) * 4, snap)
            for which in (1, 2, 3):
                payload, new = lax.optimization_barrier((strip_parts[which], new))
                under_way.append((which, lax.ppermute(payload, "gz", [(i, i ^ which) for i in range(count)])))
            snap = None
        slots = max(1, steps - 1 - step)
        far = [item for item in waiting if not item[0]]
        near = [item for item in waiting if item[0]]
        chosen = far[: -(-len(far) // slots)] + (near[: -(-len(near) // slots)] if step > SNAP_EVERY + 1 or not far else [])
        waiting = [item for item in waiting if item not in chosen]
        for _, which_part, pairs in chosen:
            payload = sent[which_part]
            payload, new = lax.optimization_barrier((payload, new))
            under_way.append((which_part, lax.ppermute(payload, "gz", pairs)))
        prev, cur = cur, new

    (first,) = merge(
        collect_kernel, (f32(count, layers, rows, nx),), own_strips, *[array for _, array in sorted(arrived + under_way, key=lambda item: item[0])]
    )
    second = lax.all_to_all(send, "gz", split_axis=0, concat_axis=0, tiled=True)
    back_a = lax.ppermute(out_a, "gz", first_pairs)
    back_b = lax.ppermute(out_b, "gz", back_pairs)
    source_final, receiver_final = choose(back_a, back_b, back=True)
    image_out = images(shifts, (first, second), lag_offsets.shape[0])
    return (image_out, source_final, receiver_final)


def solution(mesh):
    return jax.shard_map(
        local,
        mesh=mesh,
        in_specs=(
            P(("shot", "gz"), None, None),
            P(("shot", "gz"), None, None),
            P(("shot", "gz"), None, None),
            P(("shot", "gz"), None, None),
            P("gz", None, None),
            P("shot", None, "gz", None),
            P(),
            P("shot", None, None),
            P(),
            P(),
        ),
        out_specs=(
            P("shot", None, "gz", None),
            P(("shot", "gz"), None, None),
            P(("shot", "gz"), None, None),
        ),
        check_vma=False,
    )
```

```python
import functools

import jax
import jax.numpy as jnp
import numpy as np
from jax import lax
from jax.experimental import pallas as pl
from jax.experimental.pallas import tpu as pltpu
from jax.sharding import PartitionSpec as P


SNAP_EVERY = 6
REACH = 4
EARLY = 4
PACKED = 2

SCALE = 5040.0
NEAR = (8064.0, -1008.0, 128.0, -9.0)
CENTRE = -43050.0
damping = 0.25
smoothing = 16.0

VMEM = pl.BlockSpec(memory_space=pltpu.VMEM)
SMEM = pl.BlockSpec(memory_space=pltpu.SMEM)
ANY = pl.BlockSpec(memory_space=pl.ANY)
HBM = pl.BlockSpec(memory_space=pltpu.HBM)
PARAMS = pltpu.CompilerParams(vmem_limit_bytes=24 * 1024 * 1024)


def f32(*shape):
    return jax.ShapeDtypeStruct(shape, jnp.float32)


def held(*shape):
    return pltpu.VMEM(shape, jnp.float32)


def cost(flops, bytes_accessed):
    return pl.CostEstimate(flops=int(flops), bytes_accessed=int(bytes_accessed), transcendentals=0)


def banded(size):
    apart = np.abs(np.arange(size)[:, None] - np.arange(size)[None, :])
    table = np.zeros((size, size), np.float32)
    for k, weight in enumerate(NEAR):
        table[apart == k + 1] = weight
    return table


def pairs_to_fields(count):
    first, second = [], []
    for base in range(0, count, 4):
        first += [(base, base), (base + 1, base + 2), (base + 2, base + 1), (base + 3, base + 3)]
        second += [(base, base + 2), (base + 1, base), (base + 2, base + 3), (base + 3, base + 1)]
    return first, second


def pairs_of_halos(count, shots):
    between = []
    for shot in range(shots):
        base = shot * count
        for group in range(count // 4 - 1):
            for field in range(2):
                low, high = base + 4 * group + 2 * field + 1, base + 4 * group + 4 + 2 * field
                between += [(low, high), (high, low)]
        for end in (0, 2, count - 3, count - 1):
            between.append((base + end, (shot ^ 1) * count + end if shots % 2 == 0 else base + (end ^ 2)))
    return between, [(i, i ^ 1) for i in range(count)]


def my_field():
    return lax.rem(lax.axis_index("gz") // 2, 2)


def my_half():
    return lax.rem(lax.axis_index("gz"), 2)


def place_of(local, layers):
    return jnp.where(my_half() == 0, local, layers - 1 - local)


def in_order(run, here, there):
    pl.when(my_half() == 0)(lambda: run(here, there))
    pl.when(my_half() != 0)(lambda: run(there, here))


def copy_both(pairs, sem):
    copies = [pltpu.make_async_copy(a, b, sem.at[i]) for i, (a, b) in enumerate(pairs)]
    for copy in copies:
        copy.start()
    for copy in copies:
        copy.wait()


def choose_kernel(here, there, first, second, sem):
    in_order(lambda a, b: copy_both(((a, first), (b, second)), sem), here, there)


def choose_back_kernel(here, there, first, second, one, two, sem):
    in_order(lambda a, b: copy_both(((a, one), (b, two)), sem), here, there)
    copy_both(((one, first), (two, second)), sem)


def choose(here, there, back=False):
    like = jax.ShapeDtypeStruct(here.shape, here.dtype)
    staged = [pltpu.VMEM(here.shape, here.dtype)] * 2 if back else []
    return pl.pallas_call(
        choose_back_kernel if back else choose_kernel,
        out_shape=(like, like),
        in_specs=[ANY if back else HBM] * 2,
        out_specs=(ANY if back else VMEM,) * 2,
        scratch_shapes=[*staged, pltpu.SemaphoreType.DMA((2,))],
        compiler_params=PARAMS,
        name="choose",
    )(here, there)


def prepare_kernel(layers, face_steps, lags, faces, late, early, shifts, gathered):
    steps = face_steps.shape[0]
    nx = shifts.shape[1] // 2
    gathered[...] = jnp.zeros_like(gathered)

    def gather(step, layer, row):
        base = face_steps[step] * (8 * layers) + layer
        gathered[row : row + 4] = faces[pl.ds(base + 4 * layers, 4, stride=layers), :]
        gathered[row + 4 : row + 8] = faces[pl.ds(base, 4, stride=layers), :]

    for plane in range(steps // PACKED):
        for layer in range(layers):
            for step in range(PACKED):
                gather(PACKED * plane + step, layer, 8 * (PACKED * layer + step))
        if plane < EARLY // PACKED:
            early[plane] = gathered[...].T
        else:
            late[plane - EARLY // PACKED] = gathered[...].T

    apart = lax.broadcasted_iota(jnp.int32, (nx, nx), 1) - lax.broadcasted_iota(jnp.int32, (nx, nx), 0)
    for index in range(lags.shape[0]):
        columns = slice(index * nx, (index + 1) * nx)
        for which, lag in ((0, lags[index]), (1, -lags[index])):
            moved = jnp.where(apart == lag, 1.0, 0.0).astype(jnp.bfloat16)
            shifts[which, :nx, columns] = moved
            shifts[which, nx:, columns] = moved


def prepare(saved_faces, face_steps, lag_offsets, nx):
    slots, eight, layers, ny = saved_faces.shape
    planes = face_steps.shape[0] // PACKED
    return pl.pallas_call(
        functools.partial(prepare_kernel, layers),
        out_shape=(
            f32(planes - EARLY // PACKED, ny, 128),
            f32(EARLY // PACKED, ny, 128),
            jax.ShapeDtypeStruct((2, 2 * nx, lag_offsets.shape[0] * nx), jnp.bfloat16),
        ),
        in_specs=[SMEM, SMEM, VMEM],
        out_specs=(VMEM,) * 3,
        scratch_shapes=[pltpu.VMEM((128, ny), jnp.float32)],
        compiler_params=PARAMS,
        name="prepare",
    )(face_steps, lag_offsets, saved_faces.reshape(slots * eight * layers, ny))


def for_each_part(layers, run):
    def one_layer(j, carry):
        place = place_of(j, layers)
        part = (place >= layers // 2).astype(jnp.int32)
        q = place - part * (layers // 2)
        pl.when(part == my_field())(lambda: run(j, q, 0))
        pl.when(part != my_field())(lambda: run(j, q, 1))
        return carry

    lax.fori_loop(0, layers, one_layer, 0, unroll=2)


def merge_now_kernel(now_a, now_b, cur, low, high):
    layers = 2 * now_a.shape[0]

    def run(j, q, which):
        cur[REACH + j] = (now_a, now_b)[which][q]

    for_each_part(layers, run)
    low[...] = cur[REACH : 2 * REACH]
    high[...] = cur[layers : layers + REACH]


def merge_rest_kernel(shared, before_a, before_b, speed_a, speed_b, prev, speed):
    flipped = (lax.rem(lax.axis_index("shot"), 2) == 1) & shared

    def run(j, q, which):
        prev[REACH + j] = (before_a, before_b)[which][q]
        ahead, other = (speed_a, speed_b) if which == 0 else (speed_b, speed_a)
        speed[j] = jnp.where(flipped, other[q], ahead[q]) * (1.0 / SCALE)

    for_each_part(2 * before_a.shape[0], run)


def merge(kernel, shapes, *parts):
    return pl.pallas_call(
        kernel, out_shape=shapes, in_specs=[VMEM] * len(parts), out_specs=(VMEM,) * len(shapes), compiler_params=PARAMS
    )(*parts)


def split(u):
    high = u.astype(jnp.bfloat16)
    return high, (u - high.astype(jnp.float32)).astype(jnp.bfloat16)


def advance(step, across, along, cur, prev, speed, faces, new, local):
    layers, ny, nx = speed.shape
    column = lax.broadcasted_iota(jnp.int32, (ny, nx), 1)
    edge = ((column < REACH) | (column >= nx - REACH)) & (my_field() == 0)

    def placed(layer):
        place = place_of(layer, layers)
        part = (place >= layers // 2).astype(jnp.int32)
        plane, inside = (step if step < EARLY else step - EARLY) // PACKED, step % PACKED
        lane = 8 * (PACKED * (place - part * (layers // 2)) + inside) + REACH
        held = jnp.where(part == 0, faces[0][plane], faces[1][plane])
        return pltpu.roll(held, lax.rem(128 - lane, 128), axis=1)

    for first in range(0, len(local), 2):
        pair = local[first : first + 2]
        inputs = [cur[REACH + layer] for layer in pair]
        halves = [split(u) for u in inputs]
        along_sum = jnp.dot(
            along[...],
            jnp.concatenate([jnp.concatenate(half, axis=0) for half in halves], axis=1),
            preferred_element_type=jnp.float32,
        )
        across_sum = jnp.dot(
            jnp.concatenate([jnp.concatenate(half, axis=1) for half in halves], axis=0),
            across[...],
            preferred_element_type=jnp.float32,
        )
        for i, layer in enumerate(pair):
            e, u = REACH + layer, inputs[i]
            total = across_sum[i * ny : (i + 1) * ny] + along_sum[:, i * nx : (i + 1) * nx]
            for k in range(REACH):
                total = total + NEAR[k] * (cur[e + (k + 1)] + cur[e - (k + 1)])
            total = total + CENTRE * u
            updated = 2.0 * u - prev[e] + speed[layer] * total
            new[e] = jnp.where(edge, placed(layer), updated)


def fill_low(low, cur):
    index = lax.axis_index("gz")
    place = 2 * (index // 4) + my_half()
    inside = (place > 0) & (place < lax.axis_size("gz") // 2 - 1)
    for d in range(REACH):
        cur[REACH - 1 - d] = jnp.where(inside, low[d], 0.0)


def fill_high(high, cur):
    layers = cur.shape[0] - 2 * REACH
    for d in range(REACH):
        cur[REACH + layers + d] = high[REACH - 1 - d]


def add_trace(step, traces, new):
    @pl.when(lax.axis_index("gz") == 2)
    def _():
        new[REACH] = new[REACH] + traces[step].astype(jnp.float32)


def keep_snapshot(step, phase, new, snap):
    count, layers, rows, _ = snap.shape
    window = step // SNAP_EVERY

    @pl.when(phase[window] == step - window * SNAP_EVERY)
    def _():
        def one_layer(j, carry):
            place = place_of(j, layers)
            for strip in range(count):
                snap[strip, place] = new[REACH + j, strip * rows : (strip + 1) * rows, :]
            return carry

        lax.fori_loop(0, layers, one_layer, 0)


def lower_kernel(step, across, along, low, speed, face_a, face_b, traces, cur_in, prev, cur, new, low_out):
    fill_low(low, cur)
    advance(step, across, along, cur, prev, speed, (face_a, face_b), new, list(range(REACH)))
    add_trace(step, traces, new)
    low_out[...] = new[REACH : 2 * REACH]


def upper_kernel(step, across, along, high, speed, face_a, face_b, cur_in, prev, cur, new, high_out):
    layers = speed.shape[0]
    fill_high(high, cur)
    advance(step, across, along, cur, prev, speed, (face_a, face_b), new, list(range(layers - REACH, layers)))
    high_out[...] = new[layers : layers + REACH]


def inner_kernel(step, faces, keep, phase, across, along, speed, *rest):
    face, rest = rest[:faces], rest[faces:]
    cur, prev, new = rest[0], rest[1], rest[-2] if keep else rest[-1]
    layers = speed.shape[0]
    advance(step, across, along, cur, prev, speed, face, new, list(range(REACH, layers - REACH)))
    if keep:
        keep_snapshot(step, phase, new, rest[-1])


def last_kernel(
    step, phase, across, along, low, high, traces, speed, face_a, face_b, cur_in, prev, snap_in, cur, new, snap, out_a, out_b, send
):
    layers = speed.shape[0]
    fill_low(low, cur)
    fill_high(high, cur)
    outer = [*range(REACH), *range(layers - REACH, layers)]
    advance(step, across, along, cur, prev, speed, (face_a, face_b), new, outer)
    add_trace(step, traces, new)
    keep_snapshot(step, phase, new, snap)

    def run(j, q, which):
        (out_a, out_b)[which][q] = new[REACH + j]

    for_each_part(layers, run)

    def one_strip(strip, carry):
        send[strip] = snap[strip]
        return carry

    lax.fori_loop(0, snap.shape[0], one_strip, 0)


def spread_kernel(snap, *outs):
    mine = lax.rem(lax.axis_index("gz"), 4)
    for which, out in enumerate(outs):

        def one(group, carry):
            out[group] = snap[4 * group + jnp.bitwise_xor(mine, which)]
            return carry

        lax.fori_loop(0, out.shape[0], one, 0)


def regather_kernel(*refs):
    held_by, (own, *parts) = refs[:4], refs[4:]
    groups = held_by[0].shape[0]
    pieces = len(parts) // (groups - 1)
    size = 4 // pieces
    group = lax.axis_index("gz") // 4
    mine = lax.rem(lax.axis_index("gz"), 4)
    for which, strips in enumerate(held_by):
        source = jnp.bitwise_xor(mine, which)
        own[source] = strips[group]
        for i, part in enumerate(parts):
            first = (i % pieces) * size

            @pl.when((source >= first) & (source < first + size))
            def _(i=i, part=part, first=first, source=source, strips=strips):
                part[source - first] = strips[jnp.bitwise_xor(group, i // pieces + 1)]


def collect_kernel(own, *refs):
    parts, out = refs[:-1], refs[-1]
    pieces = len(parts) // (out.shape[0] // 4 - 1)
    size = 4 // pieces
    group = lax.axis_index("gz") // 4
    for i in range(4):
        out[4 * group + i] = own[i]
    for i, part in enumerate(parts):
        first = 4 * jnp.bitwise_xor(group, i // pieces + 1) + (i % pieces) * size
        for j in range(size):
            out[first + j] = part[j]


def image_kernel(shifts, *refs):
    windows, (out, light, stage, sem) = refs[:-4], refs[-4:]
    _, layers, rows, nx = windows[0].shape
    lags, depth = out.shape[:2]
    size = layers * rows
    blocks = depth // layers
    table = sweep_table(depth)

    carried = jnp.zeros((rows, nx), jnp.float32)
    for d in range(depth):
        block, layer = d // layers, d % layers
        device = (block // 2) * 4 + block % 2
        squares = sum(window[device, layer] * window[device, layer] for window in windows)
        carried = squares * table[d] + carried * (smoothing * table[d])
        light[d] = carried
    carried = jnp.zeros((rows, nx), jnp.float32)
    for d in reversed(range(depth)):
        carried = light[d] + carried * (smoothing * table[d])
        light[d] = 1.0 / (carried + damping)

    def put(block, slot):
        return pltpu.make_async_copy(
            stage.at[slot], out.at[:, pl.ds(block * layers, layers)], sem.at[slot]
        )

    def one_block(block, carry):
        slot = lax.rem(block, 2)
        device = (block // 2) * 4 + lax.rem(block, 2)
        pl.when(block >= 2)(lambda: put(block - 2, slot).wait())

        def both(device, window):
            return jnp.concatenate(split(window[device].reshape(size, nx)), axis=1)

        sources = [both(device, window) for window in windows]
        receivers = [both(device + 2, window) for window in windows]
        inverse = light[pl.ds(block * layers, layers)].reshape(size, nx)
        for lag in range(0, lags, 2):
            columns = slice(lag * nx, (lag + 2) * nx)
            raw = 0.0
            for window in range(len(windows)):
                raw = raw + jnp.dot(
                    sources[window], shifts[0, :, columns], preferred_element_type=jnp.float32
                ) * jnp.dot(receivers[window], shifts[1, :, columns], preferred_element_type=jnp.float32)
            for i in range(2):
                value = (raw[:, i * nx : (i + 1) * nx] * inverse).astype(stage.dtype)
                stage[slot, lag + i] = value.reshape(layers, rows, nx)
        put(block, slot).start()
        return carry

    lax.fori_loop(0, blocks, one_block, 0)
    for block in (blocks - 2, blocks - 1):
        put(block, block % 2).wait()


def sweep_table(depth):
    table, before = [], 0.0
    for _ in range(depth):
        before = 1.0 / (1.0 + 2.0 * smoothing - smoothing * smoothing * before)
        table.append(before)
    return table


def images(shifts, windows, lags):
    count, layers, rows, nx = windows[0].shape
    depth = count // 2 * layers
    return pl.pallas_call(
        image_kernel,
        out_shape=jax.ShapeDtypeStruct((lags, depth, rows, nx), jnp.bfloat16),
        in_specs=[VMEM] * (1 + len(windows)),
        out_specs=ANY,
        scratch_shapes=[
            pltpu.VMEM((depth, rows, nx), jnp.float32),
            pltpu.VMEM((2, lags, layers, rows, nx), jnp.bfloat16),
            pltpu.SemaphoreType.DMA((2,)),
        ],
        compiler_params=PARAMS,
        name="images",
    )(shifts, *windows)


def local(
    source_now,
    source_before,
    receiver_now,
    receiver_before,
    speed_term,
    saved_faces,
    face_steps,
    traces,
    lag_offsets,
    snap_phase,
):
    count = lax.axis_size("gz")
    own, ny, nx = source_now.shape
    layers = 2 * own
    rows = ny // count
    steps = face_steps.shape[0]
    first_pairs, second_pairs = pairs_to_fields(count)
    back_pairs = [(b, a) for a, b in second_pairs]
    shots = lax.axis_size("shot")
    between, within = pairs_of_halos(count, shots)
    band_x, band_y = banded(nx), banded(ny)
    across = jnp.asarray(np.concatenate([band_x, band_x], axis=0), jnp.bfloat16)
    along = jnp.asarray(np.concatenate([band_y, band_y], axis=1), jnp.bfloat16)

    def regroup(a, b):
        return lax.ppermute(a, "gz", first_pairs), lax.ppermute(b, "gz", second_pairs)

    tall = held(layers + 2 * REACH, ny, nx)
    whole = f32(layers, ny, nx)
    slab = f32(REACH, ny, nx)
    half = f32(own, ny, nx)
    strips = held(count, layers, rows, nx)
    plane = ny * nx

    shared = shots % 2 == 0
    if shared:
        both = [
            (shot * count + a, shot * count + b)
            for shot in range(shots)
            for a, b in (first_pairs, second_pairs)[shot % 2]
        ]
        one = lax.ppermute(speed_term, ("shot", "gz"), both)
        speed_parts = one, lax.ppermute(one, "shot", [(shot, shot ^ 1) for shot in range(shots)])
    else:
        speed_parts = regroup(speed_term, speed_term)
    now = regroup(*choose(source_now, receiver_now))
    before = regroup(*choose(source_before, receiver_before))
    late, early, shifts = prepare(saved_faces, face_steps, lag_offsets, nx)
    early = regroup(early, early)
    cur, low, high = merge(merge_now_kernel, (tall, slab, slab), *now)
    low = lax.ppermute(low, ("shot", "gz"), between)
    high = lax.ppermute(high, "gz", within)
    prev, speed = merge(functools.partial(merge_rest_kernel, shared), (tall, whole), *before, *speed_parts)

    groups = count // 4
    pieces = max(1, 8 // groups)
    waiting, under_way, arrived = [], [], []

    snap = None
    for step in range(steps):
        faces = late if step >= EARLY else early
        wide = len(faces)
        if step < steps - 1:
            lower = pl.pallas_call(
                functools.partial(lower_kernel, step),
                out_shape=(tall, tall, slab),
                in_specs=[VMEM] * 9,
                out_specs=(VMEM,) * 3,
                input_output_aliases={7: 0, 8: 1},
                compiler_params=PARAMS,
                cost_estimate=cost(60 * 4 * plane, 4 * 20 * plane),
                name="lower",
            )
            upper = pl.pallas_call(
                functools.partial(upper_kernel, step),
                out_shape=(tall, tall, slab),
                in_specs=[VMEM] * 8,
                out_specs=(VMEM,) * 3,
                input_output_aliases={6: 0, 7: 1},
                compiler_params=PARAMS,
                cost_estimate=cost(60 * 4 * plane, 4 * 20 * plane),
                name="upper",
            )
            cur, new, low = lower(across, along, low, speed, *faces, traces, cur, prev)
            low = lax.ppermute(low, ("shot", "gz"), between)
            cur, new, high = upper(across, along, high, speed, *faces, cur, new)
            high = lax.ppermute(high, "gz", within)
            landed = []
            if step not in (SNAP_EVERY, SNAP_EVERY + 1):
                low, *landed = lax.optimization_barrier((low, *[array for _, array in under_way]))
            if step not in (SNAP_EVERY, SNAP_EVERY + 1):
                arrived += [(part, array) for (part, _), array in zip(under_way, landed)]
                under_way = []
        else:
            new = prev
        operands = (snap_phase, across, along, speed, *faces, cur, new)
        inner = functools.partial(
            pl.pallas_call,
            compiler_params=PARAMS,
            cost_estimate=cost(60 * (layers - 8) * plane, 4 * 40 * plane),
            name="inner",
        )
        if step < steps - 1:
            alias = {5 + wide: 0}
            if snap is not None:
                operands, alias = (*operands, snap), {5 + wide: 0, 6 + wide: 1}
            new, snap = inner(
                functools.partial(inner_kernel, step, wide, True),
                out_shape=(tall, strips),
                in_specs=[SMEM] + [VMEM] * (len(operands) - 1),
                out_specs=(VMEM,) * 2,
                input_output_aliases=alias,
            )(*operands)
        else:
            (new,) = inner(
                functools.partial(inner_kernel, step, wide, False, None),
                out_shape=(tall,),
                in_specs=[VMEM] * (len(operands) - 1),
                out_specs=(VMEM,),
                input_output_aliases={4 + wide: 0},
            )(*operands[1:])
            last = pl.pallas_call(
                functools.partial(last_kernel, step),
                out_shape=(tall, tall, strips, half, half, f32(*strips.shape)),
                in_specs=[SMEM] + [VMEM] * 11,
                out_specs=(VMEM,) * 6,
                input_output_aliases={9: 0, 10: 1, 11: 2},
                compiler_params=PARAMS,
                name="last",
            )
            _, _, _, out_a, out_b, send = last(snap_phase, across, along, low, high, traces, speed, *faces, cur, new, snap)
        if step == 0:
            late, new = lax.optimization_barrier((late, new))
            late = regroup(late, late)
        if step == SNAP_EVERY - 1:
            strip_parts = merge(spread_kernel, (f32(groups, layers, rows, nx),) * 4, snap)
            for which in (1, 2, 3):
                payload, new = lax.optimization_barrier((strip_parts[which], new))
                under_way.append((which, lax.ppermute(payload, "gz", [(i, i ^ which) for i in range(count)])))
            snap = None
        if step == SNAP_EVERY + 1:
            *landed, new = lax.optimization_barrier((*[array for _, array in under_way], new))
            own_strips, *sent = merge(
                regather_kernel,
                (f32(4, layers, rows, nx), *[f32(4 // pieces, layers, rows, nx)] * (pieces * (groups - 1))),
                strip_parts[0],
                *landed,
            )
            waiting = [
                (j < pieces, j, [(i, 4 * ((i // 4) ^ (j // pieces + 1)) + i % 4) for i in range(count)])
                for j in range(len(sent))
            ]
            under_way = []
        slots = max(1, steps - 1 - step)
        far = [item for item in waiting if not item[0]]
        near = [item for item in waiting if item[0]]
        chosen = far[: -(-len(far) // slots)] + (near[: -(-len(near) // slots)] if step > SNAP_EVERY + 1 or not far else [])
        waiting = [item for item in waiting if item not in chosen]
        for _, which_part, pairs in chosen:
            payload = sent[which_part]
            payload, new = lax.optimization_barrier((payload, new))
            under_way.append((which_part, lax.ppermute(payload, "gz", pairs)))
        prev, cur = cur, new

    (first,) = merge(
        collect_kernel, (f32(count, layers, rows, nx),), own_strips, *[array for _, array in sorted(arrived + under_way, key=lambda item: item[0])]
    )
    second = lax.all_to_all(send, "gz", split_axis=0, concat_axis=0, tiled=True)
    back_a = lax.ppermute(out_a, "gz", first_pairs)
    back_b = lax.ppermute(out_b, "gz", back_pairs)
    source_final, receiver_final = choose(back_a, back_b, back=True)
    image_out = images(shifts, (first, second), lag_offsets.shape[0])
    return (image_out, source_final, receiver_final)


def solution(mesh):
    return jax.shard_map(
        local,
        mesh=mesh,
        in_specs=(
            P(("shot", "gz"), None, None),
            P(("shot", "gz"), None, None),
            P(("shot", "gz"), None, None),
            P(("shot", "gz"), None, None),
            P("gz", None, None),
            P("shot", None, "gz", None),
            P(),
            P("shot", None, None),
            P(),
            P(),
        ),
        out_specs=(
            P("shot", None, "gz", None),
            P(("shot", "gz"), None, None),
            P(("shot", "gz"), None, None),
        ),
        check_vma=False,
    )
```

```python
import functools

import jax
import jax.numpy as jnp
import numpy as np
from jax import lax
from jax.experimental import pallas as pl
from jax.experimental.pallas import tpu as pltpu
from jax.sharding import PartitionSpec as P


SNAP_EVERY = 6
REACH = 4
EARLY = 4
PACKED = 2

SCALE = 5040.0
NEAR = (8064.0, -1008.0, 128.0, -9.0)
CENTRE = -43050.0
damping = 0.25
smoothing = 16.0

VMEM = pl.BlockSpec(memory_space=pltpu.VMEM)
SMEM = pl.BlockSpec(memory_space=pltpu.SMEM)
ANY = pl.BlockSpec(memory_space=pl.ANY)
HBM = pl.BlockSpec(memory_space=pltpu.HBM)
PARAMS = pltpu.CompilerParams(vmem_limit_bytes=24 * 1024 * 1024)


def f32(*shape):
    return jax.ShapeDtypeStruct(shape, jnp.float32)


def held(*shape):
    return pltpu.VMEM(shape, jnp.float32)


def cost(flops, bytes_accessed):
    return pl.CostEstimate(flops=int(flops), bytes_accessed=int(bytes_accessed), transcendentals=0)


def banded(size):
    apart = np.abs(np.arange(size)[:, None] - np.arange(size)[None, :])
    table = np.zeros((size, size), np.float32)
    for k, weight in enumerate(NEAR):
        table[apart == k + 1] = weight
    return table


def pairs_to_fields(count):
    first, second = [], []
    for base in range(0, count, 4):
        first += [(base, base), (base + 1, base + 2), (base + 2, base + 1), (base + 3, base + 3)]
        second += [(base, base + 2), (base + 1, base), (base + 2, base + 3), (base + 3, base + 1)]
    return first, second


def pairs_of_halos(count, shots):
    between = []
    for shot in range(shots):
        base = shot * count
        for group in range(count // 4 - 1):
            for field in range(2):
                low, high = base + 4 * group + 2 * field + 1, base + 4 * group + 4 + 2 * field
                between += [(low, high), (high, low)]
        for end in (0, 2, count - 3, count - 1):
            between.append((base + end, (shot ^ 1) * count + end if shots % 2 == 0 else base + (end ^ 2)))
    return between, [(i, i ^ 1) for i in range(count)]


def my_field():
    return lax.rem(lax.axis_index("gz") // 2, 2)


def my_half():
    return lax.rem(lax.axis_index("gz"), 2)


def place_of(local, layers):
    return jnp.where(my_half() == 0, local, layers - 1 - local)


def in_order(run, here, there):
    pl.when(my_half() == 0)(lambda: run(here, there))
    pl.when(my_half() != 0)(lambda: run(there, here))


def copy_both(pairs, sem):
    copies = [pltpu.make_async_copy(a, b, sem.at[i]) for i, (a, b) in enumerate(pairs)]
    for copy in copies:
        copy.start()
    for copy in copies:
        copy.wait()


def choose_kernel(here, there, first, second, sem):
    in_order(lambda a, b: copy_both(((a, first), (b, second)), sem), here, there)


def choose_back_kernel(here, there, first, second, one, two, sem):
    in_order(lambda a, b: copy_both(((a, one), (b, two)), sem), here, there)
    copy_both(((one, first), (two, second)), sem)


def choose(here, there, back=False):
    like = jax.ShapeDtypeStruct(here.shape, here.dtype)
    staged = [pltpu.VMEM(here.shape, here.dtype)] * 2 if back else []
    return pl.pallas_call(
        choose_back_kernel if back else choose_kernel,
        out_shape=(like, like),
        in_specs=[ANY if back else HBM] * 2,
        out_specs=(ANY if back else VMEM,) * 2,
        scratch_shapes=[*staged, pltpu.SemaphoreType.DMA((2,))],
        compiler_params=PARAMS,
        name="choose",
    )(here, there)


def prepare_kernel(layers, face_steps, lags, faces, late, early, shifts, gathered):
    steps = face_steps.shape[0]
    nx = shifts.shape[1] // 2
    gathered[...] = jnp.zeros_like(gathered)

    def gather(step, layer, row):
        base = face_steps[step] * (8 * layers) + layer
        gathered[row : row + 4] = faces[pl.ds(base + 4 * layers, 4, stride=layers), :]
        gathered[row + 4 : row + 8] = faces[pl.ds(base, 4, stride=layers), :]

    for plane in range(steps // PACKED):
        for layer in range(layers):
            for step in range(PACKED):
                gather(PACKED * plane + step, layer, 8 * (PACKED * layer + step))
        if plane < EARLY // PACKED:
            early[plane] = gathered[...].T
        else:
            late[plane - EARLY // PACKED] = gathered[...].T

    apart = lax.broadcasted_iota(jnp.int32, (nx, nx), 1) - lax.broadcasted_iota(jnp.int32, (nx, nx), 0)
    for index in range(lags.shape[0]):
        columns = slice(index * nx, (index + 1) * nx)
        for which, lag in ((0, lags[index]), (1, -lags[index])):
            moved = jnp.where(apart == lag, 1.0, 0.0).astype(jnp.bfloat16)
            shifts[which, :nx, columns] = moved
            shifts[which, nx:, columns] = moved


def prepare(saved_faces, face_steps, lag_offsets, nx):
    slots, eight, layers, ny = saved_faces.shape
    planes = face_steps.shape[0] // PACKED
    return pl.pallas_call(
        functools.partial(prepare_kernel, layers),
        out_shape=(
            f32(planes - EARLY // PACKED, ny, 128),
            f32(EARLY // PACKED, ny, 128),
            jax.ShapeDtypeStruct((2, 2 * nx, lag_offsets.shape[0] * nx), jnp.bfloat16),
        ),
        in_specs=[SMEM, SMEM, VMEM],
        out_specs=(VMEM,) * 3,
        scratch_shapes=[pltpu.VMEM((128, ny), jnp.float32)],
        compiler_params=PARAMS,
        name="prepare",
    )(face_steps, lag_offsets, saved_faces.reshape(slots * eight * layers, ny))


def for_each_part(layers, run):
    def one_layer(j, carry):
        place = place_of(j, layers)
        part = (place >= layers // 2).astype(jnp.int32)
        q = place - part * (layers // 2)
        pl.when(part == my_field())(lambda: run(j, q, 0))
        pl.when(part != my_field())(lambda: run(j, q, 1))
        return carry

    lax.fori_loop(0, layers, one_layer, 0, unroll=2)


def merge_now_kernel(now_a, now_b, cur, low, high):
    layers = 2 * now_a.shape[0]

    def run(j, q, which):
        cur[REACH + j] = (now_a, now_b)[which][q]

    for_each_part(layers, run)
    low[...] = cur[REACH : 2 * REACH]
    high[...] = cur[layers : layers + REACH]


def merge_rest_kernel(shared, before_a, before_b, speed_a, speed_b, prev, speed):
    flipped = (lax.rem(lax.axis_index("shot"), 2) == 1) & shared

    def run(j, q, which):
        prev[REACH + j] = (before_a, before_b)[which][q]
        ahead, other = (speed_a, speed_b) if which == 0 else (speed_b, speed_a)
        speed[j] = jnp.where(flipped, other[q], ahead[q]) * (1.0 / SCALE)

    for_each_part(2 * before_a.shape[0], run)


def merge(kernel, shapes, *parts):
    return pl.pallas_call(
        kernel, out_shape=shapes, in_specs=[VMEM] * len(parts), out_specs=(VMEM,) * len(shapes), compiler_params=PARAMS
    )(*parts)


def split(u):
    high = u.astype(jnp.bfloat16)
    return high, (u - high.astype(jnp.float32)).astype(jnp.bfloat16)


def advance(step, across, along, cur, prev, speed, faces, new, local):
    layers, ny, nx = speed.shape
    column = lax.broadcasted_iota(jnp.int32, (ny, nx), 1)
    edge = ((column < REACH) | (column >= nx - REACH)) & (my_field() == 0)

    def placed(layer):
        place = place_of(layer, layers)
        part = (place >= layers // 2).astype(jnp.int32)
        plane, inside = (step if step < EARLY else step - EARLY) // PACKED, step % PACKED
        lane = 8 * (PACKED * (place - part * (layers // 2)) + inside) + REACH
        held = jnp.where(part == 0, faces[0][plane], faces[1][plane])
        return pltpu.roll(held, lax.rem(128 - lane, 128), axis=1)

    for first in range(0, len(local), 2):
        pair = local[first : first + 2]
        inputs = [cur[REACH + layer] for layer in pair]
        halves = [split(u) for u in inputs]
        along_sum = jnp.dot(
            along[...],
            jnp.concatenate([jnp.concatenate(half, axis=0) for half in halves], axis=1),
            preferred_element_type=jnp.float32,
        )
        across_sum = jnp.dot(
            jnp.concatenate([jnp.concatenate(half, axis=1) for half in halves], axis=0),
            across[...],
            preferred_element_type=jnp.float32,
        )
        for i, layer in enumerate(pair):
            e, u = REACH + layer, inputs[i]
            total = across_sum[i * ny : (i + 1) * ny] + along_sum[:, i * nx : (i + 1) * nx]
            for k in range(REACH):
                total = total + NEAR[k] * (cur[e + (k + 1)] + cur[e - (k + 1)])
            total = total + CENTRE * u
            updated = 2.0 * u - prev[e] + speed[layer] * total
            new[e] = jnp.where(edge, placed(layer), updated)


def fill_low(low, cur):
    index = lax.axis_index("gz")
    place = 2 * (index // 4) + my_half()
    inside = (place > 0) & (place < lax.axis_size("gz") // 2 - 1)
    for d in range(REACH):
        cur[REACH - 1 - d] = jnp.where(inside, low[d], 0.0)


def fill_high(high, cur):
    layers = cur.shape[0] - 2 * REACH
    for d in range(REACH):
        cur[REACH + layers + d] = high[REACH - 1 - d]


def add_trace(step, traces, new):
    @pl.when(lax.axis_index("gz") == 2)
    def _():
        new[REACH] = new[REACH] + traces[step].astype(jnp.float32)


def keep_snapshot(step, phase, new, snap):
    count, layers, rows, _ = snap.shape
    window = step // SNAP_EVERY

    @pl.when(phase[window] == step - window * SNAP_EVERY)
    def _():
        def one_layer(j, carry):
            place = place_of(j, layers)
            for strip in range(count):
                snap[strip, place] = new[REACH + j, strip * rows : (strip + 1) * rows, :]
            return carry

        lax.fori_loop(0, layers, one_layer, 0)


def lower_kernel(step, across, along, low, speed, face_a, face_b, traces, cur_in, prev, cur, new, low_out):
    fill_low(low, cur)
    advance(step, across, along, cur, prev, speed, (face_a, face_b), new, list(range(REACH)))
    add_trace(step, traces, new)
    low_out[...] = new[REACH : 2 * REACH]


def upper_kernel(step, across, along, high, speed, face_a, face_b, cur_in, prev, cur, new, high_out):
    layers = speed.shape[0]
    fill_high(high, cur)
    advance(step, across, along, cur, prev, speed, (face_a, face_b), new, list(range(layers - REACH, layers)))
    high_out[...] = new[layers : layers + REACH]


def inner_kernel(step, faces, keep, phase, across, along, speed, *rest):
    face, rest = rest[:faces], rest[faces:]
    cur, prev, new = rest[0], rest[1], rest[-2] if keep else rest[-1]
    layers = speed.shape[0]
    advance(step, across, along, cur, prev, speed, face, new, list(range(REACH, layers - REACH)))
    if keep:
        keep_snapshot(step, phase, new, rest[-1])


def last_kernel(
    step, phase, across, along, low, high, traces, speed, face_a, face_b, cur_in, prev, snap_in, cur, new, snap, out_a, out_b, send
):
    layers = speed.shape[0]
    fill_low(low, cur)
    fill_high(high, cur)
    outer = [*range(REACH), *range(layers - REACH, layers)]
    advance(step, across, along, cur, prev, speed, (face_a, face_b), new, outer)
    add_trace(step, traces, new)
    keep_snapshot(step, phase, new, snap)

    def run(j, q, which):
        (out_a, out_b)[which][q] = new[REACH + j]

    for_each_part(layers, run)

    def one_strip(strip, carry):
        send[strip] = snap[strip]
        return carry

    lax.fori_loop(0, snap.shape[0], one_strip, 0)


def spread_kernel(snap, *outs):
    mine = lax.rem(lax.axis_index("gz"), 4)
    for which, out in enumerate(outs):

        def one(group, carry):
            out[group] = snap[4 * group + jnp.bitwise_xor(mine, which)]
            return carry

        lax.fori_loop(0, out.shape[0], one, 0)


def regather_kernel(*refs):
    held_by, (own, *parts) = refs[:4], refs[4:]
    groups = held_by[0].shape[0]
    pieces = len(parts) // (groups - 1)
    size = 4 // pieces
    group = lax.axis_index("gz") // 4
    mine = lax.rem(lax.axis_index("gz"), 4)
    for which, strips in enumerate(held_by):
        source = jnp.bitwise_xor(mine, which)
        own[source] = strips[group]
        for i, part in enumerate(parts):
            first = (i % pieces) * size

            @pl.when((source >= first) & (source < first + size))
            def _(i=i, part=part, first=first, source=source, strips=strips):
                part[source - first] = strips[jnp.bitwise_xor(group, i // pieces + 1)]


def collect_kernel(own, *refs):
    parts, out = refs[:-1], refs[-1]
    pieces = len(parts) // (out.shape[0] // 4 - 1)
    size = 4 // pieces
    group = lax.axis_index("gz") // 4
    for i in range(4):
        out[4 * group + i] = own[i]
    for i, part in enumerate(parts):
        first = 4 * jnp.bitwise_xor(group, i // pieces + 1) + (i % pieces) * size
        for j in range(size):
            out[first + j] = part[j]


def image_kernel(shifts, *refs):
    windows, (out, light, parts, stage, sem) = refs[:-5], refs[-5:]
    _, layers, rows, nx = windows[0].shape
    lags, depth = out.shape[:2]
    size = layers * rows
    groups = depth // (2 * layers)
    table = sweep_table(depth)

    def fill(group, carry):
        for which in range(2):
            for window in range(len(windows)):
                for half in range(2):
                    first = (2 * window + half) * size
                    value = windows[window][4 * group + 2 * which + half].reshape(size, nx)
                    high, low = split(value)
                    parts[which, group, first : first + size, :nx] = high
                    parts[which, group, first : first + size, nx:] = low
        return carry

    lax.fori_loop(0, groups, fill, 0)

    carried = jnp.zeros((rows, nx), jnp.float32)
    for d in range(depth):
        block, layer = d // layers, d % layers
        device = (block // 2) * 4 + block % 2
        squares = sum(window[device, layer] * window[device, layer] for window in windows)
        carried = squares * table[d] + carried * (smoothing * table[d])
        light[d] = carried
    carried = jnp.zeros((rows, nx), jnp.float32)
    for d in reversed(range(depth)):
        carried = light[d] + carried * (smoothing * table[d])
        light[d] = 1.0 / (carried + damping)

    def put(pair, slot):
        return pltpu.make_async_copy(stage.at[slot], out.at[pl.ds(2 * pair, 2)], sem.at[slot])

    def one_pair(pair, carry):
        slot = lax.rem(pair, 2)
        pl.when(pair >= 2)(lambda: put(pair - 2, slot).wait())
        columns = pl.ds(pl.multiple_of(pair * 2 * nx, 2 * nx), 2 * nx)
        toward, away = shifts[0, :, columns], shifts[1, :, columns]

        def one_group(group, carry):
            moved = jnp.dot(parts[0, group], toward, preferred_element_type=jnp.float32) * jnp.dot(
                parts[1, group], away, preferred_element_type=jnp.float32
            )
            raw = sum(moved[2 * size * window : 2 * size * (window + 1)] for window in range(len(windows)))
            where = pl.ds(2 * layers * group, 2 * layers)
            inverse = light[where].reshape(2 * size, nx)
            for i in range(2):
                value = (raw[:, i * nx : (i + 1) * nx] * inverse).astype(stage.dtype)
                stage[slot, i, where] = value.reshape(2 * layers, rows, nx)
            return carry

        lax.fori_loop(0, groups, one_group, 0)
        put(pair, slot).start()
        return carry

    lax.fori_loop(0, lags // 2, one_pair, 0)
    for pair in (lags // 2 - 2, lags // 2 - 1):
        put(pair, pair % 2).wait()


def sweep_table(depth):
    table, before = [], 0.0
    for _ in range(depth):
        before = 1.0 / (1.0 + 2.0 * smoothing - smoothing * smoothing * before)
        table.append(before)
    return table


def images(shifts, windows, lags):
    count, layers, rows, nx = windows[0].shape
    depth = count // 2 * layers
    return pl.pallas_call(
        image_kernel,
        out_shape=jax.ShapeDtypeStruct((lags, depth, rows, nx), jnp.bfloat16),
        in_specs=[VMEM] * (1 + len(windows)),
        out_specs=ANY,
        scratch_shapes=[
            pltpu.VMEM((depth, rows, nx), jnp.float32),
            pltpu.VMEM((2, count // 4, 2 * len(windows) * layers * rows, 2 * nx), jnp.bfloat16),
            pltpu.VMEM((2, 2, depth, rows, nx), jnp.bfloat16),
            pltpu.SemaphoreType.DMA((2,)),
        ],
        compiler_params=PARAMS,
        name="images",
    )(shifts, *windows)


def local(
    source_now,
    source_before,
    receiver_now,
    receiver_before,
    speed_term,
    saved_faces,
    face_steps,
    traces,
    lag_offsets,
    snap_phase,
):
    count = lax.axis_size("gz")
    own, ny, nx = source_now.shape
    layers = 2 * own
    rows = ny // count
    steps = face_steps.shape[0]
    first_pairs, second_pairs = pairs_to_fields(count)
    back_pairs = [(b, a) for a, b in second_pairs]
    shots = lax.axis_size("shot")
    between, within = pairs_of_halos(count, shots)
    band_x, band_y = banded(nx), banded(ny)
    across = jnp.asarray(np.concatenate([band_x, band_x], axis=0), jnp.bfloat16)
    along = jnp.asarray(np.concatenate([band_y, band_y], axis=1), jnp.bfloat16)

    def regroup(a, b):
        return lax.ppermute(a, "gz", first_pairs), lax.ppermute(b, "gz", second_pairs)

    tall = held(layers + 2 * REACH, ny, nx)
    whole = f32(layers, ny, nx)
    slab = f32(REACH, ny, nx)
    half = f32(own, ny, nx)
    strips = held(count, layers, rows, nx)
    plane = ny * nx

    shared = shots % 2 == 0
    if shared:
        both = [
            (shot * count + a, shot * count + b)
            for shot in range(shots)
            for a, b in (first_pairs, second_pairs)[shot % 2]
        ]
        one = lax.ppermute(speed_term, ("shot", "gz"), both)
        speed_parts = one, lax.ppermute(one, "shot", [(shot, shot ^ 1) for shot in range(shots)])
    else:
        speed_parts = regroup(speed_term, speed_term)
    now = regroup(*choose(source_now, receiver_now))
    before = regroup(*choose(source_before, receiver_before))
    late, early, shifts = prepare(saved_faces, face_steps, lag_offsets, nx)
    early = regroup(early, early)
    cur, low, high = merge(merge_now_kernel, (tall, slab, slab), *now)
    low = lax.ppermute(low, ("shot", "gz"), between)
    high = lax.ppermute(high, "gz", within)
    prev, speed = merge(functools.partial(merge_rest_kernel, shared), (tall, whole), *before, *speed_parts)

    groups = count // 4
    pieces = max(1, 8 // groups)
    waiting, under_way, arrived = [], [], []

    snap = None
    for step in range(steps):
        faces = late if step >= EARLY else early
        wide = len(faces)
        if step < steps - 1:
            lower = pl.pallas_call(
                functools.partial(lower_kernel, step),
                out_shape=(tall, tall, slab),
                in_specs=[VMEM] * 9,
                out_specs=(VMEM,) * 3,
                input_output_aliases={7: 0, 8: 1},
                compiler_params=PARAMS,
                cost_estimate=cost(60 * 4 * plane, 4 * 20 * plane),
                name="lower",
            )
            upper = pl.pallas_call(
                functools.partial(upper_kernel, step),
                out_shape=(tall, tall, slab),
                in_specs=[VMEM] * 8,
                out_specs=(VMEM,) * 3,
                input_output_aliases={6: 0, 7: 1},
                compiler_params=PARAMS,
                cost_estimate=cost(60 * 4 * plane, 4 * 20 * plane),
                name="upper",
            )
            cur, new, low = lower(across, along, low, speed, *faces, traces, cur, prev)
            low = lax.ppermute(low, ("shot", "gz"), between)
            cur, new, high = upper(across, along, high, speed, *faces, cur, new)
            high = lax.ppermute(high, "gz", within)
            landed = []
            if step not in (SNAP_EVERY, SNAP_EVERY + 1):
                low, *landed = lax.optimization_barrier((low, *[array for _, array in under_way]))
            if step not in (SNAP_EVERY, SNAP_EVERY + 1):
                arrived += [(part, array) for (part, _), array in zip(under_way, landed)]
                under_way = []
        else:
            new = prev
        operands = (snap_phase, across, along, speed, *faces, cur, new)
        inner = functools.partial(
            pl.pallas_call,
            compiler_params=PARAMS,
            cost_estimate=cost(60 * (layers - 8) * plane, 4 * 40 * plane),
            name="inner",
        )
        if step < steps - 1:
            alias = {5 + wide: 0}
            if snap is not None:
                operands, alias = (*operands, snap), {5 + wide: 0, 6 + wide: 1}
            new, snap = inner(
                functools.partial(inner_kernel, step, wide, True),
                out_shape=(tall, strips),
                in_specs=[SMEM] + [VMEM] * (len(operands) - 1),
                out_specs=(VMEM,) * 2,
                input_output_aliases=alias,
            )(*operands)
        else:
            (new,) = inner(
                functools.partial(inner_kernel, step, wide, False, None),
                out_shape=(tall,),
                in_specs=[VMEM] * (len(operands) - 1),
                out_specs=(VMEM,),
                input_output_aliases={4 + wide: 0},
            )(*operands[1:])
            last = pl.pallas_call(
                functools.partial(last_kernel, step),
                out_shape=(tall, tall, strips, half, half, f32(*strips.shape)),
                in_specs=[SMEM] + [VMEM] * 11,
                out_specs=(VMEM,) * 6,
                input_output_aliases={9: 0, 10: 1, 11: 2},
                compiler_params=PARAMS,
                name="last",
            )
            _, _, _, out_a, out_b, send = last(snap_phase, across, along, low, high, traces, speed, *faces, cur, new, snap)
        if step == 0:
            late, new = lax.optimization_barrier((late, new))
            late = regroup(late, late)
        if step == SNAP_EVERY - 1:
            strip_parts = merge(spread_kernel, (f32(groups, layers, rows, nx),) * 4, snap)
            for which in (1, 2, 3):
                payload, new = lax.optimization_barrier((strip_parts[which], new))
                under_way.append((which, lax.ppermute(payload, "gz", [(i, i ^ which) for i in range(count)])))
            snap = None
        if step == SNAP_EVERY + 1:
            *landed, new = lax.optimization_barrier((*[array for _, array in under_way], new))
            own_strips, *sent = merge(
                regather_kernel,
                (f32(4, layers, rows, nx), *[f32(4 // pieces, layers, rows, nx)] * (pieces * (groups - 1))),
                strip_parts[0],
                *landed,
            )
            waiting = [
                (j < pieces, j, [(i, 4 * ((i // 4) ^ (j // pieces + 1)) + i % 4) for i in range(count)])
                for j in range(len(sent))
            ]
            under_way = []
        slots = max(1, steps - 1 - step)
        far = [item for item in waiting if not item[0]]
        near = [item for item in waiting if item[0]]
        chosen = far[: -(-len(far) // slots)] + (near[: -(-len(near) // slots)] if step > SNAP_EVERY + 1 or not far else [])
        waiting = [item for item in waiting if item not in chosen]
        for _, which_part, pairs in chosen:
            payload = sent[which_part]
            payload, new = lax.optimization_barrier((payload, new))
            under_way.append((which_part, lax.ppermute(payload, "gz", pairs)))
        prev, cur = cur, new

    (first,) = merge(
        collect_kernel, (f32(count, layers, rows, nx),), own_strips, *[array for _, array in sorted(arrived + under_way, key=lambda item: item[0])]
    )
    second = lax.all_to_all(send, "gz", split_axis=0, concat_axis=0, tiled=True)
    back_a = lax.ppermute(out_a, "gz", first_pairs)
    back_b = lax.ppermute(out_b, "gz", back_pairs)
    source_final, receiver_final = choose(back_a, back_b, back=True)
    image_out = images(shifts, (first, second), lag_offsets.shape[0])
    return (image_out, source_final, receiver_final)


def solution(mesh):
    return jax.shard_map(
        local,
        mesh=mesh,
        in_specs=(
            P(("shot", "gz"), None, None),
            P(("shot", "gz"), None, None),
            P(("shot", "gz"), None, None),
            P(("shot", "gz"), None, None),
            P("gz", None, None),
            P("shot", None, "gz", None),
            P(),
            P("shot", None, None),
            P(),
            P(),
        ),
        out_specs=(
            P("shot", None, "gz", None),
            P(("shot", "gz"), None, None),
            P(("shot", "gz"), None, None),
        ),
        check_vma=False,
    )
```

```python
import functools

import jax
import jax.numpy as jnp
import numpy as np
from jax import lax
from jax.experimental import pallas as pl
from jax.experimental.pallas import tpu as pltpu
from jax.sharding import PartitionSpec as P


SNAP_EVERY = 6
REACH = 4
EARLY = 4
PACKED = 2

SCALE = 5040.0
NEAR = (8064.0, -1008.0, 128.0, -9.0)
CENTRE = -43050.0
damping = 0.25
smoothing = 16.0

VMEM = pl.BlockSpec(memory_space=pltpu.VMEM)
SMEM = pl.BlockSpec(memory_space=pltpu.SMEM)
ANY = pl.BlockSpec(memory_space=pl.ANY)
HBM = pl.BlockSpec(memory_space=pltpu.HBM)
PARAMS = pltpu.CompilerParams(vmem_limit_bytes=24 * 1024 * 1024)


def f32(*shape):
    return jax.ShapeDtypeStruct(shape, jnp.float32)


def held(*shape):
    return pltpu.VMEM(shape, jnp.float32)


def cost(flops, bytes_accessed):
    return pl.CostEstimate(flops=int(flops), bytes_accessed=int(bytes_accessed), transcendentals=0)


def banded(size):
    apart = np.abs(np.arange(size)[:, None] - np.arange(size)[None, :])
    table = np.zeros((size, size), np.float32)
    for k, weight in enumerate(NEAR):
        table[apart == k + 1] = weight
    return table


def pairs_to_fields(count):
    first, second = [], []
    for base in range(0, count, 4):
        first += [(base, base), (base + 1, base + 2), (base + 2, base + 1), (base + 3, base + 3)]
        second += [(base, base + 2), (base + 1, base), (base + 2, base + 3), (base + 3, base + 1)]
    return first, second


def pairs_of_halos(count, shots):
    between = []
    for shot in range(shots):
        base = shot * count
        for group in range(count // 4 - 1):
            for field in range(2):
                low, high = base + 4 * group + 2 * field + 1, base + 4 * group + 4 + 2 * field
                between += [(low, high), (high, low)]
        for end in (0, 2, count - 3, count - 1):
            between.append((base + end, (shot ^ 1) * count + end if shots % 2 == 0 else base + (end ^ 2)))
    return between, [(i, i ^ 1) for i in range(count)]


def my_field():
    return lax.rem(lax.axis_index("gz") // 2, 2)


def my_half():
    return lax.rem(lax.axis_index("gz"), 2)


def place_of(local, layers):
    return jnp.where(my_half() == 0, local, layers - 1 - local)


def in_order(run, here, there):
    pl.when(my_half() == 0)(lambda: run(here, there))
    pl.when(my_half() != 0)(lambda: run(there, here))


def copy_both(pairs, sem):
    copies = [pltpu.make_async_copy(a, b, sem.at[i]) for i, (a, b) in enumerate(pairs)]
    for copy in copies:
        copy.start()
    for copy in copies:
        copy.wait()


def choose_kernel(here, there, first, second, sem):
    in_order(lambda a, b: copy_both(((a, first), (b, second)), sem), here, there)


def choose_back_kernel(here, there, first, second, one, two, sem):
    in_order(lambda a, b: copy_both(((a, one), (b, two)), sem), here, there)
    copy_both(((one, first), (two, second)), sem)


def choose(here, there, back=False):
    like = jax.ShapeDtypeStruct(here.shape, here.dtype)
    staged = [pltpu.VMEM(here.shape, here.dtype)] * 2 if back else []
    return pl.pallas_call(
        choose_back_kernel if back else choose_kernel,
        out_shape=(like, like),
        in_specs=[ANY if back else HBM] * 2,
        out_specs=(ANY if back else VMEM,) * 2,
        scratch_shapes=[*staged, pltpu.SemaphoreType.DMA((2,))],
        compiler_params=PARAMS,
        name="choose",
    )(here, there)


def prepare_kernel(layers, face_steps, lags, faces, late, early, shifts, gathered):
    steps = face_steps.shape[0]
    nx = shifts.shape[1] // 2
    gathered[...] = jnp.zeros_like(gathered)

    def gather(step, layer, row):
        base = face_steps[step] * (8 * layers) + layer
        gathered[row : row + 4] = faces[pl.ds(base + 4 * layers, 4, stride=layers), :]
        gathered[row + 4 : row + 8] = faces[pl.ds(base, 4, stride=layers), :]

    for plane in range(steps // PACKED):
        for layer in range(layers):
            for step in range(PACKED):
                gather(PACKED * plane + step, layer, 8 * (PACKED * layer + step))
        if plane < EARLY // PACKED:
            early[plane] = gathered[...].T
        else:
            late[plane - EARLY // PACKED] = gathered[...].T

    apart = lax.broadcasted_iota(jnp.int32, (nx, nx), 1) - lax.broadcasted_iota(jnp.int32, (nx, nx), 0)
    for index in range(lags.shape[0]):
        columns = slice(index * nx, (index + 1) * nx)
        for which, lag in ((0, lags[index]), (1, -lags[index])):
            moved = jnp.where(apart == lag, 1.0, 0.0).astype(jnp.bfloat16)
            shifts[which, :nx, columns] = moved
            shifts[which, nx:, columns] = moved


def prepare(saved_faces, face_steps, lag_offsets, nx):
    slots, eight, layers, ny = saved_faces.shape
    planes = face_steps.shape[0] // PACKED
    return pl.pallas_call(
        functools.partial(prepare_kernel, layers),
        out_shape=(
            f32(planes - EARLY // PACKED, ny, 128),
            f32(EARLY // PACKED, ny, 128),
            jax.ShapeDtypeStruct((2, 2 * nx, lag_offsets.shape[0] * nx), jnp.bfloat16),
        ),
        in_specs=[SMEM, SMEM, VMEM],
        out_specs=(VMEM,) * 3,
        scratch_shapes=[pltpu.VMEM((128, ny), jnp.float32)],
        compiler_params=PARAMS,
        name="prepare",
    )(face_steps, lag_offsets, saved_faces.reshape(slots * eight * layers, ny))


def for_each_part(layers, run):
    def one_layer(j, carry):
        place = place_of(j, layers)
        part = (place >= layers // 2).astype(jnp.int32)
        q = place - part * (layers // 2)
        pl.when(part == my_field())(lambda: run(j, q, 0))
        pl.when(part != my_field())(lambda: run(j, q, 1))
        return carry

    lax.fori_loop(0, layers, one_layer, 0, unroll=2)


def merge_now_kernel(now_a, now_b, cur, low, high):
    layers = 2 * now_a.shape[0]

    def run(j, q, which):
        cur[REACH + j] = (now_a, now_b)[which][q]

    for_each_part(layers, run)
    low[...] = cur[REACH : 2 * REACH]
    high[...] = cur[layers : layers + REACH]


def merge_rest_kernel(shared, before_a, before_b, speed_a, speed_b, prev, speed):
    flipped = (lax.rem(lax.axis_index("shot"), 2) == 1) & shared

    def run(j, q, which):
        prev[REACH + j] = (before_a, before_b)[which][q]
        ahead, other = (speed_a, speed_b) if which == 0 else (speed_b, speed_a)
        speed[j] = jnp.where(flipped, other[q], ahead[q]) * (1.0 / SCALE)

    for_each_part(2 * before_a.shape[0], run)


def merge(kernel, shapes, *parts):
    return pl.pallas_call(
        kernel, out_shape=shapes, in_specs=[VMEM] * len(parts), out_specs=(VMEM,) * len(shapes), compiler_params=PARAMS
    )(*parts)


def split(u):
    high = u.astype(jnp.bfloat16)
    return high, (u - high.astype(jnp.float32)).astype(jnp.bfloat16)


def advance(step, across, along, cur, prev, speed, faces, new, local):
    layers, ny, nx = speed.shape
    column = lax.broadcasted_iota(jnp.int32, (ny, nx), 1)
    edge = ((column < REACH) | (column >= nx - REACH)) & (my_field() == 0)

    def placed(layer):
        place = place_of(layer, layers)
        part = (place >= layers // 2).astype(jnp.int32)
        plane, inside = (step if step < EARLY else step - EARLY) // PACKED, step % PACKED
        lane = 8 * (PACKED * (place - part * (layers // 2)) + inside) + REACH
        held = jnp.where(part == 0, faces[0][plane], faces[1][plane])
        return pltpu.roll(held, lax.rem(128 - lane, 128), axis=1)

    for first in range(0, len(local), 2):
        pair = local[first : first + 2]
        inputs = [cur[REACH + layer] for layer in pair]
        halves = [split(u) for u in inputs]
        along_sum = jnp.dot(
            along[...],
            jnp.concatenate([jnp.concatenate(half, axis=0) for half in halves], axis=1),
            preferred_element_type=jnp.float32,
        )
        across_sum = jnp.dot(
            jnp.concatenate([jnp.concatenate(half, axis=1) for half in halves], axis=0),
            across[...],
            preferred_element_type=jnp.float32,
        )
        for i, layer in enumerate(pair):
            e, u = REACH + layer, inputs[i]
            total = across_sum[i * ny : (i + 1) * ny] + along_sum[:, i * nx : (i + 1) * nx]
            for k in range(REACH):
                total = total + NEAR[k] * (cur[e + (k + 1)] + cur[e - (k + 1)])
            total = total + CENTRE * u
            updated = 2.0 * u - prev[e] + speed[layer] * total
            new[e] = jnp.where(edge, placed(layer), updated)


def fill_low(low, cur):
    index = lax.axis_index("gz")
    place = 2 * (index // 4) + my_half()
    inside = (place > 0) & (place < lax.axis_size("gz") // 2 - 1)
    for d in range(REACH):
        cur[REACH - 1 - d] = jnp.where(inside, low[d], 0.0)


def fill_high(high, cur):
    layers = cur.shape[0] - 2 * REACH
    for d in range(REACH):
        cur[REACH + layers + d] = high[REACH - 1 - d]


def add_trace(step, traces, new):
    @pl.when(lax.axis_index("gz") == 2)
    def _():
        new[REACH] = new[REACH] + traces[step].astype(jnp.float32)


def keep_snapshot(step, phase, new, snap):
    count, layers, rows, _ = snap.shape
    window = step // SNAP_EVERY

    @pl.when(phase[window] == step - window * SNAP_EVERY)
    def _():
        def one_layer(j, carry):
            place = place_of(j, layers)
            for strip in range(count):
                snap[strip, place] = new[REACH + j, strip * rows : (strip + 1) * rows, :]
            return carry

        lax.fori_loop(0, layers, one_layer, 0)


def lower_kernel(step, across, along, low, speed, face_a, face_b, traces, cur_in, prev, cur, new, low_out):
    fill_low(low, cur)
    advance(step, across, along, cur, prev, speed, (face_a, face_b), new, list(range(REACH)))
    add_trace(step, traces, new)
    low_out[...] = new[REACH : 2 * REACH]


def upper_kernel(step, across, along, high, speed, face_a, face_b, cur_in, prev, cur, new, high_out):
    layers = speed.shape[0]
    fill_high(high, cur)
    advance(step, across, along, cur, prev, speed, (face_a, face_b), new, list(range(layers - REACH, layers)))
    high_out[...] = new[layers : layers + REACH]


def inner_kernel(step, faces, keep, phase, across, along, speed, *rest):
    face, rest = rest[:faces], rest[faces:]
    cur, prev, new = rest[0], rest[1], rest[-2] if keep else rest[-1]
    layers = speed.shape[0]
    advance(step, across, along, cur, prev, speed, face, new, list(range(REACH, layers - REACH)))
    if keep:
        keep_snapshot(step, phase, new, rest[-1])


def last_kernel(
    step, phase, across, along, low, high, traces, speed, face_a, face_b, cur_in, prev, snap_in, cur, new, snap, out_a, out_b, send
):
    layers = speed.shape[0]
    fill_low(low, cur)
    fill_high(high, cur)
    outer = [*range(REACH), *range(layers - REACH, layers)]
    advance(step, across, along, cur, prev, speed, (face_a, face_b), new, outer)
    add_trace(step, traces, new)
    keep_snapshot(step, phase, new, snap)

    def run(j, q, which):
        (out_a, out_b)[which][q] = new[REACH + j]

    for_each_part(layers, run)

    def one_strip(strip, carry):
        send[strip] = snap[strip]
        return carry

    lax.fori_loop(0, snap.shape[0], one_strip, 0)


def spread_kernel(snap, *outs):
    mine = lax.rem(lax.axis_index("gz"), 4)
    for which, out in enumerate(outs):

        def one(group, carry):
            out[group] = snap[4 * group + jnp.bitwise_xor(mine, which)]
            return carry

        lax.fori_loop(0, out.shape[0], one, 0)


def regather_kernel(*refs):
    held_by, (own, *parts) = refs[:2], refs[2:]
    group = lax.axis_index("gz") // 4
    for i, strips in enumerate(held_by):
        own[i] = strips[group]
        for distance, part in enumerate(parts):
            part[i] = strips[jnp.bitwise_xor(group, distance + 1)]


def collect_kernel(*refs):
    parts, out = refs[:-1], refs[-1]
    group = lax.axis_index("gz") // 4
    mine = lax.rem(lax.axis_index("gz"), 4)
    for i, part in enumerate(parts):
        first = 4 * jnp.bitwise_xor(group, i // 2)
        for j in range(2):
            out[first + jnp.bitwise_xor(mine, 2 * (i % 2) + j)] = part[j]


def image_kernel(shifts, *refs):
    windows, (out, light, stage, sem) = refs[:-4], refs[-4:]
    _, layers, rows, nx = windows[0].shape
    lags, depth = out.shape[:2]
    size = layers * rows
    blocks = depth // layers
    table = sweep_table(depth)

    carried = jnp.zeros((rows, nx), jnp.float32)
    for d in range(depth):
        block, layer = d // layers, d % layers
        device = (block // 2) * 4 + block % 2
        squares = sum(window[device, layer] * window[device, layer] for window in windows)
        carried = squares * table[d] + carried * (smoothing * table[d])
        light[d] = carried
    carried = jnp.zeros((rows, nx), jnp.float32)
    for d in reversed(range(depth)):
        carried = light[d] + carried * (smoothing * table[d])
        light[d] = 1.0 / (carried + damping)

    def put(block, slot):
        return pltpu.make_async_copy(
            stage.at[slot], out.at[:, pl.ds(block * layers, layers)], sem.at[slot]
        )

    def one_block(block, carry):
        slot = lax.rem(block, 2)
        device = (block // 2) * 4 + lax.rem(block, 2)
        pl.when(block >= 2)(lambda: put(block - 2, slot).wait())

        def both(device, window):
            return jnp.concatenate(split(window[device].reshape(size, nx)), axis=1)

        sources = [both(device, window) for window in windows]
        receivers = [both(device + 2, window) for window in windows]
        inverse = light[pl.ds(block * layers, layers)].reshape(size, nx)
        for lag in range(0, lags, 2):
            columns = slice(lag * nx, (lag + 2) * nx)
            raw = 0.0
            for window in range(len(windows)):
                raw = raw + jnp.dot(
                    sources[window], shifts[0, :, columns], preferred_element_type=jnp.float32
                ) * jnp.dot(receivers[window], shifts[1, :, columns], preferred_element_type=jnp.float32)
            for i in range(2):
                value = (raw[:, i * nx : (i + 1) * nx] * inverse).astype(stage.dtype)
                stage[slot, lag + i] = value.reshape(layers, rows, nx)
        put(block, slot).start()
        return carry

    lax.fori_loop(0, blocks, one_block, 0)
    for block in (blocks - 2, blocks - 1):
        put(block, block % 2).wait()


def sweep_table(depth):
    table, before = [], 0.0
    for _ in range(depth):
        before = 1.0 / (1.0 + 2.0 * smoothing - smoothing * smoothing * before)
        table.append(before)
    return table


def images(shifts, windows, lags):
    count, layers, rows, nx = windows[0].shape
    depth = count // 2 * layers
    return pl.pallas_call(
        image_kernel,
        out_shape=jax.ShapeDtypeStruct((lags, depth, rows, nx), jnp.bfloat16),
        in_specs=[VMEM] * (1 + len(windows)),
        out_specs=ANY,
        scratch_shapes=[
            pltpu.VMEM((depth, rows, nx), jnp.float32),
            pltpu.VMEM((2, lags, layers, rows, nx), jnp.bfloat16),
            pltpu.SemaphoreType.DMA((2,)),
        ],
        compiler_params=PARAMS,
        name="images",
    )(shifts, *windows)


def local(
    source_now,
    source_before,
    receiver_now,
    receiver_before,
    speed_term,
    saved_faces,
    face_steps,
    traces,
    lag_offsets,
    snap_phase,
):
    count = lax.axis_size("gz")
    own, ny, nx = source_now.shape
    layers = 2 * own
    rows = ny // count
    steps = face_steps.shape[0]
    first_pairs, second_pairs = pairs_to_fields(count)
    back_pairs = [(b, a) for a, b in second_pairs]
    shots = lax.axis_size("shot")
    between, within = pairs_of_halos(count, shots)
    band_x, band_y = banded(nx), banded(ny)
    across = jnp.asarray(np.concatenate([band_x, band_x], axis=0), jnp.bfloat16)
    along = jnp.asarray(np.concatenate([band_y, band_y], axis=1), jnp.bfloat16)

    def regroup(a, b):
        return lax.ppermute(a, "gz", first_pairs), lax.ppermute(b, "gz", second_pairs)

    tall = held(layers + 2 * REACH, ny, nx)
    whole = f32(layers, ny, nx)
    slab = f32(REACH, ny, nx)
    half = f32(own, ny, nx)
    strips = held(count, layers, rows, nx)
    plane = ny * nx

    shared = shots % 2 == 0
    if shared:
        both = [
            (shot * count + a, shot * count + b)
            for shot in range(shots)
            for a, b in (first_pairs, second_pairs)[shot % 2]
        ]
        one = lax.ppermute(speed_term, ("shot", "gz"), both)
        speed_parts = one, lax.ppermute(one, "shot", [(shot, shot ^ 1) for shot in range(shots)])
    else:
        speed_parts = regroup(speed_term, speed_term)
    now = regroup(*choose(source_now, receiver_now))
    before = regroup(*choose(source_before, receiver_before))
    late, early, shifts = prepare(saved_faces, face_steps, lag_offsets, nx)
    early = regroup(early, early)
    cur, low, high = merge(merge_now_kernel, (tall, slab, slab), *now)
    low = lax.ppermute(low, ("shot", "gz"), between)
    high = lax.ppermute(high, "gz", within)
    prev, speed = merge(functools.partial(merge_rest_kernel, shared), (tall, whole), *before, *speed_parts)

    groups = count // 4
    near, far, under_way, arrived = [], [], [], []

    snap = None
    for step in range(steps):
        faces = late if step >= EARLY else early
        wide = len(faces)
        if step < steps - 1:
            lower = pl.pallas_call(
                functools.partial(lower_kernel, step),
                out_shape=(tall, tall, slab),
                in_specs=[VMEM] * 9,
                out_specs=(VMEM,) * 3,
                input_output_aliases={7: 0, 8: 1},
                compiler_params=PARAMS,
                cost_estimate=cost(60 * 4 * plane, 4 * 20 * plane),
                name="lower",
            )
            upper = pl.pallas_call(
                functools.partial(upper_kernel, step),
                out_shape=(tall, tall, slab),
                in_specs=[VMEM] * 8,
                out_specs=(VMEM,) * 3,
                input_output_aliases={6: 0, 7: 1},
                compiler_params=PARAMS,
                cost_estimate=cost(60 * 4 * plane, 4 * 20 * plane),
                name="upper",
            )
            cur, new, low = lower(across, along, low, speed, *faces, traces, cur, prev)
            low = lax.ppermute(low, ("shot", "gz"), between)
            cur, new, high = upper(across, along, high, speed, *faces, cur, new)
            high = lax.ppermute(high, "gz", within)
            if step > SNAP_EVERY:
                low, *landed = lax.optimization_barrier((low, *[array for _, array in under_way]))
                arrived += [(part, array) for (part, _), array in zip(under_way, landed)]
                under_way = []
        else:
            new = prev
        operands = (snap_phase, across, along, speed, *faces, cur, new)
        inner = functools.partial(
            pl.pallas_call,
            compiler_params=PARAMS,
            cost_estimate=cost(60 * (layers - 8) * plane, 4 * 40 * plane),
            name="inner",
        )
        if step < steps - 1:
            alias = {5 + wide: 0}
            if snap is not None:
                operands, alias = (*operands, snap), {5 + wide: 0, 6 + wide: 1}
            new, snap = inner(
                functools.partial(inner_kernel, step, wide, True),
                out_shape=(tall, strips),
                in_specs=[SMEM] + [VMEM] * (len(operands) - 1),
                out_specs=(VMEM,) * 2,
                input_output_aliases=alias,
            )(*operands)
        else:
            (new,) = inner(
                functools.partial(inner_kernel, step, wide, False, None),
                out_shape=(tall,),
                in_specs=[VMEM] * (len(operands) - 1),
                out_specs=(VMEM,),
                input_output_aliases={4 + wide: 0},
            )(*operands[1:])
            last = pl.pallas_call(
                functools.partial(last_kernel, step),
                out_shape=(tall, tall, strips, half, half, f32(*strips.shape)),
                in_specs=[SMEM] + [VMEM] * 11,
                out_specs=(VMEM,) * 6,
                input_output_aliases={9: 0, 10: 1, 11: 2},
                compiler_params=PARAMS,
                name="last",
            )
            _, _, _, out_a, out_b, send = last(snap_phase, across, along, low, high, traces, speed, *faces, cur, new, snap)
        if step == 0:
            late, new = lax.optimization_barrier((late, new))
            late = regroup(late, late)
        if step == SNAP_EVERY - 1:
            strip_parts = merge(spread_kernel, (f32(groups, layers, rows, nx),) * 4, snap)
            held_by = [strip_parts[0]]
            for which in (1, 2, 3):
                payload, new = lax.optimization_barrier((strip_parts[which], new))
                held_by.append(lax.ppermute(payload, "gz", [(i, i ^ which) for i in range(count)]))
            snap = None
        if step in (SNAP_EVERY, SNAP_EVERY + 1):
            side = step - SNAP_EVERY
            *landed, new = lax.optimization_barrier((*held_by[2 * side : 2 * side + 2], new))
            own, *sent = merge(regather_kernel, (f32(2, layers, rows, nx),) * groups, *landed)
            arrived.append((side, own))
            for distance in range(1, groups):
                (near if distance == 1 else far).append((2 * distance + side, sent[distance - 1]))
        if step >= SNAP_EVERY:
            slots = max(1, steps - 2 - step)
            total = len(far) + (groups - 2 if step == SNAP_EVERY else 0)
            many = min(len(far), -(-total // slots))
            chosen, far = far[:many], far[many:]
            if step > SNAP_EVERY + 1:
                chosen, near = chosen + near[:1], near[1:]
            for part, payload in chosen:
                payload, new = lax.optimization_barrier((payload, new))
                pairs = [(i, 4 * ((i // 4) ^ (part // 2)) + i % 4) for i in range(count)]
                under_way.append((part, lax.ppermute(payload, "gz", pairs)))
        prev, cur = cur, new

    (first,) = merge(
        collect_kernel, (f32(count, layers, rows, nx),), *[array for _, array in sorted(arrived + under_way, key=lambda item: item[0])]
    )
    second = lax.all_to_all(send, "gz", split_axis=0, concat_axis=0, tiled=True)
    back_a = lax.ppermute(out_a, "gz", first_pairs)
    back_b = lax.ppermute(out_b, "gz", back_pairs)
    source_final, receiver_final = choose(back_a, back_b, back=True)
    image_out = images(shifts, (first, second), lag_offsets.shape[0])
    return (image_out, source_final, receiver_final)


def solution(mesh):
    return jax.shard_map(
        local,
        mesh=mesh,
        in_specs=(
            P(("shot", "gz"), None, None),
            P(("shot", "gz"), None, None),
            P(("shot", "gz"), None, None),
            P(("shot", "gz"), None, None),
            P("gz", None, None),
            P("shot", None, "gz", None),
            P(),
            P("shot", None, None),
            P(),
            P(),
        ),
        out_specs=(
            P("shot", None, "gz", None),
            P(("shot", "gz"), None, None),
            P(("shot", "gz"), None, None),
        ),
        check_vma=False,
    )
```

```python
import functools

import jax
import jax.numpy as jnp
import numpy as np
from jax import lax
from jax.experimental import pallas as pl
from jax.experimental.pallas import tpu as pltpu
from jax.sharding import PartitionSpec as P


SNAP_EVERY = 6
REACH = 4
EARLY = 4
PACKED = 2

SCALE = 5040.0
NEAR = (8064.0, -1008.0, 128.0, -9.0)
CENTRE = -43050.0
damping = 0.25
smoothing = 16.0

VMEM = pl.BlockSpec(memory_space=pltpu.VMEM)
SMEM = pl.BlockSpec(memory_space=pltpu.SMEM)
ANY = pl.BlockSpec(memory_space=pl.ANY)
HBM = pl.BlockSpec(memory_space=pltpu.HBM)
PARAMS = pltpu.CompilerParams(vmem_limit_bytes=24 * 1024 * 1024)


def f32(*shape):
    return jax.ShapeDtypeStruct(shape, jnp.float32)


def held(*shape):
    return pltpu.VMEM(shape, jnp.float32)


def cost(flops, bytes_accessed):
    return pl.CostEstimate(flops=int(flops), bytes_accessed=int(bytes_accessed), transcendentals=0)


def banded(size):
    apart = np.abs(np.arange(size)[:, None] - np.arange(size)[None, :])
    table = np.zeros((size, size), np.float32)
    for k, weight in enumerate(NEAR):
        table[apart == k + 1] = weight
    return table


def pairs_to_fields(count):
    first, second = [], []
    for base in range(0, count, 4):
        first += [(base, base), (base + 1, base + 2), (base + 2, base + 1), (base + 3, base + 3)]
        second += [(base, base + 2), (base + 1, base), (base + 2, base + 3), (base + 3, base + 1)]
    return first, second


def pairs_of_halos(count, shots):
    between = []
    for shot in range(shots):
        base = shot * count
        for group in range(count // 4 - 1):
            for field in range(2):
                low, high = base + 4 * group + 2 * field + 1, base + 4 * group + 4 + 2 * field
                between += [(low, high), (high, low)]
        for end in (0, 2, count - 3, count - 1):
            between.append((base + end, (shot ^ 1) * count + end if shots % 2 == 0 else base + (end ^ 2)))
    return between, [(i, i ^ 1) for i in range(count)]


def my_field():
    return lax.rem(lax.axis_index("gz") // 2, 2)


def my_half():
    return lax.rem(lax.axis_index("gz"), 2)


def place_of(local, layers):
    return jnp.where(my_half() == 0, local, layers - 1 - local)


def in_order(run, here, there):
    pl.when(my_half() == 0)(lambda: run(here, there))
    pl.when(my_half() != 0)(lambda: run(there, here))


def copy_both(pairs, sem):
    copies = [pltpu.make_async_copy(a, b, sem.at[i]) for i, (a, b) in enumerate(pairs)]
    for copy in copies:
        copy.start()
    for copy in copies:
        copy.wait()


def choose_kernel(here, there, first, second, sem):
    in_order(lambda a, b: copy_both(((a, first), (b, second)), sem), here, there)


def choose_back_kernel(here, there, first, second, one, two, sem):
    in_order(lambda a, b: copy_both(((a, one), (b, two)), sem), here, there)
    copy_both(((one, first), (two, second)), sem)


def choose(here, there, back=False):
    like = jax.ShapeDtypeStruct(here.shape, here.dtype)
    staged = [pltpu.VMEM(here.shape, here.dtype)] * 2 if back else []
    return pl.pallas_call(
        choose_back_kernel if back else choose_kernel,
        out_shape=(like, like),
        in_specs=[ANY if back else HBM] * 2,
        out_specs=(ANY if back else VMEM,) * 2,
        scratch_shapes=[*staged, pltpu.SemaphoreType.DMA((2,))],
        compiler_params=PARAMS,
        name="choose",
    )(here, there)


def prepare_kernel(layers, face_steps, lags, faces, late, early, shifts, gathered):
    steps = face_steps.shape[0]
    nx = shifts.shape[1] // 2
    gathered[...] = jnp.zeros_like(gathered)

    def gather(step, layer, row):
        base = face_steps[step] * (8 * layers) + layer
        gathered[row : row + 4] = faces[pl.ds(base + 4 * layers, 4, stride=layers), :]
        gathered[row + 4 : row + 8] = faces[pl.ds(base, 4, stride=layers), :]

    for plane in range(steps // PACKED):
        for layer in range(layers):
            for step in range(PACKED):
                gather(PACKED * plane + step, layer, 8 * (PACKED * layer + step))
        if plane < EARLY // PACKED:
            early[plane] = gathered[...].T
        else:
            late[plane - EARLY // PACKED] = gathered[...].T

    apart = lax.broadcasted_iota(jnp.int32, (nx, nx), 1) - lax.broadcasted_iota(jnp.int32, (nx, nx), 0)
    for index in range(lags.shape[0]):
        columns = slice(index * nx, (index + 1) * nx)
        for which, lag in ((0, lags[index]), (1, -lags[index])):
            moved = jnp.where(apart == lag, 1.0, 0.0).astype(jnp.bfloat16)
            shifts[which, :nx, columns] = moved
            shifts[which, nx:, columns] = moved


def prepare(saved_faces, face_steps, lag_offsets, nx):
    slots, eight, layers, ny = saved_faces.shape
    planes = face_steps.shape[0] // PACKED
    return pl.pallas_call(
        functools.partial(prepare_kernel, layers),
        out_shape=(
            f32(planes - EARLY // PACKED, ny, 128),
            f32(EARLY // PACKED, ny, 128),
            jax.ShapeDtypeStruct((2, 2 * nx, lag_offsets.shape[0] * nx), jnp.bfloat16),
        ),
        in_specs=[SMEM, SMEM, VMEM],
        out_specs=(VMEM,) * 3,
        scratch_shapes=[pltpu.VMEM((128, ny), jnp.float32)],
        compiler_params=PARAMS,
        name="prepare",
    )(face_steps, lag_offsets, saved_faces.reshape(slots * eight * layers, ny))


def for_each_part(layers, run):
    def one_layer(j, carry):
        place = place_of(j, layers)
        part = (place >= layers // 2).astype(jnp.int32)
        q = place - part * (layers // 2)
        pl.when(part == my_field())(lambda: run(j, q, 0))
        pl.when(part != my_field())(lambda: run(j, q, 1))
        return carry

    lax.fori_loop(0, layers, one_layer, 0, unroll=2)


def merge_now_kernel(now_a, now_b, cur, low, high):
    layers = 2 * now_a.shape[0]

    def run(j, q, which):
        cur[REACH + j] = (now_a, now_b)[which][q]

    for_each_part(layers, run)
    low[...] = cur[REACH : 2 * REACH]
    high[...] = cur[layers : layers + REACH]


def merge_rest_kernel(shared, before_a, before_b, speed_a, speed_b, prev, speed):
    flipped = (lax.rem(lax.axis_index("shot"), 2) == 1) & shared

    def run(j, q, which):
        prev[REACH + j] = (before_a, before_b)[which][q]
        ahead, other = (speed_a, speed_b) if which == 0 else (speed_b, speed_a)
        speed[j] = jnp.where(flipped, other[q], ahead[q]) * (1.0 / SCALE)

    for_each_part(2 * before_a.shape[0], run)


def merge(kernel, shapes, *parts):
    return pl.pallas_call(
        kernel, out_shape=shapes, in_specs=[VMEM] * len(parts), out_specs=(VMEM,) * len(shapes), compiler_params=PARAMS
    )(*parts)


def split(u):
    high = u.astype(jnp.bfloat16)
    return high, (u - high.astype(jnp.float32)).astype(jnp.bfloat16)


def advance(step, across, along, cur, prev, speed, faces, new, local):
    layers, ny, nx = speed.shape
    column = lax.broadcasted_iota(jnp.int32, (ny, nx), 1)
    edge = ((column < REACH) | (column >= nx - REACH)) & (my_field() == 0)

    def placed(layer):
        place = place_of(layer, layers)
        part = (place >= layers // 2).astype(jnp.int32)
        plane, inside = (step if step < EARLY else step - EARLY) // PACKED, step % PACKED
        lane = 8 * (PACKED * (place - part * (layers // 2)) + inside) + REACH
        held = jnp.where(part == 0, faces[0][plane], faces[1][plane])
        return pltpu.roll(held, lax.rem(128 - lane, 128), axis=1)

    for first in range(0, len(local), 2):
        pair = local[first : first + 2]
        inputs = [cur[REACH + layer] for layer in pair]
        halves = [split(u) for u in inputs]
        along_sum = jnp.dot(
            along[...],
            jnp.concatenate([jnp.concatenate(half, axis=0) for half in halves], axis=1),
            preferred_element_type=jnp.float32,
        )
        across_sum = jnp.dot(
            jnp.concatenate([jnp.concatenate(half, axis=1) for half in halves], axis=0),
            across[...],
            preferred_element_type=jnp.float32,
        )
        for i, layer in enumerate(pair):
            e, u = REACH + layer, inputs[i]
            total = across_sum[i * ny : (i + 1) * ny] + along_sum[:, i * nx : (i + 1) * nx]
            for k in range(REACH):
                total = total + NEAR[k] * (cur[e + (k + 1)] + cur[e - (k + 1)])
            total = total + CENTRE * u
            updated = 2.0 * u - prev[e] + speed[layer] * total
            new[e] = jnp.where(edge, placed(layer), updated)


def fill_low(low, cur):
    index = lax.axis_index("gz")
    place = 2 * (index // 4) + my_half()
    inside = (place > 0) & (place < lax.axis_size("gz") // 2 - 1)
    for d in range(REACH):
        cur[REACH - 1 - d] = jnp.where(inside, low[d], 0.0)


def fill_high(high, cur):
    layers = cur.shape[0] - 2 * REACH
    for d in range(REACH):
        cur[REACH + layers + d] = high[REACH - 1 - d]


def add_trace(step, traces, new):
    @pl.when(lax.axis_index("gz") == 2)
    def _():
        new[REACH] = new[REACH] + traces[step].astype(jnp.float32)


def keep_snapshot(step, phase, new, snap):
    count, layers, rows, _ = snap.shape
    window = step // SNAP_EVERY

    @pl.when(phase[window] == step - window * SNAP_EVERY)
    def _():
        def one_layer(j, carry):
            place = place_of(j, layers)
            for strip in range(count):
                snap[strip, place] = new[REACH + j, strip * rows : (strip + 1) * rows, :]
            return carry

        lax.fori_loop(0, layers, one_layer, 0)


def lower_kernel(step, across, along, low, speed, face_a, face_b, traces, cur_in, prev, cur, new, low_out):
    fill_low(low, cur)
    advance(step, across, along, cur, prev, speed, (face_a, face_b), new, list(range(REACH)))
    add_trace(step, traces, new)
    low_out[...] = new[REACH : 2 * REACH]


def upper_kernel(step, across, along, high, speed, face_a, face_b, cur_in, prev, cur, new, high_out):
    layers = speed.shape[0]
    fill_high(high, cur)
    advance(step, across, along, cur, prev, speed, (face_a, face_b), new, list(range(layers - REACH, layers)))
    high_out[...] = new[layers : layers + REACH]


def inner_kernel(step, faces, keep, phase_in, across, along, speed, *rest):
    if keep:
        rest, (phase, sem) = rest[:-2], rest[-2:]
        fetch = pltpu.make_async_copy(phase_in, phase, sem)
        fetch.start()
    face, rest = rest[:faces], rest[faces:]
    cur, prev, new = rest[0], rest[1], rest[-2] if keep else rest[-1]
    layers = speed.shape[0]
    advance(step, across, along, cur, prev, speed, face, new, list(range(REACH, layers - REACH)))
    if keep:
        fetch.wait()
        keep_snapshot(step, phase, new, rest[-1])


def last_kernel(
    step, phase_in, across, along, low, high, traces, speed, face_a, face_b, cur_in, prev, snap_in,
    cur, new, snap, out_a, out_b, send, phase, sem,
):
    fetch = pltpu.make_async_copy(phase_in, phase, sem)
    fetch.start()
    layers = speed.shape[0]
    fill_low(low, cur)
    fill_high(high, cur)
    outer = [*range(REACH), *range(layers - REACH, layers)]
    advance(step, across, along, cur, prev, speed, (face_a, face_b), new, outer)
    add_trace(step, traces, new)
    fetch.wait()
    keep_snapshot(step, phase, new, snap)

    def run(j, q, which):
        (out_a, out_b)[which][q] = new[REACH + j]

    for_each_part(layers, run)

    def one_strip(strip, carry):
        send[strip] = snap[strip]
        return carry

    lax.fori_loop(0, snap.shape[0], one_strip, 0)


def spread_kernel(snap, *outs):
    mine = lax.rem(lax.axis_index("gz"), 4)
    for which, out in enumerate(outs):

        def one(group, carry):
            out[group] = snap[4 * group + jnp.bitwise_xor(mine, which)]
            return carry

        lax.fori_loop(0, out.shape[0], one, 0)


def regather_kernel(*refs):
    held_by, (own, *parts) = refs[:4], refs[4:]
    groups = held_by[0].shape[0]
    pieces = len(parts) // (groups - 1)
    size = 4 // pieces
    group = lax.axis_index("gz") // 4
    mine = lax.rem(lax.axis_index("gz"), 4)
    for which, strips in enumerate(held_by):
        source = jnp.bitwise_xor(mine, which)
        own[source] = strips[group]
        for i, part in enumerate(parts):
            first = (i % pieces) * size

            @pl.when((source >= first) & (source < first + size))
            def _(i=i, part=part, first=first, source=source, strips=strips):
                part[source - first] = strips[jnp.bitwise_xor(group, i // pieces + 1)]


def collect_kernel(own, *refs):
    parts, out = refs[:-1], refs[-1]
    pieces = len(parts) // (out.shape[0] // 4 - 1)
    size = 4 // pieces
    group = lax.axis_index("gz") // 4
    for i in range(4):
        out[4 * group + i] = own[i]
    for i, part in enumerate(parts):
        first = 4 * jnp.bitwise_xor(group, i // pieces + 1) + (i % pieces) * size
        for j in range(size):
            out[first + j] = part[j]


def image_kernel(shifts, *refs):
    windows, (out, light, stage, sem) = refs[:-4], refs[-4:]
    _, layers, rows, nx = windows[0].shape
    lags, depth = out.shape[:2]
    size = layers * rows
    blocks = depth // layers
    table = sweep_table(depth)

    carried = jnp.zeros((rows, nx), jnp.float32)
    for d in range(depth):
        block, layer = d // layers, d % layers
        device = (block // 2) * 4 + block % 2
        squares = sum(window[device, layer] * window[device, layer] for window in windows)
        carried = squares * table[d] + carried * (smoothing * table[d])
        light[d] = carried
    carried = jnp.zeros((rows, nx), jnp.float32)
    for d in reversed(range(depth)):
        carried = light[d] + carried * (smoothing * table[d])
        light[d] = 1.0 / (carried + damping)

    def put(block, slot):
        return pltpu.make_async_copy(
            stage.at[slot], out.at[:, pl.ds(block * layers, layers)], sem.at[slot]
        )

    def one_block(block, carry):
        slot = lax.rem(block, 2)
        device = (block // 2) * 4 + lax.rem(block, 2)
        pl.when(block >= 2)(lambda: put(block - 2, slot).wait())

        def both(device, window):
            return jnp.concatenate(split(window[device].reshape(size, nx)), axis=1)

        sources = [both(device, window) for window in windows]
        receivers = [both(device + 2, window) for window in windows]
        inverse = light[pl.ds(block * layers, layers)].reshape(size, nx)
        for lag in range(0, lags, 2):
            columns = slice(lag * nx, (lag + 2) * nx)
            raw = 0.0
            for window in range(len(windows)):
                raw = raw + jnp.dot(
                    sources[window], shifts[0, :, columns], preferred_element_type=jnp.float32
                ) * jnp.dot(receivers[window], shifts[1, :, columns], preferred_element_type=jnp.float32)
            for i in range(2):
                value = (raw[:, i * nx : (i + 1) * nx] * inverse).astype(stage.dtype)
                stage[slot, lag + i] = value.reshape(layers, rows, nx)
        put(block, slot).start()
        return carry

    lax.fori_loop(0, blocks, one_block, 0)
    for block in (blocks - 2, blocks - 1):
        put(block, block % 2).wait()


def sweep_table(depth):
    table, before = [], 0.0
    for _ in range(depth):
        before = 1.0 / (1.0 + 2.0 * smoothing - smoothing * smoothing * before)
        table.append(before)
    return table


def images(shifts, windows, lags):
    count, layers, rows, nx = windows[0].shape
    depth = count // 2 * layers
    return pl.pallas_call(
        image_kernel,
        out_shape=jax.ShapeDtypeStruct((lags, depth, rows, nx), jnp.bfloat16),
        in_specs=[VMEM] * (1 + len(windows)),
        out_specs=ANY,
        scratch_shapes=[
            pltpu.VMEM((depth, rows, nx), jnp.float32),
            pltpu.VMEM((2, lags, layers, rows, nx), jnp.bfloat16),
            pltpu.SemaphoreType.DMA((2,)),
        ],
        compiler_params=PARAMS,
        name="images",
    )(shifts, *windows)


def local(
    source_now,
    source_before,
    receiver_now,
    receiver_before,
    speed_term,
    saved_faces,
    face_steps,
    traces,
    lag_offsets,
    snap_phase,
):
    count = lax.axis_size("gz")
    own, ny, nx = source_now.shape
    layers = 2 * own
    rows = ny // count
    steps = face_steps.shape[0]
    first_pairs, second_pairs = pairs_to_fields(count)
    back_pairs = [(b, a) for a, b in second_pairs]
    shots = lax.axis_size("shot")
    between, within = pairs_of_halos(count, shots)
    band_x, band_y = banded(nx), banded(ny)
    across = jnp.asarray(np.concatenate([band_x, band_x], axis=0), jnp.bfloat16)
    along = jnp.asarray(np.concatenate([band_y, band_y], axis=1), jnp.bfloat16)

    def regroup(a, b):
        return lax.ppermute(a, "gz", first_pairs), lax.ppermute(b, "gz", second_pairs)

    tall = held(layers + 2 * REACH, ny, nx)
    whole = f32(layers, ny, nx)
    slab = f32(REACH, ny, nx)
    half = f32(own, ny, nx)
    strips = held(count, layers, rows, nx)
    plane = ny * nx

    shared = shots % 2 == 0
    if shared:
        both = [
            (shot * count + a, shot * count + b)
            for shot in range(shots)
            for a, b in (first_pairs, second_pairs)[shot % 2]
        ]
        one = lax.ppermute(speed_term, ("shot", "gz"), both)
        speed_parts = one, lax.ppermute(one, "shot", [(shot, shot ^ 1) for shot in range(shots)])
    else:
        speed_parts = regroup(speed_term, speed_term)
    now = regroup(*choose(source_now, receiver_now))
    before = regroup(*choose(source_before, receiver_before))
    late, early, shifts = prepare(saved_faces, face_steps, lag_offsets, nx)
    early = regroup(early, early)
    cur, low, high = merge(merge_now_kernel, (tall, slab, slab), *now)
    low = lax.ppermute(low, ("shot", "gz"), between)
    high = lax.ppermute(high, "gz", within)
    prev, speed = merge(functools.partial(merge_rest_kernel, shared), (tall, whole), *before, *speed_parts)

    groups = count // 4
    pieces = max(1, 8 // groups)
    waiting, under_way, arrived = [], [], []

    snap = None
    for step in range(steps):
        faces = late if step >= EARLY else early
        wide = len(faces)
        if step < steps - 1:
            lower = pl.pallas_call(
                functools.partial(lower_kernel, step),
                out_shape=(tall, tall, slab),
                in_specs=[VMEM] * 9,
                out_specs=(VMEM,) * 3,
                input_output_aliases={7: 0, 8: 1},
                compiler_params=PARAMS,
                cost_estimate=cost(60 * 4 * plane, 4 * 20 * plane),
                name="lower",
            )
            upper = pl.pallas_call(
                functools.partial(upper_kernel, step),
                out_shape=(tall, tall, slab),
                in_specs=[VMEM] * 8,
                out_specs=(VMEM,) * 3,
                input_output_aliases={6: 0, 7: 1},
                compiler_params=PARAMS,
                cost_estimate=cost(60 * 4 * plane, 4 * 20 * plane),
                name="upper",
            )
            cur, new, low = lower(across, along, low, speed, *faces, traces, cur, prev)
            low = lax.ppermute(low, ("shot", "gz"), between)
            cur, new, high = upper(across, along, high, speed, *faces, cur, new)
            high = lax.ppermute(high, "gz", within)
            landed = []
            if step not in (SNAP_EVERY, SNAP_EVERY + 1):
                low, *landed = lax.optimization_barrier((low, *[array for _, array in under_way]))
            if step not in (SNAP_EVERY, SNAP_EVERY + 1):
                arrived += [(part, array) for (part, _), array in zip(under_way, landed)]
                under_way = []
        else:
            new = prev
        operands = (snap_phase, across, along, speed, *faces, cur, new)
        inner = functools.partial(
            pl.pallas_call,
            compiler_params=PARAMS,
            cost_estimate=cost(60 * (layers - 8) * plane, 4 * 40 * plane),
            name="inner",
        )
        if step < steps - 1:
            alias = {5 + wide: 0}
            if snap is not None:
                operands, alias = (*operands, snap), {5 + wide: 0, 6 + wide: 1}
            new, snap = inner(
                functools.partial(inner_kernel, step, wide, True),
                out_shape=(tall, strips),
                in_specs=[ANY] + [VMEM] * (len(operands) - 1),
                out_specs=(VMEM,) * 2,
                scratch_shapes=[pltpu.SMEM(snap_phase.shape, jnp.int32), pltpu.SemaphoreType.DMA],
                input_output_aliases=alias,
            )(*operands)
        else:
            (new,) = inner(
                functools.partial(inner_kernel, step, wide, False, None),
                out_shape=(tall,),
                in_specs=[VMEM] * (len(operands) - 1),
                out_specs=(VMEM,),
                input_output_aliases={4 + wide: 0},
            )(*operands[1:])
            last = pl.pallas_call(
                functools.partial(last_kernel, step),
                out_shape=(tall, tall, strips, half, half, f32(*strips.shape)),
                in_specs=[ANY] + [VMEM] * 11,
                out_specs=(VMEM,) * 6,
                scratch_shapes=[pltpu.SMEM(snap_phase.shape, jnp.int32), pltpu.SemaphoreType.DMA],
                input_output_aliases={9: 0, 10: 1, 11: 2},
                compiler_params=PARAMS,
                name="last",
            )
            _, _, _, out_a, out_b, send = last(snap_phase, across, along, low, high, traces, speed, *faces, cur, new, snap)
        if step == 0:
            late, new = lax.optimization_barrier((late, new))
            late = regroup(late, late)
        if step == SNAP_EVERY - 1:
            strip_parts = merge(spread_kernel, (f32(groups, layers, rows, nx),) * 4, snap)
            for which in (1, 2, 3):
                payload, new = lax.optimization_barrier((strip_parts[which], new))
                under_way.append((which, lax.ppermute(payload, "gz", [(i, i ^ which) for i in range(count)])))
            snap = None
        if step == SNAP_EVERY + 1:
            *landed, new = lax.optimization_barrier((*[array for _, array in under_way], new))
            own_strips, *sent = merge(
                regather_kernel,
                (f32(4, layers, rows, nx), *[f32(4 // pieces, layers, rows, nx)] * (pieces * (groups - 1))),
                strip_parts[0],
                *landed,
            )
            waiting = [
                (j < pieces, j, [(i, 4 * ((i // 4) ^ (j // pieces + 1)) + i % 4) for i in range(count)])
                for j in range(len(sent))
            ]
            under_way = []
        slots = max(1, steps - 1 - step)
        far = [item for item in waiting if not item[0]]
        near = [item for item in waiting if item[0]]
        chosen = far[: -(-len(far) // slots)] + (near[: -(-len(near) // slots)] if step > SNAP_EVERY + 1 or not far else [])
        waiting = [item for item in waiting if item not in chosen]
        for _, which_part, pairs in chosen:
            payload = sent[which_part]
            payload, new = lax.optimization_barrier((payload, new))
            under_way.append((which_part, lax.ppermute(payload, "gz", pairs)))
        prev, cur = cur, new

    (first,) = merge(
        collect_kernel, (f32(count, layers, rows, nx),), own_strips, *[array for _, array in sorted(arrived + under_way, key=lambda item: item[0])]
    )
    second = lax.all_to_all(send, "gz", split_axis=0, concat_axis=0, tiled=True)
    back_a = lax.ppermute(out_a, "gz", first_pairs)
    back_b = lax.ppermute(out_b, "gz", back_pairs)
    source_final, receiver_final = choose(back_a, back_b, back=True)
    image_out = images(shifts, (first, second), lag_offsets.shape[0])
    return (image_out, source_final, receiver_final)


def solution(mesh):
    return jax.shard_map(
        local,
        mesh=mesh,
        in_specs=(
            P(("shot", "gz"), None, None),
            P(("shot", "gz"), None, None),
            P(("shot", "gz"), None, None),
            P(("shot", "gz"), None, None),
            P("gz", None, None),
            P("shot", None, "gz", None),
            P(),
            P("shot", None, None),
            P(),
            P(),
        ),
        out_specs=(
            P("shot", None, "gz", None),
            P(("shot", "gz"), None, None),
            P(("shot", "gz"), None, None),
        ),
        check_vma=False,
    )
```
